32 devices in a mesh: dp: 4 (over z), ep: 8 (over y, x, core).
Axes of the slice: x: 2, y: 2, z: 4, core: 2. Of those that a mesh axis runs over, the one named last changes fastest.
Arguments:
- residual: bfloat16 [256, 2880], P(('dp', 'ep')), may hold values from -6 to 6
- queries: bfloat16 [256, 4096], P('dp', 'ep'), may hold values from -16 to 16
- fresh_key_value: bfloat16 [256, 2, 512], P('dp'), may hold values from -6 to 6
- prompt_page_cache: bfloat16 [8, 128, 2, 512], P('dp'), may hold values from -16 to 16
- group_page_table: int32 [4, 2], replicated, may hold values from -1 to 7, as said below
- prompt_length: int32 [4], replicated, may hold values from 64 to 256, as said below
- suffix_length: int32 [4, 8], P('dp'), may hold values from 1 to 16, 64 in all within a row
- request_group: int32 [32], P('dp'), may hold values from 0 to 3, never falling along the last dimension, each value on 1 to 16 neighbouring positions
- request_adapter_index: int32 [32], P('dp'), may hold values from 0 to 63, as said below
- adapter_slot_index: int32 [64], replicated, may hold values from -1 to 15, as said below
- adapter_down_maps: bfloat16 [16, 4096, 16], P(None, 'ep'), may hold values from -0.09375 to 0.09375
- adapter_up_maps: bfloat16 [16, 16, 2880], P('dp'), may hold values from -1.5 to 1.5
- sinks: float32 [64], P('ep'), may hold values from 2 to 6
- output_weight: bfloat16 [4096, 2880], P('ep'), may hold values from -0.09375 to 0.09375
- output_bias: bfloat16 [2880], replicated, may hold values from -3 to 3
- norm_weight: bfloat16 [2880], replicated, may hold values from 0.5 to 1.5
- token_experts: int32 [256, 4], P(('dp', 'ep')), may hold values from 0 to 7, all different within a row; in each aligned block of 8 rows (0 to 7, 8 to 15, ...) at most 8 rows name the same one
- expert_gate_weight: float32 [256, 4], P(('dp', 'ep')), may hold values from 0.1 to 0.6
- expert_slot_index: int32 [8], replicated, may hold values from 0 to 7, each once
- gate_weight: bfloat16 [8, 2880, 2880], P('ep', 'dp'), may hold values from -0.3125 to 0.3125
- up_weight: bfloat16 [8, 2880, 2880], P('ep', 'dp'), may hold values from -0.3125 to 0.3125
- down_weight: bfloat16 [8, 2880, 2880], P('ep', 'dp'), may hold values from -0.013671875 to 0.013671875
- gate_bias: bfloat16 [8, 2880], P('ep', 'dp'), may hold values from -3 to 3
- up_bias: bfloat16 [8, 2880], P('ep', 'dp'), may hold values from -3 to 3
- down_bias: bfloat16 [8, 2880], P('ep', 'dp'), may hold values from -3 to 3
Outputs:
- layer_out: bfloat16 [256, 2880], P(('dp', 'ep'))
The draws below stay inside these ranges and needn't reach their ends.
Inputs may be any that keep to these rules, and one draw needn't show every extreme that they name: `group_page_table`: row g lists the pages of group g's prompt in order, page s holding prompt positions s * 128 to (s + 1) * 128 - 1; every group has at least one page, unused entries are -1 and follow the used ones, and no page appears twice. `prompt_length`: each group's prompt fills its pages but the last, and at least half of the last. `suffix_length`: row b sums to 64. `request_group`: never falling; each group has 1 to 16 requests. `request_adapter_index`: every request names a loaded adapter (adapter_slot_index not -1). `adapter_slot_index`: each slot 0 to 15 holds exactly one adapter; the others are -1. `token_experts`: each token names 4 different experts; within the rows of one device no expert is named by more than 8 rows. `expert_slot_index`: each slot holds one expert.
All inputs are finite; a program needn't handle non-finite values.
Results may differ from the reference program's by a relative error of at most 0.015.
Values may be sent and summed in bfloat16 or wider, within the bound.
A program may use at most 64 MiB of HBM per device.

```python
import math
import jax
import jax.numpy as jnp
import numpy as np
from jax import lax

MODEL_WIDTH = 2880
QUERY_HEADS = 64
KV = 8
HEAD_WIDTH = 64
FF = 2880
EXPERTS = 8
TOP = 4
ADAPTER_RANK = 16
LOADED_ADAPTERS = 16
ADAPTER_IDS = 64
PAGE = 128
MAXP = 2
REQ_DEV = 8
TOK_DEV = 8
TOK_ROW = 64
NEW_TOKENS = 256
REQS = 32
GROUPS = 4
POOL = 8
MAXLEN = 16
CAP = 8
N_DP = 4


def draw_queries(key, part):
    return jnp.clip(jax.random.normal(key, (NEW_TOKENS, QUERY_HEADS * HEAD_WIDTH), jnp.float32), -6.0, 6.0).astype(jnp.bfloat16)


def draw_prompt_page_cache(key, part):
    cache_shape = (POOL, PAGE, 2, KV * HEAD_WIDTH)
    return jnp.clip(jax.random.normal(key, cache_shape, jnp.float32), -6.0, 6.0).astype(jnp.bfloat16)


def page_plan(key):
    group_ids = jnp.arange(GROUPS, dtype=jnp.int32)
    counts = jax.random.randint(jax.random.fold_in(key, 11), (GROUPS,), 1, MAXP + 1)
    forced = jax.random.randint(jax.random.fold_in(key, 12), (), 0, GROUPS)
    single = (forced + 1) % GROUPS
    counts = jnp.where(group_ids == forced, MAXP, counts)
    counts = jnp.where(group_ids == single, 1, counts)
    order = jax.random.permutation(jax.random.fold_in(key, 13), POOL).astype(jnp.int32)
    last_place = jnp.argmax(order == POOL - 1).astype(jnp.int32)
    head_place = (forced * MAXP).astype(jnp.int32)
    head_value = order[head_place]
    order = order.at[last_place].set(head_value).at[head_place].set(POOL - 1)
    table = order[:GROUPS * MAXP].reshape(GROUPS, MAXP)
    slot_ids = jnp.arange(MAXP, dtype=jnp.int32)
    table = jnp.where(slot_ids[None, :] < counts[:, None], table, -1)
    last_fill = jax.random.randint(jax.random.fold_in(key, 14), (GROUPS,), PAGE // 2, PAGE + 1)
    last_fill = jnp.where(group_ids == forced, PAGE, last_fill)
    last_fill = jnp.where(group_ids == single, PAGE // 2, last_fill)
    lengths = (counts - 1) * PAGE + last_fill
    return (table.astype(jnp.int32), lengths.astype(jnp.int32))


def draw_group_page_table(key, part):
    return page_plan(key)[0]


def draw_prompt_length(key, part):
    return page_plan(key)[1]


def adapter_plan(key):
    inner = 1 + jax.random.permutation(jax.random.fold_in(key, 21), ADAPTER_IDS - 2)[:LOADED_ADAPTERS - 2].astype(jnp.int32)
    ends = jnp.array([0, ADAPTER_IDS - 1], jnp.int32)
    chosen = jax.random.permutation(jax.random.fold_in(key, 23), jnp.concatenate([ends, inner])).astype(jnp.int32)
    slot_table = jnp.full((ADAPTER_IDS,), -1, jnp.int32).at[chosen].set(jnp.arange(LOADED_ADAPTERS, dtype=jnp.int32))
    picks = jax.random.randint(jax.random.fold_in(key, 22), (REQS,), 0, LOADED_ADAPTERS)
    first_place = jnp.argmax(chosen == 0).astype(jnp.int32)
    top_place = jnp.argmax(chosen == ADAPTER_IDS - 1).astype(jnp.int32)
    picks = picks.at[0].set(first_place).at[1].set(top_place)
    return (slot_table, chosen[picks].astype(jnp.int32))


def draw_adapter_slot_index(key, part):
    return adapter_plan(key)[0]


def draw_request_adapter_index(key, part):
    return adapter_plan(key)[1]


def block_levels(stream_key, dims, shards, low, high):
    def one(axis_at, blocks):
        draws = jax.random.uniform(jax.random.fold_in(jax.random.fold_in(stream_key, 6), axis_at), (blocks,), jnp.float32, low / len(shards), high / len(shards))
        return jnp.repeat(jnp.exp(draws), dims[axis_at] // blocks).reshape((-1,) + (1,) * (len(dims) - axis_at - 1))

    level = one(*shards[0])
    for cut in shards[1:]:
        level = level * one(*cut)
    return level


def split_up(amount, total, reach, lean):
    weights = [(1 << 20) // math.isqrt(standing ** lean) + 1 for standing in range(2, amount + 1)]
    rest, holding = total - reach - (amount - 1), [1] * (amount - 1)
    while rest > 0:
        free = [i for i in range(amount - 1) if holding[i] < reach]
        mass, left = sum([weights[i] for i in free]), rest
        for i in free:
            extra = min(reach - holding[i], max(1, left * weights[i] // mass), rest)
            holding[i] = holding[i] + extra
            rest = rest - extra
    return np.array([reach] + holding)


def ragged_sizes(key, amount, total, reach, skew):
    if amount == 2:
        one = jax.random.randint(key, (), max(1, total - reach), min(reach, total - 1) + 1)
        return jnp.stack([one, total - one])
    sizes = jnp.asarray(split_up(amount, total, reach, skew), jnp.int32)
    pairs = (amount - 1) // 2
    donor, receiver = sizes[1:1 + 2 * pairs:2], sizes[2:2 + 2 * pairs:2]
    margin = jnp.minimum(donor - 1, reach - receiver)
    passed = jax.random.randint(jax.random.fold_in(key, 1), (pairs,), 0, 1 << 20) % (margin + 1)
    sizes = sizes.at[1:1 + 2 * pairs:2].set(donor - passed).at[2:2 + 2 * pairs:2].set(receiver + passed)
    return sizes[jax.random.permutation(jax.random.fold_in(key, 2), amount)]


def deal_out(own_key, own, number, rows, amount, top, reach, lean):
    ranking = jax.random.permutation(own_key, amount)
    packed, usual = shares(amount, rows * top, reach, lean, True), shares(amount, rows * top, reach, lean, False)
    places = jnp.arange(amount)

    def named(sizes, turn):
        used = int((sizes > 0).sum())
        fixed = max(1, used // 4)
        passed = fixed + (places - fixed + turn * (used - fixed)) % max(1, amount - fixed)
        return jnp.zeros((amount,), jnp.int32).at[ranking[jnp.where(places < fixed, places, passed)]].set(jnp.asarray(sizes, jnp.int32))

    sizes = jnp.where(number % 4 == 0, named(packed, number // 4), named(usual, number - number // 4 - 1))
    mixed = jax.random.permutation(jax.random.fold_in(own, 3), amount)
    giver, sink = mixed[0:amount // 2 * 2:2], mixed[1:amount // 2 * 2:2]
    margin = jnp.minimum(sizes[giver] - 1, reach - sizes[sink]) // 2
    margin = jnp.where((giver == ranking[0]) | (sink == ranking[0]) | (sizes[sink] == 0), 0, jnp.maximum(margin, 0))
    passed = jax.random.randint(jax.random.fold_in(own, 4), (amount // 2,), 0, 1 << 20) % (margin + 1)
    sizes = sizes.at[giver].add(-passed).at[sink].add(passed)
    items = jnp.searchsorted(jnp.cumsum(sizes), jnp.arange(rows * top), side="right").astype(jnp.int32)
    listing = items.reshape(top, rows).T
    listing = listing[jax.random.permutation(jax.random.fold_in(own, 1), rows)]
    turn = jax.random.randint(jax.random.fold_in(own, 2), (rows, 1), 0, top)
    return jnp.take_along_axis(listing, (jnp.arange(top)[None, :] + turn) % top, axis=1)


def shares(number_of, total, most, skew, full):
    portions = [(1 << 20) // math.isqrt(grade ** skew) + 1 for grade in range(1, number_of + 1)]
    largest = most if full else min(most, max(-(-total // number_of), total * portions[0] // sum(portions)))
    least = 1 if total - largest >= number_of - 1 else 0
    given, spare = [largest] + [least] * (number_of - 1), total - largest - least * (number_of - 1)
    while spare > 0:
        free = [i for i in range(1, number_of) if given[i] < largest] or [i for i in range(1, number_of) if given[i] < most]
        mass, budget = sum([portions[i] for i in free]), spare
        for i in free:
            extra = min(most - given[i], max(1, budget * portions[i] // mass), spare)
            given[i] = given[i] + extra
            spare = spare - extra
    return np.array(given)


def centred(key, dims, width, limit, shards=(), held_as=jnp.bfloat16):
    result = jax.random.normal(key, dims, jnp.float32) * width
    if len(shards) > 0:
        result = block_levels(key, dims, shards, -0.22, 0.18) * result
    return jnp.clip(result, min=-limit, max=limit).astype(held_as)


def setup_inputs(seed: int = 0) -> dict:
    seeds = jax.random.split(jax.random.key(seed), 26)
    residual = centred(seeds[0], (NEW_TOKENS, MODEL_WIDTH), 1.0, 6.0, ((0, 32),))
    queries = draw_queries(jax.random.fold_in(seeds[25], 71), 0)
    fresh_key_value = centred(seeds[2], (NEW_TOKENS, 2, KV * HEAD_WIDTH), 1.0, 6.0, ((0, 4),))
    prompt_page_cache = draw_prompt_page_cache(jax.random.fold_in(seeds[25], 71), 0)
    group_page_table = draw_group_page_table(jax.random.fold_in(seeds[25], 71), 0)
    prompt_length = draw_prompt_length(jax.random.fold_in(seeds[25], 71), 0)
    suffix_length = jax.vmap(lambda own: ragged_sizes(own, REQ_DEV, TOK_ROW, MAXLEN, 2))(jax.random.split(seeds[6], N_DP)).reshape((N_DP, REQ_DEV)).astype(jnp.int32)
    request_group = jnp.searchsorted(jnp.cumsum(ragged_sizes(seeds[7], GROUPS, REQS, 16, 1)), jnp.arange(REQS), side="right").astype(jnp.int32)
    request_adapter_index = draw_request_adapter_index(jax.random.fold_in(seeds[25], 71), 0)
    adapter_slot_index = draw_adapter_slot_index(jax.random.fold_in(seeds[25], 71), 0)
    adapter_down_maps = centred(seeds[10], (LOADED_ADAPTERS, QUERY_HEADS * HEAD_WIDTH, ADAPTER_RANK), (QUERY_HEADS * HEAD_WIDTH) ** -0.5, 0.09375, ((1, 8),))
    adapter_up_maps = centred(seeds[11], (LOADED_ADAPTERS, ADAPTER_RANK, MODEL_WIDTH), ADAPTER_RANK ** -0.5, 1.5, ((0, 4),))
    sinks = jnp.clip(2.0 + 4.0 * jax.random.uniform(seeds[12], (QUERY_HEADS,), jnp.float32) ** block_levels(seeds[12], (QUERY_HEADS,), ((0, 8),), -0.2, 0.2), 2.0, 6.0)
    output_weight = centred(seeds[13], (QUERY_HEADS * HEAD_WIDTH, MODEL_WIDTH), (QUERY_HEADS * HEAD_WIDTH) ** -0.5, 0.09375, ((0, 8),))
    output_bias = centred(seeds[14], (MODEL_WIDTH,), 0.5, 3.0)
    norm_weight = jnp.clip(1.0 + 0.1 * jax.random.normal(seeds[15], (MODEL_WIDTH,), jnp.float32), 0.5, 1.5).astype(jnp.bfloat16)
    token_experts_keys = jax.random.split(jax.random.fold_in(seeds[16], 1), NEW_TOKENS // TOK_DEV)
    token_experts_turns = jax.random.permutation(jax.random.fold_in(seeds[16], 3), NEW_TOKENS // TOK_DEV)
    token_experts = jax.vmap(lambda own, number: deal_out(jax.random.fold_in(seeds[16], 2), own, number, TOK_DEV, EXPERTS, TOP, CAP, 2))(token_experts_keys, token_experts_turns).reshape((NEW_TOKENS, TOP))
    expert_gate_weight = jnp.clip(0.1 + 0.5 * jax.random.uniform(seeds[17], (NEW_TOKENS, TOP), jnp.float32) ** block_levels(seeds[17], (NEW_TOKENS, TOP), ((0, 32),), -0.2, 0.2), 0.1, 0.6)
    expert_slot_index = jax.random.permutation(seeds[18], EXPERTS).astype(jnp.int32)
    gate_weight = centred(seeds[19], (EXPERTS, FF, MODEL_WIDTH), (MODEL_WIDTH // 8) ** -0.5, 0.3125, ((0, 8), (1, 4)))
    up_weight = centred(seeds[20], (EXPERTS, FF, MODEL_WIDTH), (MODEL_WIDTH // 8) ** -0.5, 0.3125, ((0, 8), (1, 4)))
    down_weight = centred(seeds[21], (EXPERTS, MODEL_WIDTH, FF), (FF * 64) ** -0.5, 0.013671875, ((0, 8), (1, 4)))
    gate_bias = centred(seeds[22], (EXPERTS, FF), 0.5, 3.0, ((0, 8), (1, 4)))
    up_bias = centred(seeds[23], (EXPERTS, FF), 0.5, 3.0, ((0, 8), (1, 4)))
    down_bias = centred(seeds[24], (EXPERTS, MODEL_WIDTH), 0.5, 3.0, ((0, 8), (1, 4)))
    return {"residual": residual, "queries": queries, "fresh_key_value": fresh_key_value, "prompt_page_cache": prompt_page_cache, "group_page_table": group_page_table, "prompt_length": prompt_length, "suffix_length": suffix_length, "request_group": request_group, "request_adapter_index": request_adapter_index, "adapter_slot_index": adapter_slot_index, "adapter_down_maps": adapter_down_maps, "adapter_up_maps": adapter_up_maps, "sinks": sinks, "output_weight": output_weight, "output_bias": output_bias, "norm_weight": norm_weight, "token_experts": token_experts, "expert_gate_weight": expert_gate_weight, "expert_slot_index": expert_slot_index, "gate_weight": gate_weight, "up_weight": up_weight, "down_weight": down_weight, "gate_bias": gate_bias, "up_bias": up_bias, "down_bias": down_bias}


THETA = 150000.0
NEG = -1e+30
LIMIT = 7.0
ALPHA = 1.702
EPSILON = 1e-05
ADAPTER_SCALE = 2.0

def settle(values):
    return lax.optimization_barrier(values.astype(jnp.bfloat16)).astype(jnp.float32)

def rotate(values, positions):
    head_width = values.shape[-1]
    half_size = head_width // 2
    frequency = THETA ** (-2.0 * jnp.arange(half_size, dtype=jnp.float32) / head_width)
    angles = positions.astype(jnp.float32)[:, None] * frequency[None, :]
    cosine = jnp.cos(angles)[:, None, :]
    sine_part = jnp.sin(angles)[:, None, :]
    front_part = values[..., :half_size]
    back_part = values[..., half_size:]
    return jnp.concatenate([front_part * cosine - back_part * sine_part, back_part * cosine + front_part * sine_part], axis=-1)

def token_layout(lengths, groups, request_adapter, adapter_slot_index, prompt_length, tok_count):
    finish = jnp.cumsum(lengths).astype(jnp.int32)
    starts = (finish - lengths).astype(jnp.int32)
    token_index = jnp.arange(tok_count, dtype=jnp.int32)
    member = (token_index[:, None] >= starts[None, :]) & (token_index[:, None] < finish[None, :])
    member_int = member.astype(jnp.int32)
    request_local = lax.optimization_barrier(jnp.sum(member_int * jnp.arange(lengths.shape[0], dtype=jnp.int32)[None, :], axis=1))
    token_group = lax.optimization_barrier(jnp.sum(member_int * groups[None, :], axis=1))
    offset = token_index - lax.optimization_barrier(jnp.sum(member_int * starts[None, :], axis=1))
    group_hit = token_group[:, None] == jnp.arange(prompt_length.shape[0], dtype=jnp.int32)[None, :]
    prompt_base = lax.optimization_barrier(jnp.sum(jnp.where(group_hit, prompt_length[None, :], 0), axis=1))
    token_adapter = lax.optimization_barrier(jnp.sum(member_int * request_adapter[None, :], axis=1))
    id_hit = token_adapter[:, None] == jnp.arange(adapter_slot_index.shape[0], dtype=jnp.int32)[None, :]
    token_slot = lax.optimization_barrier(jnp.sum(jnp.where(id_hit, adapter_slot_index[None, :], 0), axis=1))
    return (request_local, token_group, (prompt_base + offset).astype(jnp.int32), token_slot.astype(jnp.int32))

def page_layout(group_page_table, pool_total):
    page_ids = jnp.arange(pool_total, dtype=jnp.int32)
    matches = group_page_table[:, :, None] == page_ids[None, None, :]
    match_int = matches.astype(jnp.int32)
    group_ids = jnp.arange(group_page_table.shape[0], dtype=jnp.int32)
    slot_ids = jnp.arange(group_page_table.shape[1], dtype=jnp.int32)
    page_group = lax.optimization_barrier(jnp.sum(match_int * group_ids[:, None, None], axis=(0, 1)))
    page_slot = lax.optimization_barrier(jnp.sum(match_int * slot_ids[None, :, None], axis=(0, 1)))
    page_used = lax.optimization_barrier(jnp.sum(match_int, axis=(0, 1))) > 0
    return (page_group, page_slot, page_used)

def reference(residual, queries, fresh_key_value, prompt_page_cache, group_page_table, prompt_length, suffix_length, request_group, request_adapter_index, adapter_slot_index, adapter_down_maps, adapter_up_maps, sinks, output_weight, output_bias, norm_weight, token_experts, expert_gate_weight, expert_slot_index, gate_weight, up_weight, down_weight, gate_bias, up_bias, down_bias):
    score_scale = 1.0 / math.sqrt(HEAD_WIDTH)
    group_size = QUERY_HEADS // KV
    page_group, page_slot, page_used = page_layout(group_page_table, POOL)
    group_hit = page_group[:, None] == jnp.arange(GROUPS, dtype=jnp.int32)[None, :]
    page_limit = lax.optimization_barrier(jnp.sum(jnp.where(group_hit, prompt_length[None, :], 0), axis=1))
    key_pos = page_slot[:, None] * PAGE + jnp.arange(PAGE, dtype=jnp.int32)[None, :]
    key_valid = (page_used[:, None] & (key_pos < page_limit[:, None])).reshape(-1)
    key_group = jnp.broadcast_to(page_group[:, None], (POOL, PAGE)).reshape(-1)
    pool_keys = jnp.repeat(prompt_page_cache[:, :, 0, :].reshape(POOL * PAGE, KV, HEAD_WIDTH), group_size, axis=1)
    pool_values = jnp.repeat(prompt_page_cache[:, :, 1, :].reshape(POOL * PAGE, KV, HEAD_WIDTH), group_size, axis=1)
    sink_col = sinks.astype(jnp.float32)[:, None]

    def one_block(block_id):
        lengths = suffix_length[block_id]
        groups = lax.dynamic_slice_in_dim(request_group, (block_id * REQ_DEV).astype(jnp.int32), REQ_DEV)
        request_adapter = lax.dynamic_slice_in_dim(request_adapter_index, (block_id * REQ_DEV).astype(jnp.int32), REQ_DEV)
        request_local, token_group, positions, token_slot = token_layout(lengths, groups, request_adapter, adapter_slot_index, prompt_length, TOK_ROW)
        rows_query = lax.dynamic_slice_in_dim(queries, (block_id * TOK_ROW).astype(jnp.int32), TOK_ROW, 0)
        queries_rot = rotate(rows_query.reshape(TOK_ROW, QUERY_HEADS, HEAD_WIDTH).astype(jnp.float32), positions)
        rows_kv = lax.dynamic_slice_in_dim(fresh_key_value, (block_id * TOK_ROW).astype(jnp.int32), TOK_ROW, 0)
        keys_rot = rotate(rows_kv[:, 0, :].reshape(TOK_ROW, KV, HEAD_WIDTH).astype(jnp.float32), positions)
        keys_all = jnp.concatenate([pool_keys.astype(jnp.float32), jnp.repeat(settle(keys_rot), group_size, axis=1)], axis=0)
        values_all = jnp.concatenate([pool_values, jnp.repeat(rows_kv[:, 1, :].reshape(TOK_ROW, KV, HEAD_WIDTH), group_size, axis=1)], axis=0).astype(jnp.float32)
        token_index = jnp.arange(TOK_ROW, dtype=jnp.int32)
        local_ok = (request_local[:, None] == request_local[None, :]) & (token_index[None, :] <= token_index[:, None])
        pool_ok = (token_group[:, None] == key_group[None, :]) & key_valid[None, :]
        visible = jnp.concatenate([pool_ok, local_ok], axis=1)
        scores = jnp.einsum('thd,khd->htk', settle(queries_rot), keys_all) * score_scale
        masked = jnp.where(visible[None], scores, NEG)
        peak = jnp.maximum(sink_col, lax.optimization_barrier(jnp.max(masked, axis=-1)))
        probs = jnp.exp(masked - peak[..., None])
        denom = jnp.exp(sink_col - peak) + lax.optimization_barrier(jnp.sum(probs, axis=-1))
        mixed = jnp.einsum('htk,khd->htd', settle(probs), values_all)
        attended_block = (mixed / denom[..., None]).transpose(1, 0, 2).reshape(TOK_ROW, QUERY_HEADS * HEAD_WIDTH).astype(jnp.bfloat16)
        return (attended_block, token_slot)
    attention_output, token_slot = lax.map(one_block, jnp.arange(N_DP, dtype=jnp.int32))
    attention_output = attention_output.reshape(NEW_TOKENS, QUERY_HEADS * HEAD_WIDTH)
    token_slot = token_slot.reshape(NEW_TOKENS)
    adapter_onehot = token_slot[:, None] == jnp.arange(LOADED_ADAPTERS, dtype=jnp.int32)[None, :]
    adapter_columns = adapter_down_maps.transpose(1, 0, 2).reshape(QUERY_HEADS * HEAD_WIDTH, LOADED_ADAPTERS * ADAPTER_RANK)
    reduced_rank = jnp.dot(attention_output, adapter_columns, preferred_element_type=jnp.float32).reshape(NEW_TOKENS, LOADED_ADAPTERS, ADAPTER_RANK)
    adapter_middle = lax.optimization_barrier(jnp.sum(reduced_rank * adapter_onehot.astype(jnp.float32)[:, :, None], axis=1)).astype(jnp.bfloat16)
    spread_rows = adapter_onehot.astype(jnp.bfloat16)[:, :, None] * adapter_middle[:, None, :]
    adapter_update = (ADAPTER_SCALE * jnp.dot(spread_rows.reshape(NEW_TOKENS, LOADED_ADAPTERS * ADAPTER_RANK), adapter_up_maps.reshape(LOADED_ADAPTERS * ADAPTER_RANK, MODEL_WIDTH), preferred_element_type=jnp.float32)).astype(jnp.bfloat16)
    projected_rows = jnp.dot(attention_output, output_weight, preferred_element_type=jnp.float32)
    residual_stream = residual.astype(jnp.float32) + projected_rows + output_bias.astype(jnp.float32) + adapter_update.astype(jnp.float32)
    stream = settle(residual_stream)
    mean_square = lax.optimization_barrier(jnp.mean(stream * stream, axis=-1, keepdims=True))
    normed = (stream * lax.rsqrt(mean_square + EPSILON) * norm_weight.astype(jnp.float32)).astype(jnp.bfloat16)
    expert_hit = token_experts[:, :, None] == jnp.arange(EXPERTS, dtype=jnp.int32)[None, None, :]
    route_col = lax.optimization_barrier(jnp.sum(jnp.where(expert_hit, expert_slot_index[None, None, :], 0), axis=2))

    def one_slot(running, slot_id):
        gate_pre = jnp.dot(normed, gate_weight[slot_id].T, preferred_element_type=jnp.float32) + gate_bias[slot_id].astype(jnp.float32)
        up_pre = jnp.dot(normed, up_weight[slot_id].T, preferred_element_type=jnp.float32) + up_bias[slot_id].astype(jnp.float32)
        gate_pre = jnp.minimum(gate_pre, LIMIT)
        up_pre = jnp.clip(up_pre, -LIMIT, LIMIT)
        hidden = ((up_pre + 1.0) * gate_pre * jax.nn.sigmoid(ALPHA * gate_pre)).astype(jnp.bfloat16)
        expert_out = (jnp.dot(hidden, down_weight[slot_id].T, preferred_element_type=jnp.float32) + down_bias[slot_id].astype(jnp.float32)).astype(jnp.bfloat16)
        slot_weight = lax.optimization_barrier(jnp.sum(jnp.where(route_col == slot_id, expert_gate_weight, 0.0), axis=1))
        return (running + slot_weight[:, None] * expert_out.astype(jnp.float32), None)
    moe_sum, _ = lax.scan(one_slot, jnp.zeros((NEW_TOKENS, MODEL_WIDTH), jnp.float32), jnp.arange(EXPERTS, dtype=jnp.int32))
    return (stream + moe_sum).astype(jnp.bfloat16)
```

```python
import functools
import math

import jax
import jax.numpy as jnp
from jax import lax
from jax.experimental import pallas as pl
from jax.experimental.pallas import tpu as pltpu
from jax.sharding import PartitionSpec as P

THETA = 150000.0
NEG = -1e30
LIMIT = 7.0
ALPHA = 1.702
EPSILON = 1e-05
ADAPTER_SCALE = 2.0
LAST_DIMS = (((1,), (1,)), ((), ()))


def settle(values):
    return lax.optimization_barrier(values.astype(jnp.bfloat16)).astype(jnp.float32)


def rotate(values, positions):
    head_width = values.shape[-1]
    half_size = head_width // 2
    frequency = THETA ** (-2.0 * jnp.arange(half_size, dtype=jnp.float32) / head_width)
    angles = positions.astype(jnp.float32)[:, None] * frequency[None, :]
    cosine = jnp.cos(angles)[:, None, :]
    sine_part = jnp.sin(angles)[:, None, :]
    front_part = values[..., :half_size]
    back_part = values[..., half_size:]
    return jnp.concatenate(
        [front_part * cosine - back_part * sine_part, back_part * cosine + front_part * sine_part],
        axis=-1,
    )


def token_layout(lengths, groups, request_adapter, adapter_slot_index, prompt_length, tok_count):
    order = jnp.arange(lengths.shape[0], dtype=jnp.int32)
    finish = jnp.sum(jnp.where(order[None, :] <= order[:, None], lengths[None, :], 0), axis=1)
    starts = finish - lengths
    token_index = jnp.arange(tok_count, dtype=jnp.int32)
    member = (token_index[:, None] >= starts[None, :]) & (token_index[:, None] < finish[None, :])
    member_int = member.astype(jnp.int32)
    request_local = jnp.sum(
        member_int * jnp.arange(lengths.shape[0], dtype=jnp.int32)[None, :], axis=1
    )
    token_group = jnp.sum(member_int * groups[None, :], axis=1)
    offset = token_index - jnp.sum(member_int * starts[None, :], axis=1)
    group_hit = token_group[:, None] == jnp.arange(prompt_length.shape[0], dtype=jnp.int32)[None, :]
    prompt_base = jnp.sum(jnp.where(group_hit, prompt_length[None, :], 0), axis=1)
    token_adapter = jnp.sum(member_int * request_adapter[None, :], axis=1)
    id_hit = (
        token_adapter[:, None] == jnp.arange(adapter_slot_index.shape[0], dtype=jnp.int32)[None, :]
    )
    token_slot = jnp.sum(jnp.where(id_hit, adapter_slot_index[None, :], 0), axis=1)
    return (request_local, token_group, prompt_base + offset, token_slot)


def page_layout(group_page_table, pool_total):
    page_ids = jnp.arange(pool_total, dtype=jnp.int32)
    matches = group_page_table[:, :, None] == page_ids[None, None, :]
    match_int = matches.astype(jnp.int32)
    group_ids = jnp.arange(group_page_table.shape[0], dtype=jnp.int32)
    slot_ids = jnp.arange(group_page_table.shape[1], dtype=jnp.int32)
    page_group = jnp.sum(match_int * group_ids[:, None, None], axis=(0, 1))
    page_slot = jnp.sum(match_int * slot_ids[None, :, None], axis=(0, 1))
    page_used = jnp.sum(match_int, axis=(0, 1)) > 0
    return (page_group, page_slot, page_used)


def expert_hidden(rows, gate_matrix, up_matrix, gate_offset, up_offset):
    gate_pre = lax.dot_general(
        rows, gate_matrix, LAST_DIMS, preferred_element_type=jnp.float32
    ) + gate_offset.astype(jnp.float32)
    up_pre = lax.dot_general(
        rows, up_matrix, LAST_DIMS, preferred_element_type=jnp.float32
    ) + up_offset.astype(jnp.float32)
    gate_pre = jnp.minimum(gate_pre, LIMIT)
    up_pre = jnp.clip(up_pre, -LIMIT, LIMIT)
    return ((up_pre + 1.0) * gate_pre * jax.nn.sigmoid(ALPHA * gate_pre)).astype(jnp.bfloat16)


def device(dp, ep):
    return {"dp": dp, "ep": ep}


def send(src, dst, send_sem, recv_sem, dp, ep):
    copy = pltpu.make_async_remote_copy(
        src_ref=src,
        dst_ref=dst,
        send_sem=send_sem,
        recv_sem=recv_sem,
        device_id=device(dp, ep),
        device_id_type=pl.DeviceIdType.MESH,
    )
    copy.start()
    return copy


def greet(peers):
    barrier = pltpu.get_barrier_semaphore()
    for dp, ep in peers:
        pl.semaphore_signal(
            barrier, inc=1, device_id=device(dp, ep), device_id_type=pl.DeviceIdType.MESH
        )
    pl.semaphore_wait(barrier, len(peers))


def flip(index, bits):
    out = index
    for bit in (1, 2, 4):
        if bits & bit:
            out = out + bit * (1 - 2 * ((index // bit) % 2))
    return out


def token_fields(tokens, axis, lengths, groups, adapters, slots, prompt):
    shape = (tokens, 1) if axis == 0 else (1, tokens)
    token = lax.broadcasted_iota(jnp.int32, shape, axis)
    zero = jnp.zeros(shape, jnp.int32)
    request, group, position, slot = zero, zero, zero, zero
    start = lengths[0, 0] * 0
    for m in range(lengths.shape[1]):
        finish = start + lengths[0, m]
        inside = (token >= start) & (token < finish)
        request = jnp.where(inside, m, request)
        if axis == 0:
            group = jnp.where(inside, groups[m], group)
            position = jnp.where(inside, token - start + prompt[groups[m]], position)
            slot = jnp.where(inside, slots[adapters[m]], slot)
        start = finish
    return request, group, position, slot


def rotation(positions, head_width, lanes):
    half = head_width // 2
    lane = lax.broadcasted_iota(jnp.int32, (positions.shape[0], lanes), 1)
    place = lax.rem(lane, half).astype(jnp.float32)
    frequency = jnp.exp(place * (-2.0 * math.log(THETA) / head_width))
    angles = positions.astype(jnp.float32) * frequency
    cosine, sine = jnp.cos(angles), jnp.sin(angles)
    front = lax.rem(lane, head_width) < half
    signed = jnp.where(front, -sine, sine)

    def turn(values):
        values = values.astype(jnp.float32)
        partner = jnp.where(
            front, pltpu.roll(values, lanes - half, 1), pltpu.roll(values, half, 1)
        )
        return (values * cosine + partner * signed).astype(jnp.bfloat16)

    return turn


def page_groups(page, page_len, table, prompt):
    group, limit = jnp.int32(-1), jnp.int32(0)
    for s in range(table.shape[0]):
        for g in range(table.shape[1]):
            hit = table[s, g] == page
            group = jnp.where(hit, g, group)
            limit = jnp.where(hit, prompt[g] - s * page_len, limit)
    lane = lax.broadcasted_iota(jnp.int32, (1, page_len), 1)
    return jnp.where(lane < limit, group, -1)


def layer_body(
    nd,
    ne,
    rank_size,
    page_len,
    small_count,
    pages,
    fresh,
    *rest,
):
    small_hbm, rest = rest[:small_count], rest[small_count:]
    (gate_hbm, up_hbm, down_hbm, project_hbm, layer_out), rest = rest[:5], rest[5:]
    small, rest = rest[:small_count], rest[small_count:]
    (
        lengths,
        groups,
        adapters,
        slots,
        table,
        prompt,
        expert_slots,
        sinks,
        queries,
        route_experts,
        route_weights,
        adapter_columns,
        residual,
        up,
        gate_offset,
        up_offset,
        down_offset,
        bias,
        gain,
    ) = small
    (
        merged,
        combine,
        proj,
        rank,
        pages_all,
        weights,
        project_matrix,
        gathered,
        gate_matrix,
        up_matrix,
        down_matrix,
        hidden,
        outs,
        outs_in,
        sums,
        proj_in,
        rank_in,
        delta,
        delta_in,
        rank_s,
        rank_r,
        proj_s,
        proj_r,
        delta_s,
        delta_r,
        plane_s,
        plane_r,
        chip_s,
        chip_r,
        hop_s,
        hop_r,
        pass_s,
        pass_r,
        load_sem,
        unit_s,
        unit_r,
        relay_s,
        out_s,
        out_r,
        sum_s,
        sum_r,
        page_s,
        page_r,
        combine_s,
        combine_r,
        small_sem,
    ) = rest
    i, j = lax.axis_index("dp"), lax.axis_index("ep")
    loads = [
        pltpu.make_async_copy(source, target, load_sem.at[n])
        for n, (source, target) in enumerate(
            (
                (gate_hbm.at[0], gate_matrix),
                (up_hbm.at[0], up_matrix),
                (down_hbm.at[0], down_matrix),
                (project_hbm, project_matrix),
            )
        )
    ]
    small_loads = [
        pltpu.make_async_copy(source, target, small_sem.at[n])
        for n, (source, target) in enumerate(zip(small_hbm, small))
    ]
    for copy in small_loads:
        copy.start()
    for n in (3, 0, 1, 2):
        loads[n].start()
    everyone = [(d, e) for d in range(nd) for e in range(ne) if d or e]
    greet([(lax.rem(i + d, nd), lax.rem(j + e, ne)) for d, e in everyone])
    page_copies, combine_copies = [], []
    for d in range(1, nd):
        ti = lax.rem(i + d, nd)
        page_copies.append(
            send(pages, pages_all.at[i], page_s.at[d - 1], page_r.at[d - 1], ti, j)
        )
    for copy in small_loads:
        copy.wait()
    rows = residual.shape[0]
    experts_of = route_experts[...]
    holders = jnp.zeros_like(experts_of)
    for e in range(expert_slots.shape[0]):
        holders = jnp.where(experts_of == e, expert_slots[e], holders)
    combine[...] = jnp.zeros_like(combine)
    for e in range(ne):
        combine[e : e + 1, :rows] = jnp.sum(
            jnp.where(holders == e, route_weights[...], 0.0), axis=0, keepdims=True
        )
    for d in range(1, nd):
        ti = lax.rem(i + d, nd)
        combine_copies.append(
            send(combine, weights.at[i], combine_s.at[d - 1], combine_r.at[d - 1], ti, j)
        )
    pages_all[i] = pages[...]
    weights[i] = combine[...]
    heads = sinks.shape[0]
    tokens_row = queries.shape[0]
    head_width = fresh.shape[1] // 2
    lanes = 2 * head_width
    page_count = pages.shape[0] // page_len
    scale = 1.0 / math.sqrt(head_width)
    request, group, position, slot = token_fields(
        tokens_row, 0, lengths, groups, adapters, slots, prompt
    )
    request_row = token_fields(tokens_row, 1, lengths, groups, adapters, slots, prompt)[0]
    turn = rotation(position, head_width, lanes)
    turned = [turn(queries[:, n * lanes : (n + 1) * lanes]) for n in range(heads // 2)]
    query_rows = jnp.concatenate(
        [pair[:, n * head_width : (n + 1) * head_width] for pair in turned for n in (0, 1)], axis=0
    )
    row_index = lax.broadcasted_iota(jnp.int32, (tokens_row, tokens_row), 0)
    column_index = lax.broadcasted_iota(jnp.int32, (tokens_row, tokens_row), 1)

    def masked_scores(keys, mask):
        width = keys.shape[0]
        scores = scale * lax.dot_general(
            query_rows, keys, LAST_DIMS, preferred_element_type=jnp.float32
        )
        return jnp.where(mask[None], scores.reshape(heads, tokens_row, width), NEG)

    score_list = [
        masked_scores(
            turn(fresh[...])[:, :head_width],
            (request == request_row) & (column_index <= row_index),
        )
    ]
    value_list = [fresh[:, head_width:]]
    key_groups = [page_groups(p, page_len, table, prompt) for p in range(nd * page_count)]
    for copy in page_copies:
        copy.wait_recv()
    for d in range(nd):
        shard = pages_all[d]
        mask = group == jnp.concatenate(
            key_groups[d * page_count : (d + 1) * page_count], axis=1
        )
        score_list.append(masked_scores(shard[:, :head_width], mask))
        value_list.append(shard[:, head_width:])
    sink = jnp.concatenate(
        [jnp.full((1, tokens_row, 1), sinks[h], jnp.float32) for h in range(heads)], axis=0
    )
    peak = sink
    for scores in score_list:
        peak = jnp.maximum(peak, jnp.max(scores, axis=-1, keepdims=True))
    denominator = jnp.exp(sink - peak)
    weighted = jnp.zeros((heads * tokens_row, head_width), jnp.float32)
    for scores, values in zip(score_list, value_list):
        probs = jnp.exp(scores - peak)
        denominator = denominator + jnp.sum(probs, axis=-1, keepdims=True)
        weighted = weighted + jnp.dot(
            probs.reshape(heads * tokens_row, -1).astype(jnp.bfloat16),
            values,
            preferred_element_type=jnp.float32,
        )
    attended = weighted.reshape(heads, tokens_row, head_width) / denominator
    attended = jnp.concatenate([attended[h] for h in range(heads)], axis=1).astype(jnp.bfloat16)
    holder_width = up.shape[0]
    rank_width = rank.shape[3] * nd
    columns_slot = (
        lax.broadcasted_iota(jnp.int32, (tokens_row, rank_width), 1) // rank_size
    )
    rank_all = lax.dot_general(
        attended, adapter_columns[...], LAST_DIMS, preferred_element_type=jnp.float32
    )
    rank_all = jnp.where(columns_slot == slot, rank_all, 0.0)
    for e in range(ne):
        for d in range(nd):
            rank[d, e] = rank_all[
                e * rows : (e + 1) * rows, d * holder_width : (d + 1) * holder_width
            ].astype(jnp.bfloat16)
    rank_copies, proj_copies = [], []
    for d, e in everyone:
        ti, tj = lax.rem(i + d, nd), lax.rem(j + e, ne)
        rank_copies.append(
            send(rank.at[ti, tj], rank_in.at[d, e], rank_s.at[d, e], rank_r.at[d, e], ti, tj)
        )
    loads[3].wait()
    projected = lax.dot_general(
        attended, project_matrix[...], LAST_DIMS, preferred_element_type=jnp.float32
    )
    for e in range(ne):
        proj[e] = projected[e * rows : (e + 1) * rows].astype(jnp.bfloat16)
    for e in range(1, ne):
        tj = lax.rem(j + e, ne)
        proj_copies.append(
            send(proj.at[tj], proj_in.at[e - 1], proj_s.at[e - 1], proj_r.at[e - 1], i, tj)
        )
    for copy in rank_copies:
        copy.wait()
    parts = []
    for d in range(nd):
        part = rank[i, j].astype(jnp.float32) if d == 0 else rank_in[d, 0].astype(jnp.float32)
        for e in range(1, ne):
            part = part + rank_in[d, e].astype(jnp.float32)
        parts.append(part)
    middles = jnp.concatenate(parts, axis=0).astype(jnp.bfloat16)
    updates = ADAPTER_SCALE * jnp.dot(middles, up[...], preferred_element_type=jnp.float32)
    for d in range(nd):
        delta[d] = updates[d * rows : (d + 1) * rows].astype(jnp.bfloat16)
    delta_copies = [
        send(
            delta.at[d],
            delta_in.at[d - 1],
            delta_s.at[d - 1],
            delta_r.at[d - 1],
            lax.rem(i - d + nd, nd),
            j,
        )
        for d in range(1, nd)
    ]
    for copy in proj_copies:
        copy.wait()
    total = proj[j].astype(jnp.float32)
    for e in range(1, ne):
        total = total + proj_in[e - 1].astype(jnp.float32)
    total = total + residual[...].astype(jnp.float32) + bias[...].astype(jnp.float32).reshape(1, -1)
    total = total + delta[0].astype(jnp.float32)
    for copy in delta_copies:
        copy.wait()
    for d in range(1, nd):
        total = total + delta_in[d - 1].astype(jnp.float32)
    rounded = total.astype(jnp.bfloat16)
    stream = rounded.astype(jnp.float32)
    mean_square = jnp.mean(stream * stream, axis=-1, keepdims=True)
    normed = stream * lax.rsqrt(mean_square + EPSILON) * gain[...].astype(jnp.float32).reshape(1, -1)
    gathered[j, i] = normed.astype(jnp.bfloat16)
    plane_copies = [
        send(
            gathered.at[j, i],
            gathered.at[j, i],
            plane_s.at[d - 1],
            plane_r.at[d - 1],
            lax.rem(i + d, nd),
            j,
        )
        for d in range(1, nd)
    ]
    for copy in plane_copies:
        copy.wait()
    sibling, across, along = flip(j, 1), flip(j, 2), flip(j, 4)
    chip_copies = [
        send(gathered.at[j], gathered.at[j], chip_s.at[n], chip_r.at[n], i, target)
        for n, target in enumerate((across, along, sibling))
    ]
    core = lax.rem(j, 2)
    hop_from = along + core * (across - along)
    hop_to = across + core * (along - across)
    passed = []
    chunks = (0, 2, 4, 6)
    relays = nd == 4
    unit_copies = []
    relay_copies = []

    def far(a, b):
        return (a - b) * (a - b) == 9

    def units(c):
        bits = chunks[c]
        blocks = [
            gathered[flip(j, bits + n)].astype(jnp.float32).reshape(nd * rows, -1) for n in (0, 1)
        ]
        tokens = jnp.concatenate(blocks, axis=0).astype(jnp.bfloat16)
        hidden[i, c] = expert_hidden(
            tokens, gate_matrix[...], up_matrix[...], gate_offset[...], up_offset[...]
        )
        for d in range(1, nd):
            ti = lax.rem(i + d, nd)
            copy = pltpu.make_async_remote_copy(
                src_ref=hidden.at[i, c],
                dst_ref=hidden.at[i, c],
                send_sem=unit_s.at[d - 1, c],
                recv_sem=unit_r.at[i, c],
                device_id=device(ti, j),
                device_id_type=pl.DeviceIdType.MESH,
            )
            if relays:
                skip = far(i, ti)
                unit_copies.append((copy, skip))
                pl.when(jnp.logical_not(skip))(copy.start)
            else:
                unit_copies.append((copy, None))
                copy.start()

    def arrival(item, c):
        return pltpu.make_async_remote_copy(
            src_ref=hidden.at[item, c],
            dst_ref=hidden.at[item, c],
            send_sem=relay_s.at[c],
            recv_sem=unit_r.at[item, c],
            device_id=device(lax.rem(i + 1, nd), j),
            device_id_type=pl.DeviceIdType.MESH,
        )

    inner = (i == 1) | (i == nd - 2)

    def relay(c):
        if not relays:
            return

        @pl.when(inner)
        def _():
            item = lax.rem(6 - 3 * i + 6, 6)
            arrival(item, c).wait_recv()
            pltpu.make_async_remote_copy(
                src_ref=hidden.at[item, c],
                dst_ref=hidden.at[item, c],
                send_sem=relay_s.at[c],
                recv_sem=unit_r.at[item, c],
                device_id=device(3 - item, j),
                device_id_type=pl.DeviceIdType.MESH,
            ).start()

    def pass_on(other):
        n = len(passed)
        passed.append(
            send(gathered.at[other], gathered.at[other], pass_s.at[n], pass_r.at[n], i, sibling)
        )

    out_copies = []

    def finish(c):
        for d in range(1, nd):
            item = lax.rem(i + d, nd)
            if relays:
                done = inner & (item == lax.rem(6 - 3 * i + 6, 6))
                pl.when(jnp.logical_not(done))(arrival(item, c).wait_recv)
            else:
                arrival(item, c).wait_recv()
        units_all = jnp.concatenate([hidden[d, c] for d in range(nd)], axis=1)
        result = lax.dot_general(
            units_all, down_matrix[...], LAST_DIMS, preferred_element_type=jnp.float32
        ) + down_offset[...].astype(jnp.float32)
        for n in (0, 1):
            other = flip(j, chunks[c] + n)
            for d in range(nd):
                start = (n * nd + d) * rows
                outs[other, d] = result[start : start + rows].astype(jnp.bfloat16)
            if chunks[c] + n:
                place = chunks[c] + n - 1
                out_copies.append(
                    send(
                        outs.at[other], outs_in.at[place], out_s.at[place], out_r.at[place], i, other
                    )
                )

    loads[0].wait()
    loads[1].wait()
    chip_copies[2].wait_recv()
    units(0)
    chip_copies[0].wait_recv()
    pass_on(across)
    chip_copies[1].wait_recv()
    pass_on(along)
    hop = send(gathered.at[hop_from], gathered.at[hop_from], hop_s, hop_r, i, hop_to)
    passed[0].wait_recv()
    units(1)
    relay(0)
    hop.wait_recv()
    pass_on(flip(j, 6))
    passed[1].wait_recv()
    units(2)
    relay(1)
    passed[2].wait_recv()
    units(3)
    loads[2].wait()
    finish(0)
    relay(2)
    finish(1)
    finish(2)
    relay(3)
    finish(3)
    for copy in out_copies + combine_copies:
        copy.wait_recv()
    diagonal = lax.broadcasted_iota(jnp.int32, (rows, rows), 0) == lax.broadcasted_iota(
        jnp.int32, (rows, rows), 1
    )
    for d in range(nd):
        total = 0.0
        for bits in range(ne):
            piece = outs[j, d] if bits == 0 else outs_in[bits - 1, d]
            line = weights[d, pl.ds(flip(j, bits), 1), :][:, :rows]
            factor = jnp.sum(jnp.where(diagonal, line, 0.0), axis=1, keepdims=True)
            total = total + piece.astype(jnp.float32) * factor
        sums[d] = total.astype(jnp.bfloat16)
    finals = []
    for d in range(1, nd):
        ti = lax.rem(i + d, nd)
        finals.append(send(sums.at[ti], merged.at[i], sum_s.at[d - 1], sum_r.at[d - 1], ti, j))
    merged[i] = sums[i]
    for copy, skip in unit_copies:
        if skip is None:
            copy.wait_send()
        else:
            pl.when(jnp.logical_not(skip))(copy.wait_send)
    if relays:

        @pl.when(inner)
        def _():
            for c in range(4):
                arrival(0, c).wait_send()

    for copy in chip_copies + passed + [hop] + out_copies + page_copies + combine_copies:
        copy.wait_send()
    for copy in finals:
        copy.wait()
    update = jnp.concatenate([merged[d].astype(jnp.float32) for d in range(nd)], axis=1)
    layer_out[...] = (stream + update).astype(jnp.bfloat16)


def layer(nd, ne, rank_size, page_len, front, scalars, small, matrices):
    pages = front[0]
    residual, up = small[4:6]
    rows, width = residual.shape
    units = matrices[0].shape[1]
    dma = pltpu.SemaphoreType.DMA
    held = scalars + small
    args = front + held + matrices
    vmem = pl.BlockSpec(memory_space=pltpu.VMEM)
    bf16 = jnp.bfloat16
    return pl.pallas_call(
        functools.partial(layer_body, nd, ne, rank_size, page_len, len(held)),
        out_shape=jax.ShapeDtypeStruct((rows, width), bf16),
        in_specs=[vmem] * len(front)
        + [pl.BlockSpec(memory_space=pltpu.HBM)] * len(held + matrices),
        out_specs=vmem,
        scratch_shapes=[pltpu.SMEM(x.shape, x.dtype) for x in scalars]
        + [pltpu.VMEM(x.shape, x.dtype) for x in small]
        + [
            pltpu.VMEM((nd, rows, units), bf16),
            pltpu.VMEM((ne, 128), jnp.float32),
            pltpu.VMEM((ne, rows, width), bf16),
            pltpu.VMEM((nd, ne, rows, up.shape[0]), bf16),
            pltpu.VMEM((nd,) + pages.shape, bf16),
            pltpu.VMEM((nd, ne, 128), jnp.float32),
            pltpu.VMEM(matrices[3].shape, bf16),
            pltpu.VMEM((ne, nd, rows, width), bf16),
            pltpu.VMEM((units, width), bf16),
            pltpu.VMEM((units, width), bf16),
            pltpu.VMEM((units, width), bf16),
            pltpu.VMEM((nd, 4, 2 * nd * rows, units), bf16),
            pltpu.VMEM((ne, nd, rows, units), bf16),
            pltpu.VMEM((ne - 1, nd, rows, units), bf16),
            pltpu.VMEM((nd, rows, units), bf16),
            pltpu.VMEM((ne - 1, rows, width), bf16),
            pltpu.VMEM((nd, ne, rows, up.shape[0]), bf16),
            pltpu.VMEM((nd, rows, width), bf16),
            pltpu.VMEM((nd - 1, rows, width), bf16),
            dma((nd, ne)),
            dma((nd, ne)),
            dma((ne - 1,)),
            dma((ne - 1,)),
            dma((nd - 1,)),
            dma((nd - 1,)),
            dma((nd - 1,)),
            dma((nd - 1,)),
            dma((3,)),
            dma((3,)),
            dma,
            dma,
            dma((3,)),
            dma((3,)),
            dma((4,)),
            dma((nd - 1, 4)),
            dma((nd, 4)),
            dma((4,)),
            dma((ne - 1,)),
            dma((ne - 1,)),
            dma((nd - 1,)),
            dma((nd - 1,)),
            dma((nd - 1,)),
            dma((nd - 1,)),
            dma((nd - 1,)),
            dma((nd - 1,)),
            dma((len(held),)),
        ],
        compiler_params=pltpu.CompilerParams(
            collective_id=2, has_side_effects=True, vmem_limit_bytes=60 * 2**20
        ),
    )(*args)


def on_device(
    residual,
    queries,
    fresh_key_value,
    prompt_page_cache,
    group_page_table,
    prompt_length,
    suffix_length,
    request_group,
    request_adapter_index,
    adapter_slot_index,
    adapter_down_maps,
    adapter_up_maps,
    sinks,
    output_weight,
    output_bias,
    norm_weight,
    token_experts,
    expert_gate_weight,
    expert_slot_index,
    gate_weight,
    up_weight,
    down_weight,
    gate_bias,
    up_bias,
    down_bias,
):
    heads_per_device = sinks.shape[0]
    tok_row = queries.shape[0]
    head_width = queries.shape[1] // heads_per_device
    kv_count = fresh_key_value.shape[2] // head_width
    ep_count = lax.axis_size("ep")
    data_parallel_count = lax.axis_size("dp")
    group_size = heads_per_device * ep_count // kv_count
    kv_head = lax.axis_index("ep") * heads_per_device // group_size
    tokens_per_device = tok_row // ep_count
    hidden_width = residual.shape[1]
    adapter_weights = adapter_down_maps.shape[0]
    adapter_rank_size = adapter_down_maps.shape[2]
    score_scale = 1.0 / math.sqrt(head_width)
    own_kv = lax.dynamic_slice_in_dim(fresh_key_value, kv_head * head_width, head_width, 2)
    experts = expert_slot_index.shape[0]
    top_count = token_experts.shape[1]
    capacity = max(2, 8 * tokens_per_device // experts)
    direct = experts == ep_count and ep_count == 8 and capacity >= tokens_per_device
    if direct:
        own_rows = lax.dynamic_slice_in_dim(
            prompt_page_cache, kv_head * head_width, head_width, 3
        ).reshape(-1, 2 * head_width)
        return layer(
            data_parallel_count,
            ep_count,
            adapter_rank_size,
            prompt_page_cache.shape[1],
            (
                own_rows,
                own_kv.reshape(tok_row, 2 * head_width),
            ),
            (
                suffix_length,
                request_group,
                request_adapter_index,
                adapter_slot_index,
                group_page_table.T,
                prompt_length,
                expert_slot_index,
                sinks,
            ),
            (
                queries,
                token_experts.T,
                expert_gate_weight.T,
                adapter_down_maps.transpose(0, 2, 1).reshape(-1, heads_per_device * head_width),
                residual,
                adapter_up_maps.reshape(-1, hidden_width),
                gate_bias,
                up_bias,
                down_bias,
                output_bias,
                norm_weight,
            ),
            (gate_weight, up_weight, down_weight, output_weight.T),
        )
    expert_hit = token_experts[:, :, None] == jnp.arange(experts, dtype=jnp.int32)[None, None, :]
    route_col = jnp.sum(jnp.where(expert_hit, expert_slot_index[None, None, :], 0), axis=2)
    request_local, token_group, positions, token_slot = token_layout(
        suffix_length[0],
        request_group,
        request_adapter_index,
        adapter_slot_index,
        prompt_length,
        tok_row,
    )
    queries_rot = rotate(
        queries.reshape(tok_row, heads_per_device, head_width).astype(jnp.float32), positions
    ).astype(jnp.bfloat16)
    keys_new = rotate(own_kv[:, 0:1, :].astype(jnp.float32), positions)[:, 0, :].astype(
        jnp.bfloat16
    )
    values_new = own_kv[:, 1, :]
    token_index = jnp.arange(tok_row, dtype=jnp.int32)
    allowed = (request_local[:, None] == request_local[None, :]) & (
        token_index[None, :] <= token_index[:, None]
    )
    local_scores = (
        jnp.einsum("thd,sd->hts", queries_rot, keys_new, preferred_element_type=jnp.float32)
        * score_scale
    )
    local_masked = jnp.where(allowed[None], local_scores, NEG)
    sink_col = sinks[:, None]
    run_max = jnp.maximum(sink_col, jnp.max(local_masked, axis=-1))
    local_exp = jnp.exp(local_masked - run_max[..., None])
    run_total = jnp.exp(sink_col - run_max) + jnp.sum(local_exp, axis=-1)
    run_acc = jnp.einsum(
        "hts,sd->htd",
        local_exp.astype(jnp.bfloat16),
        values_new,
        preferred_element_type=jnp.float32,
    )
    page_len = prompt_page_cache.shape[1]
    pool_total = prompt_page_cache.shape[0] * data_parallel_count
    page_group, page_slot, page_used = page_layout(group_page_table, pool_total)
    group_hit = page_group[:, None] == jnp.arange(prompt_length.shape[0], dtype=jnp.int32)[None, :]
    page_limit = jnp.sum(jnp.where(group_hit, prompt_length[None, :], 0), axis=1)
    own_pages = lax.dynamic_slice_in_dim(prompt_page_cache, kv_head * head_width, head_width, 3)
    shard_rows = lax.all_gather(own_pages, "dp", axis=0, tiled=True)
    piece_pages = shard_rows.shape[0]
    keys_piece = shard_rows[:, :, 0, :].reshape(piece_pages * page_len, head_width)
    values_piece = shard_rows[:, :, 1, :].reshape(piece_pages * page_len, head_width)
    key_pos = page_slot[:, None] * page_len + jnp.arange(page_len, dtype=jnp.int32)[None, :]
    key_valid = (page_used[:, None] & (key_pos < page_limit[:, None])).reshape(-1)
    key_group = jnp.broadcast_to(page_group[:, None], (piece_pages, page_len)).reshape(-1)
    visible = (token_group[:, None] == key_group[None, :]) & key_valid[None, :]
    scores = (
        jnp.einsum("thd,sd->hts", queries_rot, keys_piece, preferred_element_type=jnp.float32)
        * score_scale
    )
    masked = jnp.where(visible[None], scores, NEG)
    new_max = jnp.maximum(run_max, jnp.max(masked, axis=-1))
    factor = jnp.exp(run_max - new_max)
    weights = jnp.exp(masked - new_max[..., None])
    new_total = run_total * factor + jnp.sum(weights, axis=-1)
    new_acc = run_acc * factor[..., None] + jnp.einsum(
        "hts,sd->htd",
        weights.astype(jnp.bfloat16),
        values_piece,
        preferred_element_type=jnp.float32,
    )
    attention_output = (
        (new_acc / new_total[..., None])
        .transpose(1, 0, 2)
        .reshape(tok_row, heads_per_device * head_width)
        .astype(jnp.bfloat16)
    )
    adapter_onehot = token_slot[:, None] == jnp.arange(adapter_weights, dtype=jnp.int32)[None, :]
    adapter_pick_all = adapter_onehot.astype(jnp.float32)
    adapter_columns = adapter_down_maps.transpose(1, 0, 2).reshape(
        heads_per_device * head_width, adapter_weights * adapter_rank_size
    )
    projected_rows = jnp.dot(attention_output, output_weight, preferred_element_type=jnp.float32)
    reduced_rank = jnp.dot(
        attention_output, adapter_columns, preferred_element_type=jnp.float32
    ).reshape(tokens_per_device * lax.axis_size("ep"), adapter_weights, adapter_rank_size)
    reduced_rank = jnp.sum(reduced_rank * adapter_pick_all[:, :, None], axis=1)
    summed_rows = lax.psum_scatter(
        jnp.concatenate([projected_rows, reduced_rank], axis=1).astype(jnp.bfloat16),
        "ep",
        scatter_dimension=0,
        tiled=True,
    ).astype(jnp.float32)
    projection_sum = summed_rows[:, :hidden_width]
    adapter_middle = summed_rows[:, hidden_width:].astype(jnp.bfloat16)
    owner_onehot = lax.dynamic_slice_in_dim(
        adapter_onehot, lax.axis_index("ep") * tokens_per_device, tokens_per_device, 0
    )
    spread_rows = owner_onehot.astype(jnp.bfloat16)[:, :, None] * adapter_middle[:, None, :]
    holder_count = adapter_up_maps.shape[0]
    outgoing = spread_rows.reshape(
        tokens_per_device, data_parallel_count, holder_count * adapter_rank_size
    )
    incoming = lax.all_to_all(outgoing, "dp", split_axis=1, concat_axis=0, tiled=True)
    adapter_updates = jnp.dot(
        incoming.reshape(data_parallel_count * tokens_per_device, holder_count * adapter_rank_size),
        adapter_up_maps.reshape(holder_count * adapter_rank_size, hidden_width),
        preferred_element_type=jnp.float32,
    )
    adapter_updates = (
        (ADAPTER_SCALE * adapter_updates)
        .astype(jnp.bfloat16)
        .reshape(data_parallel_count, tokens_per_device, hidden_width)
    )
    returned_rows = lax.all_to_all(adapter_updates, "dp", split_axis=0, concat_axis=0, tiled=True)
    adapter_update = jnp.sum(returned_rows.astype(jnp.float32), axis=0)
    stream = settle(
        residual.astype(jnp.float32)
        + projection_sum
        + output_bias.astype(jnp.float32)
        + adapter_update
    )
    mean_square = jnp.mean(stream * stream, axis=-1, keepdims=True)
    normed = (stream * lax.rsqrt(mean_square + EPSILON) * norm_weight.astype(jnp.float32)).astype(
        jnp.bfloat16
    )
    slots_all = ep_count * capacity
    route_col = route_col.reshape(-1)
    col_hot = (route_col[:, None] == jnp.arange(ep_count, dtype=jnp.int32)[None, :]).astype(
        jnp.int32
    )
    route_order = jnp.arange(route_col.shape[0], dtype=jnp.int32)
    earlier = (route_order[None, :] < route_order[:, None]).astype(jnp.int32)
    route_rank = jnp.sum(earlier * (route_col[None, :] == route_col[:, None]), axis=1)
    target_slot = route_col * capacity + route_rank
    target_hot = (target_slot[:, None] == jnp.arange(slots_all, dtype=jnp.int32)[None, :]).reshape(
        tokens_per_device, top_count, slots_all
    )
    scatter_rows = jnp.sum(target_hot.astype(jnp.float32), axis=1)
    combine = jnp.sum(jnp.where(target_hot, expert_gate_weight[:, :, None], 0.0), axis=1)
    outbound = (
        jnp.dot(scatter_rows.T.astype(jnp.bfloat16), normed, preferred_element_type=jnp.float32)
        .astype(jnp.bfloat16)
        .reshape(ep_count, capacity, hidden_width)
    )
    received = lax.all_to_all(outbound, "ep", split_axis=0, concat_axis=0, tiled=True)
    rows_flat = lax.all_gather(received[None], "dp", axis=0, tiled=True).reshape(-1, hidden_width)
    hidden = expert_hidden(rows_flat, gate_weight[0], up_weight[0], gate_bias[0], up_bias[0])
    unit_weights = down_weight[0]
    unit_sum = lax.dot_general(
        lax.all_gather(hidden, "dp", axis=1, tiled=True),
        unit_weights,
        LAST_DIMS,
        preferred_element_type=jnp.float32,
    )
    expert_out = (
        (unit_sum + down_bias[0].astype(jnp.float32))
        .astype(jnp.bfloat16)
        .reshape(data_parallel_count, slots_all, -1)
    )
    home_rows = lax.all_to_all(expert_out, "dp", split_axis=0, concat_axis=2, tiled=True)
    back_rows = lax.all_to_all(
        home_rows.reshape(ep_count, capacity, hidden_width),
        "ep",
        split_axis=0,
        concat_axis=0,
        tiled=True,
    )
    merged = jnp.dot(
        combine,
        back_rows.reshape(slots_all, hidden_width).astype(jnp.float32),
        precision=lax.Precision.HIGHEST,
        preferred_element_type=jnp.float32,
    )
    return (stream + merged).astype(jnp.bfloat16)


def solution(mesh):
    placed = (
        P(("dp", "ep"), None),
        P("dp", "ep"),
        P("dp", None, None),
        P("dp", None, None, None),
        P(),
        P(),
        P("dp", None),
        P("dp"),
        P("dp"),
        P(),
        P(None, "ep", None),
        P("dp", None, None),
        P("ep"),
        P("ep", None),
        P(),
        P(),
        P(("dp", "ep"), None),
        P(("dp", "ep"), None),
        P(),
        P("ep", "dp", None),
        P("ep", "dp", None),
        P("ep", "dp", None),
        P("ep", "dp"),
        P("ep", "dp"),
        P("ep", "dp"),
    )
    return jax.shard_map(
        on_device, mesh=mesh, in_specs=placed, out_specs=P(("dp", "ep"), None), check_vma=False
    )
```

```python
import functools
import math

import jax
import jax.numpy as jnp
from jax import lax
from jax.experimental import pallas as pl
from jax.experimental.pallas import tpu as pltpu
from jax.sharding import PartitionSpec as P

THETA = 150000.0
NEG = -1e30
LIMIT = 7.0
ALPHA = 1.702
EPSILON = 1e-05
ADAPTER_SCALE = 2.0
LAST_DIMS = (((1,), (1,)), ((), ()))


def settle(values):
    return lax.optimization_barrier(values.astype(jnp.bfloat16)).astype(jnp.float32)


def rotate(values, positions):
    head_width = values.shape[-1]
    half_size = head_width // 2
    frequency = THETA ** (-2.0 * jnp.arange(half_size, dtype=jnp.float32) / head_width)
    angles = positions.astype(jnp.float32)[:, None] * frequency[None, :]
    cosine = jnp.cos(angles)[:, None, :]
    sine_part = jnp.sin(angles)[:, None, :]
    front_part = values[..., :half_size]
    back_part = values[..., half_size:]
    return jnp.concatenate(
        [front_part * cosine - back_part * sine_part, back_part * cosine + front_part * sine_part],
        axis=-1,
    )


def token_layout(lengths, groups, request_adapter, adapter_slot_index, prompt_length, tok_count):
    order = jnp.arange(lengths.shape[0], dtype=jnp.int32)
    finish = jnp.sum(jnp.where(order[None, :] <= order[:, None], lengths[None, :], 0), axis=1)
    starts = finish - lengths
    token_index = jnp.arange(tok_count, dtype=jnp.int32)
    member = (token_index[:, None] >= starts[None, :]) & (token_index[:, None] < finish[None, :])
    member_int = member.astype(jnp.int32)
    request_local = jnp.sum(
        member_int * jnp.arange(lengths.shape[0], dtype=jnp.int32)[None, :], axis=1
    )
    token_group = jnp.sum(member_int * groups[None, :], axis=1)
    offset = token_index - jnp.sum(member_int * starts[None, :], axis=1)
    group_hit = token_group[:, None] == jnp.arange(prompt_length.shape[0], dtype=jnp.int32)[None, :]
    prompt_base = jnp.sum(jnp.where(group_hit, prompt_length[None, :], 0), axis=1)
    token_adapter = jnp.sum(member_int * request_adapter[None, :], axis=1)
    id_hit = (
        token_adapter[:, None] == jnp.arange(adapter_slot_index.shape[0], dtype=jnp.int32)[None, :]
    )
    token_slot = jnp.sum(jnp.where(id_hit, adapter_slot_index[None, :], 0), axis=1)
    return (request_local, token_group, prompt_base + offset, token_slot)


def page_layout(group_page_table, pool_total):
    page_ids = jnp.arange(pool_total, dtype=jnp.int32)
    matches = group_page_table[:, :, None] == page_ids[None, None, :]
    match_int = matches.astype(jnp.int32)
    group_ids = jnp.arange(group_page_table.shape[0], dtype=jnp.int32)
    slot_ids = jnp.arange(group_page_table.shape[1], dtype=jnp.int32)
    page_group = jnp.sum(match_int * group_ids[:, None, None], axis=(0, 1))
    page_slot = jnp.sum(match_int * slot_ids[None, :, None], axis=(0, 1))
    page_used = jnp.sum(match_int, axis=(0, 1)) > 0
    return (page_group, page_slot, page_used)


def expert_hidden(rows, gate_matrix, up_matrix, gate_offset, up_offset):
    gate_pre = lax.dot_general(
        rows, gate_matrix, LAST_DIMS, preferred_element_type=jnp.float32
    ) + gate_offset.astype(jnp.float32)
    up_pre = lax.dot_general(
        rows, up_matrix, LAST_DIMS, preferred_element_type=jnp.float32
    ) + up_offset.astype(jnp.float32)
    gate_pre = jnp.minimum(gate_pre, LIMIT)
    up_pre = jnp.clip(up_pre, -LIMIT, LIMIT)
    return ((up_pre + 1.0) * gate_pre * jax.nn.sigmoid(ALPHA * gate_pre)).astype(jnp.bfloat16)


def device(dp, ep):
    return {"dp": dp, "ep": ep}


def send(src, dst, send_sem, recv_sem, dp, ep):
    copy = pltpu.make_async_remote_copy(
        src_ref=src,
        dst_ref=dst,
        send_sem=send_sem,
        recv_sem=recv_sem,
        device_id=device(dp, ep),
        device_id_type=pl.DeviceIdType.MESH,
    )
    copy.start()
    return copy


def greet(peers):
    barrier = pltpu.get_barrier_semaphore()
    for dp, ep in peers:
        pl.semaphore_signal(
            barrier, inc=1, device_id=device(dp, ep), device_id_type=pl.DeviceIdType.MESH
        )
    pl.semaphore_wait(barrier, len(peers))


def flip(index, bits):
    out = index
    for bit in (1, 2, 4):
        if bits & bit:
            out = out + bit * (1 - 2 * ((index // bit) % 2))
    return out


def token_fields(tokens, axis, lengths, groups, adapters, slots, prompt):
    shape = (tokens, 1) if axis == 0 else (1, tokens)
    token = lax.broadcasted_iota(jnp.int32, shape, axis)
    zero = jnp.zeros(shape, jnp.int32)
    request, group, position, slot = zero, zero, zero, zero
    start = lengths[0, 0] * 0
    for m in range(lengths.shape[1]):
        finish = start + lengths[0, m]
        inside = (token >= start) & (token < finish)
        request = jnp.where(inside, m, request)
        if axis == 0:
            group = jnp.where(inside, groups[m], group)
            position = jnp.where(inside, token - start + prompt[groups[m]], position)
            slot = jnp.where(inside, slots[adapters[m]], slot)
        start = finish
    return request, group, position, slot


def rotation(positions, head_width, lanes):
    half = head_width // 2
    lane = lax.broadcasted_iota(jnp.int32, (positions.shape[0], lanes), 1)
    place = lax.rem(lane, half).astype(jnp.float32)
    frequency = jnp.exp(place * (-2.0 * math.log(THETA) / head_width))
    angles = positions.astype(jnp.float32) * frequency
    cosine, sine = jnp.cos(angles), jnp.sin(angles)
    front = lax.rem(lane, head_width) < half
    signed = jnp.where(front, -sine, sine)

    def turn(values):
        values = values.astype(jnp.float32)
        partner = jnp.where(
            front, pltpu.roll(values, lanes - half, 1), pltpu.roll(values, half, 1)
        )
        return (values * cosine + partner * signed).astype(jnp.bfloat16)

    return turn


def page_groups(page, page_len, table, prompt):
    group, limit = jnp.int32(-1), jnp.int32(0)
    for s in range(table.shape[0]):
        for g in range(table.shape[1]):
            hit = table[s, g] == page
            group = jnp.where(hit, g, group)
            limit = jnp.where(hit, prompt[g] - s * page_len, limit)
    lane = lax.broadcasted_iota(jnp.int32, (1, page_len), 1)
    return jnp.where(lane < limit, group, -1)


def line_peers(i, nd):
    if nd != 4:
        return [lax.rem(i + d, nd) for d in range(1, nd)]
    high = i // 2
    return [3 * (1 - high), 2 - high, (1 - i) * (1 - high) + (5 - i) * high]


def spread(src, dst, send_sem, recv_sem, peers, i, j):
    return [send(src, dst, send_sem.at[n], recv_sem.at[i], t, j) for n, t in enumerate(peers)]


def collect(block, send_sem, recv_sem, peers, j):
    for n, t in enumerate(peers):
        pltpu.make_async_remote_copy(
            src_ref=block(t),
            dst_ref=block(t),
            send_sem=send_sem.at[n],
            recv_sem=recv_sem.at[t],
            device_id=device(t, j),
            device_id_type=pl.DeviceIdType.MESH,
        ).wait_recv()


def own_heads(wide, half, head_width):
    keys, values = wide[:, 0, :].astype(jnp.float32), wide[:, 1, :].astype(jnp.float32)
    lane = lax.broadcasted_iota(jnp.int32, keys.shape, 1)
    keys = jnp.where(half == 0, keys, pltpu.roll(keys, head_width, 1))
    values = jnp.where(half == 0, pltpu.roll(values, head_width, 1), values)
    return jnp.where(lane < head_width, keys, values).astype(jnp.bfloat16)


def layer_body(
    nd,
    ne,
    rank_size,
    head_width,
    small_count,
    pages_hbm,
    fresh_hbm,
    *rest,
):
    small_hbm, rest = rest[:small_count], rest[small_count:]
    (gate_hbm, up_hbm, down_hbm, project_hbm, layer_out), rest = rest[:5], rest[5:]
    small, rest = rest[:small_count], rest[small_count:]
    (
        lengths,
        groups,
        adapters,
        slots,
        table,
        prompt,
        expert_slots,
        sinks,
        queries,
        route_experts,
        route_weights,
        adapter_columns,
        residual,
        up,
        gate_offset,
        up_offset,
        down_offset,
        bias,
        gain,
    ) = small
    (
        pages_wide,
        fresh_wide,
        merged,
        combine,
        proj,
        proj_wide,
        pair_out,
        pair_in,
        rank,
        pages_all,
        weights,
        project_matrix,
        gathered,
        gate_matrix,
        up_matrix,
        down_matrix,
        down_parts,
        hidden,
        outs,
        outs_in,
        sums,
        proj_in,
        rank_in,
        up_wide,
        up_part,
        delta,
        delta_full,
        rank_s,
        rank_r,
        proj_s,
        proj_r,
        pair_s,
        pair_r,
        delta_s,
        delta_r,
        wide_s,
        wide_r,
        plane_s,
        plane_r,
        chip_s,
        chip_r,
        hop_s,
        hop_r,
        pass_s,
        pass_r,
        load_sem,
        unit_s,
        unit_r,
        relay_s,
        out_s,
        out_r,
        sum_s,
        sum_r,
        page_s,
        page_r,
        combine_s,
        combine_r,
        small_sem,
        wide_sem,
    ) = rest
    i, j = lax.axis_index("dp"), lax.axis_index("ep")
    heads = sinks.shape[0]
    lanes = 2 * head_width
    page_count, page_len = pages_hbm.shape[:2]
    kv_head = j * (fresh_hbm.shape[2] // head_width) // ne
    block = pl.ds(pl.multiple_of(kv_head // 2 * lanes, lanes), lanes)
    head_loads = [
        pltpu.make_async_copy(pages_hbm.at[:, :, :, block], pages_wide, wide_sem.at[0]),
        pltpu.make_async_copy(fresh_hbm.at[:, :, block], fresh_wide, wide_sem.at[1]),
    ]
    for copy in head_loads:
        copy.start()
    peers = line_peers(i, nd)

    def carry(block, send_sem, recv_sem, target):
        return pltpu.make_async_remote_copy(
            src_ref=block,
            dst_ref=block,
            send_sem=send_sem,
            recv_sem=recv_sem,
            device_id=device(target, j),
            device_id_type=pl.DeviceIdType.MESH,
        )

    def skips(target):
        apart = (i - target) * (i - target)
        return (apart == 9) | (inner & (apart == 4))

    def unless(skip, action):
        if skip is None:
            action()
        else:
            pl.when(jnp.logical_not(skip))(action)

    loads = [
        pltpu.make_async_copy(source, target, load_sem.at[n])
        for n, (source, target) in enumerate(
            (
                (gate_hbm.at[0], gate_matrix),
                (up_hbm.at[0], up_matrix),
                (down_hbm.at[0], down_matrix),
                (project_hbm, project_matrix),
            )
        )
    ]
    small_loads = [
        pltpu.make_async_copy(source, target, small_sem.at[n])
        for n, (source, target) in enumerate(zip(small_hbm, small))
    ]
    for copy in small_loads:
        copy.start()
    half = lax.rem(kv_head, 2)
    head_loads[0].wait()
    pages_all[i] = own_heads(
        pages_wide[...].reshape(page_count * page_len, 2, lanes), half, head_width
    )
    everyone = [(d, e) for d in range(nd) for e in range(ne) if d or e]
    greet([(lax.rem(i + d, nd), lax.rem(j + e, ne)) for d, e in everyone])
    relays = nd == 4
    inner = (i == 1) | (i == nd - 2)
    far_item = lax.rem(6 - 3 * i + 6, 6)
    end = 3 - far_item
    page_copies = spread(pages_all.at[i], pages_all.at[i], page_s, page_r, peers, i, j)
    head_loads[1].wait()
    for copy in small_loads:
        copy.wait()
    for n in (3, 0, 1, 2):
        loads[n].start()
    rows = residual.shape[0]
    experts_of = route_experts[...]
    holders = jnp.zeros_like(experts_of)
    for e in range(expert_slots.shape[0]):
        holders = jnp.where(experts_of == e, expert_slots[e], holders)
    combine[...] = jnp.zeros_like(combine)
    for e in range(ne):
        combine[e : e + 1, :rows] = jnp.sum(
            jnp.where(holders == e, route_weights[...], 0.0), axis=0, keepdims=True
        )
    combine_copies = spread(combine, weights.at[i], combine_s, combine_r, peers, i, j)
    weights[i] = combine[...]
    tokens_row = queries.shape[0]
    fresh = own_heads(fresh_wide[...], half, head_width)
    scale = 1.0 / math.sqrt(head_width)
    request, group, position, slot = token_fields(
        tokens_row, 0, lengths, groups, adapters, slots, prompt
    )
    request_row = token_fields(tokens_row, 1, lengths, groups, adapters, slots, prompt)[0]
    turn = rotation(position, head_width, lanes)
    turned = [turn(queries[:, n * lanes : (n + 1) * lanes]) for n in range(heads // 2)]
    query_rows = jnp.concatenate(
        [pair[:, n * head_width : (n + 1) * head_width] for pair in turned for n in (0, 1)], axis=0
    )
    row_index = lax.broadcasted_iota(jnp.int32, (tokens_row, tokens_row), 0)
    column_index = lax.broadcasted_iota(jnp.int32, (tokens_row, tokens_row), 1)

    def masked_scores(keys, mask):
        width = keys.shape[0]
        scores = scale * lax.dot_general(
            query_rows, keys, LAST_DIMS, preferred_element_type=jnp.float32
        )
        return jnp.where(mask[None], scores.reshape(heads, tokens_row, width), NEG)

    score_list = [
        masked_scores(
            turn(fresh)[:, :head_width],
            (request == request_row) & (column_index <= row_index),
        )
    ]
    value_list = [fresh[:, head_width:]]
    key_groups = [page_groups(p, page_len, table, prompt) for p in range(nd * page_count)]
    collect(lambda t: pages_all.at[t], page_s, page_r, peers, j)
    width, part = residual.shape[1], delta.shape[2]
    own_part = pl.ds(pl.multiple_of(j * part, part), part)
    up_wide[:, :width] = up[...]
    up_wide[:, width:] = jnp.zeros((up.shape[0], ne * part - width), jnp.bfloat16)
    up_part[i] = up_wide[:, own_part]
    wide_copies = spread(up_wide.at[:, own_part], up_part.at[i], wide_s, wide_r, peers, i, j)
    for d in range(nd):
        shard = pages_all[d]
        mask = group == jnp.concatenate(
            key_groups[d * page_count : (d + 1) * page_count], axis=1
        )
        score_list.append(masked_scores(shard[:, :head_width], mask))
        value_list.append(shard[:, head_width:])
    sink = jnp.concatenate(
        [jnp.full((1, tokens_row, 1), sinks[h], jnp.float32) for h in range(heads)], axis=0
    )
    peak = sink
    for scores in score_list:
        peak = jnp.maximum(peak, jnp.max(scores, axis=-1, keepdims=True))
    denominator = jnp.exp(sink - peak)
    weighted = jnp.zeros((heads * tokens_row, head_width), jnp.float32)
    for scores, values in zip(score_list, value_list):
        probs = jnp.exp(scores - peak)
        denominator = denominator + jnp.sum(probs, axis=-1, keepdims=True)
        weighted = weighted + jnp.dot(
            probs.reshape(heads * tokens_row, -1).astype(jnp.bfloat16),
            values,
            preferred_element_type=jnp.float32,
        )
    attended = weighted.reshape(heads, tokens_row, head_width) / denominator
    attended = jnp.concatenate([attended[h] for h in range(heads)], axis=1).astype(jnp.bfloat16)
    rank_width = nd * up.shape[0]
    slot_columns = (
        lax.broadcasted_iota(jnp.int32, (tokens_row, rank_width), 1) // rank_size == slot
    )
    fold = rank.shape[1]
    rank_all = lax.dot_general(
        attended, adapter_columns[...], LAST_DIMS, preferred_element_type=jnp.float32
    )
    rank_all = jnp.where(slot_columns, rank_all, 0.0)
    rank_sum = rank_all[:, :fold]
    for n in range(1, rank_width // fold):
        rank_sum = rank_sum + rank_all[:, n * fold : (n + 1) * fold]
    rank[...] = rank_sum.astype(jnp.bfloat16)
    rank_copies, proj_copies = [], []
    for e in range(1, ne):
        rank_copies.append(
            send(
                rank, rank_in.at[e - 1], rank_s.at[e - 1], rank_r.at[e - 1], i, lax.rem(j + e, ne)
            )
        )
    loads[3].wait()
    projected = lax.dot_general(
        attended, project_matrix[...], LAST_DIMS, preferred_element_type=jnp.float32
    )
    for e in range(ne):
        proj_wide[e] = projected[e * rows : (e + 1) * rows]
    turns = (6, 2, 4, 0)
    pair_copies = []
    for n, bits in enumerate(turns):
        pair_out[n] = proj_wide[flip(j, bits + 1)].astype(jnp.bfloat16)
        pair_copies.append(
            send(pair_out.at[n], pair_in.at[n], pair_s.at[n], pair_r.at[n], i, flip(j, 1))
        )
    for n, bits in enumerate(turns):
        pair_copies[n].wait_recv()
        total = proj_wide[flip(j, bits)] + pair_in[n].astype(jnp.float32)
        if bits:
            proj[n] = total.astype(jnp.bfloat16)
            proj_copies.append(
                send(proj.at[n], proj_in.at[n], proj_s.at[n], proj_r.at[n], i, flip(j, bits))
            )
    for copy in rank_copies:
        copy.wait()
    collect(lambda t: up_part.at[t], wide_s, wide_r, peers, j)
    middle = rank[...].astype(jnp.float32)
    for e in range(1, ne):
        middle = middle + rank_in[e - 1].astype(jnp.float32)
    middles = jnp.concatenate([middle] * (rank_width // fold), axis=1)
    middles = jnp.where(slot_columns, middles, 0.0).astype(jnp.bfloat16)
    updates = 0.0
    for d in range(nd):
        updates = updates + jnp.dot(
            middles[:, d * up.shape[0] : (d + 1) * up.shape[0]],
            up_part[d],
            preferred_element_type=jnp.float32,
        )
    updates = ADAPTER_SCALE * updates
    for e in range(ne):
        delta[e] = updates[e * rows : (e + 1) * rows].astype(jnp.bfloat16)
    delta_full[:, own_part] = delta[j]
    delta_copies = []
    for e in range(1, ne):
        tj = lax.rem(j + e, ne)
        delta_copies.append(
            send(
                delta.at[tj],
                delta_full.at[:, own_part],
                delta_s.at[e - 1],
                delta_r.at[e - 1],
                i,
                tj,
            )
        )
    for copy in proj_copies:
        copy.wait()
    for n in range(3):
        total = total + proj_in[n].astype(jnp.float32)
    total = total + residual[...].astype(jnp.float32) + bias[...].astype(jnp.float32).reshape(1, -1)
    for copy in delta_copies:
        copy.wait()
    total = total + delta_full[:, :width].astype(jnp.float32)
    rounded = total.astype(jnp.bfloat16)
    stream = rounded.astype(jnp.float32)
    mean_square = jnp.mean(stream * stream, axis=-1, keepdims=True)
    normed = stream * lax.rsqrt(mean_square + EPSILON) * gain[...].astype(jnp.float32).reshape(1, -1)
    gathered[j, i] = normed.astype(jnp.bfloat16)
    plane_copies = spread(gathered.at[j, i], gathered.at[j, i], plane_s, plane_r, peers, i, j)
    sibling, across, along = flip(j, 1), flip(j, 2), flip(j, 4)
    chip_copies = []

    def to_chips(d):
        for n, target in enumerate((across, along, sibling)):
            piece = gathered.at[j, d]
            chip_copies.append(send(piece, piece, chip_s.at[n, d], chip_r.at[n, d], i, target))

    to_chips(i)
    loads[2].wait()
    units_own = down_parts.shape[2]
    for d in range(nd):
        down_parts[d] = down_matrix[:, d * units_own : (d + 1) * units_own]
    for t in reversed(peers):
        carry(gathered.at[j, t], plane_s.at[0], plane_r.at[t], t).wait_recv()
        to_chips(t)

    def from_chip(n, source):
        for d in range(nd):
            piece = gathered.at[source, d]
            pltpu.make_async_remote_copy(
                src_ref=piece,
                dst_ref=piece,
                send_sem=chip_s.at[n, d],
                recv_sem=chip_r.at[n, d],
                device_id=device(i, source),
                device_id_type=pl.DeviceIdType.MESH,
            ).wait_recv()

    core = lax.rem(j, 2)
    hop_from = along + core * (across - along)
    hop_to = across + core * (along - across)
    passed = []
    chunks = (0, 2, 4, 6)
    unit_copies = []

    def units(c):
        bits = chunks[c]
        blocks = [
            gathered[flip(j, bits + n)].astype(jnp.float32).reshape(nd * rows, -1) for n in (0, 1)
        ]
        tokens = jnp.concatenate(blocks, axis=0).astype(jnp.bfloat16)
        hidden[i, c] = expert_hidden(
            tokens, gate_matrix[...], up_matrix[...], gate_offset[...], up_offset[...]
        )
        for d, ti in enumerate(peers, 1):
            copy = carry(hidden.at[i, c], unit_s.at[d - 1, c], unit_r.at[i, c], ti)
            skip = skips(ti) if relays else None
            unit_copies.append((copy, skip))
            unless(skip, copy.start)

    def passage(item, c, n):
        return carry(hidden.at[item, c], relay_s.at[n, c], unit_r.at[item, c], end)

    def arrival(item, c):
        return carry(hidden.at[item, c], unit_s.at[0, c], unit_r.at[item, c], item)

    def relay(c, before):
        if not relays:
            return

        @pl.when(inner)
        def _():
            for n, item in enumerate((3 - i, far_item)):
                arrival(item, c).wait_recv()
                if before is not None:
                    passage(item, before, n).wait_send()
                passage(item, c, n).start()

    def pass_on(other):
        n = len(passed)
        passed.append(
            send(gathered.at[other], gathered.at[other], pass_s.at[n], pass_r.at[n], i, sibling)
        )

    out_copies = []

    def finish(c):
        result = down_offset[...].astype(jnp.float32) + lax.dot_general(
            hidden[i, c], down_parts[i], LAST_DIMS, preferred_element_type=jnp.float32
        )
        for item in reversed(peers):
            unless(inner & (item != end) if relays else None, arrival(item, c).wait_recv)
            result = result + lax.dot_general(
                hidden[item, c], down_parts[item], LAST_DIMS, preferred_element_type=jnp.float32
            )
        for n in (0, 1):
            other = flip(j, chunks[c] + n)
            for d in range(nd):
                start = (n * nd + d) * rows
                outs[other, d] = result[start : start + rows].astype(jnp.bfloat16)
            if chunks[c] + n:
                place = chunks[c] + n - 1
                out_copies.append(
                    send(
                        outs.at[other], outs_in.at[place], out_s.at[place], out_r.at[place], i, other
                    )
                )

    loads[0].wait()
    loads[1].wait()
    from_chip(2, sibling)
    units(0)
    from_chip(0, across)
    pass_on(across)
    from_chip(1, along)
    pass_on(along)
    hop = send(gathered.at[hop_from], gathered.at[hop_from], hop_s, hop_r, i, hop_to)
    passed[0].wait_recv()
    units(1)
    hop.wait_recv()
    pass_on(flip(j, 6))
    passed[1].wait_recv()
    units(2)
    relay(1, None)
    passed[2].wait_recv()
    units(3)
    for c in (2, 3, 0):
        relay(c, (3, None, 1, 2)[c])
        finish((3, None, 1, 2)[c])
    finish(0)
    for copy in out_copies:
        copy.wait_recv()
    collect(lambda t: weights.at[t], combine_s, combine_r, peers, j)
    diagonal = lax.broadcasted_iota(jnp.int32, (rows, rows), 0) == lax.broadcasted_iota(
        jnp.int32, (rows, rows), 1
    )
    for d in range(nd):
        total = 0.0
        for bits in range(ne):
            piece = outs[j, d] if bits == 0 else outs_in[bits - 1, d]
            line = weights[d, pl.ds(flip(j, bits), 1), :][:, :rows]
            factor = jnp.sum(jnp.where(diagonal, line, 0.0), axis=1, keepdims=True)
            total = total + piece.astype(jnp.float32) * factor
        sums[d] = total.astype(jnp.bfloat16)
    finals = [
        send(sums.at[t], merged.at[i], sum_s.at[n], sum_r.at[i], t, j)
        for n, t in enumerate(peers)
    ]
    merged[i] = sums[i]
    for copy, skip in unit_copies:
        unless(skip, copy.wait_send)
    if relays:

        @pl.when(inner)
        def _():
            for n in (0, 1):
                passage(0, 0, n).wait_send()

    waiting = chip_copies + passed + [hop] + out_copies + page_copies + combine_copies
    for copy in waiting + plane_copies + wide_copies + pair_copies:
        copy.wait_send()
    for copy in finals:
        copy.wait_send()
    collect(lambda t: merged.at[t], sum_s, sum_r, peers, j)
    update = jnp.concatenate([merged[d].astype(jnp.float32) for d in range(nd)], axis=1)
    layer_out[...] = (stream + update).astype(jnp.bfloat16)


def layer(nd, ne, rank_size, head_width, front, scalars, small, matrices):
    caches, fresh = front
    lanes = 2 * head_width
    page_rows = caches.shape[0] * caches.shape[1]
    residual, up = small[4:6]
    rows, width = residual.shape
    part = -(-width // (128 * ne)) * 128
    units = matrices[0].shape[1]
    dma = pltpu.SemaphoreType.DMA
    held = scalars + small
    args = front + held + matrices
    vmem = pl.BlockSpec(memory_space=pltpu.VMEM)
    bf16 = jnp.bfloat16
    return pl.pallas_call(
        functools.partial(layer_body, nd, ne, rank_size, head_width, len(held)),
        out_shape=jax.ShapeDtypeStruct((rows, width), bf16),
        in_specs=[pl.BlockSpec(memory_space=pltpu.HBM)] * len(args),
        out_specs=vmem,
        scratch_shapes=[pltpu.SMEM(x.shape, x.dtype) for x in scalars]
        + [pltpu.VMEM(x.shape, x.dtype) for x in small]
        + [
            pltpu.VMEM(caches.shape[:3] + (lanes,), bf16),
            pltpu.VMEM(fresh.shape[:2] + (lanes,), bf16),
            pltpu.VMEM((nd, rows, units), bf16),
            pltpu.VMEM((ne, 128), jnp.float32),
            pltpu.VMEM((3, rows, width), bf16),
            pltpu.VMEM((ne, rows, width), jnp.float32),
            pltpu.VMEM((4, rows, width), bf16),
            pltpu.VMEM((4, rows, width), bf16),
            pltpu.VMEM((small[0].shape[0], 128), bf16),
            pltpu.VMEM((nd, page_rows, lanes), bf16),
            pltpu.VMEM((nd, ne, 128), jnp.float32),
            pltpu.VMEM(matrices[3].shape, bf16),
            pltpu.VMEM((ne, nd, rows, width), bf16),
            pltpu.VMEM((units, width), bf16),
            pltpu.VMEM((units, width), bf16),
            pltpu.VMEM((units, width), bf16),
            pltpu.VMEM((nd, units, width // nd), bf16),
            pltpu.VMEM((nd, 4, 2 * nd * rows, units), bf16),
            pltpu.VMEM((ne, nd, rows, units), bf16),
            pltpu.VMEM((ne - 1, nd, rows, units), bf16),
            pltpu.VMEM((nd, rows, units), bf16),
            pltpu.VMEM((3, rows, width), bf16),
            pltpu.VMEM((ne - 1, small[0].shape[0], 128), bf16),
            pltpu.VMEM((up.shape[0], ne * part), bf16),
            pltpu.VMEM((nd, up.shape[0], part), bf16),
            pltpu.VMEM((ne, rows, part), bf16),
            pltpu.VMEM((rows, ne * part), bf16),
            dma((ne - 1,)),
            dma((ne - 1,)),
            dma((3,)),
            dma((3,)),
            dma((4,)),
            dma((4,)),
            dma((ne - 1,)),
            dma((ne - 1,)),
            dma((nd - 1,)),
            dma((nd,)),
            dma((nd - 1,)),
            dma((nd,)),
            dma((3, nd)),
            dma((3, nd)),
            dma,
            dma,
            dma((3,)),
            dma((3,)),
            dma((4,)),
            dma((nd - 1, 4)),
            dma((nd, 4)),
            dma((2, 4)),
            dma((ne - 1,)),
            dma((ne - 1,)),
            dma((nd - 1,)),
            dma((nd,)),
            dma((nd - 1,)),
            dma((nd,)),
            dma((nd - 1,)),
            dma((nd,)),
            dma((len(held),)),
            dma((2,)),
        ],
        compiler_params=pltpu.CompilerParams(
            collective_id=2, has_side_effects=True, vmem_limit_bytes=60 * 2**20
        ),
    )(*args)


def on_device(
    residual,
    queries,
    fresh_key_value,
    prompt_page_cache,
    group_page_table,
    prompt_length,
    suffix_length,
    request_group,
    request_adapter_index,
    adapter_slot_index,
    adapter_down_maps,
    adapter_up_maps,
    sinks,
    output_weight,
    output_bias,
    norm_weight,
    token_experts,
    expert_gate_weight,
    expert_slot_index,
    gate_weight,
    up_weight,
    down_weight,
    gate_bias,
    up_bias,
    down_bias,
):
    heads_per_device = sinks.shape[0]
    tok_row = queries.shape[0]
    head_width = queries.shape[1] // heads_per_device
    kv_count = fresh_key_value.shape[2] // head_width
    ep_count = lax.axis_size("ep")
    data_parallel_count = lax.axis_size("dp")
    group_size = heads_per_device * ep_count // kv_count
    kv_head = lax.axis_index("ep") * heads_per_device // group_size
    tokens_per_device = tok_row // ep_count
    hidden_width = residual.shape[1]
    adapter_weights = adapter_down_maps.shape[0]
    adapter_rank_size = adapter_down_maps.shape[2]
    score_scale = 1.0 / math.sqrt(head_width)
    own_kv = lax.dynamic_slice_in_dim(fresh_key_value, kv_head * head_width, head_width, 2)
    experts = expert_slot_index.shape[0]
    top_count = token_experts.shape[1]
    capacity = max(2, 8 * tokens_per_device // experts)
    direct = experts == ep_count and ep_count == 8 and capacity >= tokens_per_device
    if direct:
        return layer(
            data_parallel_count,
            ep_count,
            adapter_rank_size,
            head_width,
            (prompt_page_cache, fresh_key_value),
            (
                suffix_length,
                request_group,
                request_adapter_index,
                adapter_slot_index,
                group_page_table.T,
                prompt_length,
                expert_slot_index,
                sinks,
            ),
            (
                queries,
                token_experts.T,
                expert_gate_weight.T,
                adapter_down_maps.transpose(0, 2, 1).reshape(-1, heads_per_device * head_width),
                residual,
                adapter_up_maps.reshape(-1, hidden_width),
                gate_bias,
                up_bias,
                down_bias,
                output_bias,
                norm_weight,
            ),
            (gate_weight, up_weight, down_weight, output_weight.T),
        )
    expert_hit = token_experts[:, :, None] == jnp.arange(experts, dtype=jnp.int32)[None, None, :]
    route_col = jnp.sum(jnp.where(expert_hit, expert_slot_index[None, None, :], 0), axis=2)
    request_local, token_group, positions, token_slot = token_layout(
        suffix_length[0],
        request_group,
        request_adapter_index,
        adapter_slot_index,
        prompt_length,
        tok_row,
    )
    queries_rot = rotate(
        queries.reshape(tok_row, heads_per_device, head_width).astype(jnp.float32), positions
    ).astype(jnp.bfloat16)
    keys_new = rotate(own_kv[:, 0:1, :].astype(jnp.float32), positions)[:, 0, :].astype(
        jnp.bfloat16
    )
    values_new = own_kv[:, 1, :]
    token_index = jnp.arange(tok_row, dtype=jnp.int32)
    allowed = (request_local[:, None] == request_local[None, :]) & (
        token_index[None, :] <= token_index[:, None]
    )
    local_scores = (
        jnp.einsum("thd,sd->hts", queries_rot, keys_new, preferred_element_type=jnp.float32)
        * score_scale
    )
    local_masked = jnp.where(allowed[None], local_scores, NEG)
    sink_col = sinks[:, None]
    run_max = jnp.maximum(sink_col, jnp.max(local_masked, axis=-1))
    local_exp = jnp.exp(local_masked - run_max[..., None])
    run_total = jnp.exp(sink_col - run_max) + jnp.sum(local_exp, axis=-1)
    run_acc = jnp.einsum(
        "hts,sd->htd",
        local_exp.astype(jnp.bfloat16),
        values_new,
        preferred_element_type=jnp.float32,
    )
    page_len = prompt_page_cache.shape[1]
    pool_total = prompt_page_cache.shape[0] * data_parallel_count
    page_group, page_slot, page_used = page_layout(group_page_table, pool_total)
    group_hit = page_group[:, None] == jnp.arange(prompt_length.shape[0], dtype=jnp.int32)[None, :]
    page_limit = jnp.sum(jnp.where(group_hit, prompt_length[None, :], 0), axis=1)
    own_pages = lax.dynamic_slice_in_dim(prompt_page_cache, kv_head * head_width, head_width, 3)
    shard_rows = lax.all_gather(own_pages, "dp", axis=0, tiled=True)
    piece_pages = shard_rows.shape[0]
    keys_piece = shard_rows[:, :, 0, :].reshape(piece_pages * page_len, head_width)
    values_piece = shard_rows[:, :, 1, :].reshape(piece_pages * page_len, head_width)
    key_pos = page_slot[:, None] * page_len + jnp.arange(page_len, dtype=jnp.int32)[None, :]
    key_valid = (page_used[:, None] & (key_pos < page_limit[:, None])).reshape(-1)
    key_group = jnp.broadcast_to(page_group[:, None], (piece_pages, page_len)).reshape(-1)
    visible = (token_group[:, None] == key_group[None, :]) & key_valid[None, :]
    scores = (
        jnp.einsum("thd,sd->hts", queries_rot, keys_piece, preferred_element_type=jnp.float32)
        * score_scale
    )
    masked = jnp.where(visible[None], scores, NEG)
    new_max = jnp.maximum(run_max, jnp.max(masked, axis=-1))
    factor = jnp.exp(run_max - new_max)
    weights = jnp.exp(masked - new_max[..., None])
    new_total = run_total * factor + jnp.sum(weights, axis=-1)
    new_acc = run_acc * factor[..., None] + jnp.einsum(
        "hts,sd->htd",
        weights.astype(jnp.bfloat16),
        values_piece,
        preferred_element_type=jnp.float32,
    )
    attention_output = (
        (new_acc / new_total[..., None])
        .transpose(1, 0, 2)
        .reshape(tok_row, heads_per_device * head_width)
        .astype(jnp.bfloat16)
    )
    adapter_onehot = token_slot[:, None] == jnp.arange(adapter_weights, dtype=jnp.int32)[None, :]
    adapter_pick_all = adapter_onehot.astype(jnp.float32)
    adapter_columns = adapter_down_maps.transpose(1, 0, 2).reshape(
        heads_per_device * head_width, adapter_weights * adapter_rank_size
    )
    projected_rows = jnp.dot(attention_output, output_weight, preferred_element_type=jnp.float32)
    reduced_rank = jnp.dot(
        attention_output, adapter_columns, preferred_element_type=jnp.float32
    ).reshape(tokens_per_device * lax.axis_size("ep"), adapter_weights, adapter_rank_size)
    reduced_rank = jnp.sum(reduced_rank * adapter_pick_all[:, :, None], axis=1)
    summed_rows = lax.psum_scatter(
        jnp.concatenate([projected_rows, reduced_rank], axis=1).astype(jnp.bfloat16),
        "ep",
        scatter_dimension=0,
        tiled=True,
    ).astype(jnp.float32)
    projection_sum = summed_rows[:, :hidden_width]
    adapter_middle = summed_rows[:, hidden_width:].astype(jnp.bfloat16)
    owner_onehot = lax.dynamic_slice_in_dim(
        adapter_onehot, lax.axis_index("ep") * tokens_per_device, tokens_per_device, 0
    )
    spread_rows = owner_onehot.astype(jnp.bfloat16)[:, :, None] * adapter_middle[:, None, :]
    holder_count = adapter_up_maps.shape[0]
    outgoing = spread_rows.reshape(
        tokens_per_device, data_parallel_count, holder_count * adapter_rank_size
    )
    incoming = lax.all_to_all(outgoing, "dp", split_axis=1, concat_axis=0, tiled=True)
    adapter_updates = jnp.dot(
        incoming.reshape(data_parallel_count * tokens_per_device, holder_count * adapter_rank_size),
        adapter_up_maps.reshape(holder_count * adapter_rank_size, hidden_width),
        preferred_element_type=jnp.float32,
    )
    adapter_updates = (
        (ADAPTER_SCALE * adapter_updates)
        .astype(jnp.bfloat16)
        .reshape(data_parallel_count, tokens_per_device, hidden_width)
    )
    returned_rows = lax.all_to_all(adapter_updates, "dp", split_axis=0, concat_axis=0, tiled=True)
    adapter_update = jnp.sum(returned_rows.astype(jnp.float32), axis=0)
    stream = settle(
        residual.astype(jnp.float32)
        + projection_sum
        + output_bias.astype(jnp.float32)
        + adapter_update
    )
    mean_square = jnp.mean(stream * stream, axis=-1, keepdims=True)
    normed = (stream * lax.rsqrt(mean_square + EPSILON) * norm_weight.astype(jnp.float32)).astype(
        jnp.bfloat16
    )
    slots_all = ep_count * capacity
    route_col = route_col.reshape(-1)
    col_hot = (route_col[:, None] == jnp.arange(ep_count, dtype=jnp.int32)[None, :]).astype(
        jnp.int32
    )
    route_order = jnp.arange(route_col.shape[0], dtype=jnp.int32)
    earlier = (route_order[None, :] < route_order[:, None]).astype(jnp.int32)
    route_rank = jnp.sum(earlier * (route_col[None, :] == route_col[:, None]), axis=1)
    target_slot = route_col * capacity + route_rank
    target_hot = (target_slot[:, None] == jnp.arange(slots_all, dtype=jnp.int32)[None, :]).reshape(
        tokens_per_device, top_count, slots_all
    )
    scatter_rows = jnp.sum(target_hot.astype(jnp.float32), axis=1)
    combine = jnp.sum(jnp.where(target_hot, expert_gate_weight[:, :, None], 0.0), axis=1)
    outbound = (
        jnp.dot(scatter_rows.T.astype(jnp.bfloat16), normed, preferred_element_type=jnp.float32)
        .astype(jnp.bfloat16)
        .reshape(ep_count, capacity, hidden_width)
    )
    received = lax.all_to_all(outbound, "ep", split_axis=0, concat_axis=0, tiled=True)
    rows_flat = lax.all_gather(received[None], "dp", axis=0, tiled=True).reshape(-1, hidden_width)
    hidden = expert_hidden(rows_flat, gate_weight[0], up_weight[0], gate_bias[0], up_bias[0])
    unit_weights = down_weight[0]
    unit_sum = lax.dot_general(
        lax.all_gather(hidden, "dp", axis=1, tiled=True),
        unit_weights,
        LAST_DIMS,
        preferred_element_type=jnp.float32,
    )
    expert_out = (
        (unit_sum + down_bias[0].astype(jnp.float32))
        .astype(jnp.bfloat16)
        .reshape(data_parallel_count, slots_all, -1)
    )
    home_rows = lax.all_to_all(expert_out, "dp", split_axis=0, concat_axis=2, tiled=True)
    back_rows = lax.all_to_all(
        home_rows.reshape(ep_count, capacity, hidden_width),
        "ep",
        split_axis=0,
        concat_axis=0,
        tiled=True,
    )
    merged = jnp.dot(
        combine,
        back_rows.reshape(slots_all, hidden_width).astype(jnp.float32),
        precision=lax.Precision.HIGHEST,
        preferred_element_type=jnp.float32,
    )
    return (stream + merged).astype(jnp.bfloat16)


def solution(mesh):
    placed = (
        P(("dp", "ep"), None),
        P("dp", "ep"),
        P("dp", None, None),
        P("dp", None, None, None),
        P(),
        P(),
        P("dp", None),
        P("dp"),
        P("dp"),
        P(),
        P(None, "ep", None),
        P("dp", None, None),
        P("ep"),
        P("ep", None),
        P(),
        P(),
        P(("dp", "ep"), None),
        P(("dp", "ep"), None),
        P(),
        P("ep", "dp", None),
        P("ep", "dp", None),
        P("ep", "dp", None),
        P("ep", "dp"),
        P("ep", "dp"),
        P("ep", "dp"),
    )
    return jax.shard_map(
        on_device, mesh=mesh, in_specs=placed, out_specs=P(("dp", "ep"), None), check_vma=False
    )
```

```python
import functools
import math

import jax
import jax.numpy as jnp
from jax import lax
from jax.experimental import pallas as pl
from jax.experimental.pallas import tpu as pltpu
from jax.sharding import PartitionSpec as P

THETA = 150000.0
NEG = -1e30
LIMIT = 7.0
ALPHA = 1.702
EPSILON = 1e-05
ADAPTER_SCALE = 2.0
LAST_DIMS = (((1,), (1,)), ((), ()))


def settle(values):
    return lax.optimization_barrier(values.astype(jnp.bfloat16)).astype(jnp.float32)


def rotate(values, positions):
    head_width = values.shape[-1]
    half_size = head_width // 2
    frequency = THETA ** (-2.0 * jnp.arange(half_size, dtype=jnp.float32) / head_width)
    angles = positions.astype(jnp.float32)[:, None] * frequency[None, :]
    cosine = jnp.cos(angles)[:, None, :]
    sine_part = jnp.sin(angles)[:, None, :]
    front_part = values[..., :half_size]
    back_part = values[..., half_size:]
    return jnp.concatenate(
        [front_part * cosine - back_part * sine_part, back_part * cosine + front_part * sine_part],
        axis=-1,
    )


def token_layout(lengths, groups, request_adapter, adapter_slot_index, prompt_length, tok_count):
    order = jnp.arange(lengths.shape[0], dtype=jnp.int32)
    finish = jnp.sum(jnp.where(order[None, :] <= order[:, None], lengths[None, :], 0), axis=1)
    starts = finish - lengths
    token_index = jnp.arange(tok_count, dtype=jnp.int32)
    member = (token_index[:, None] >= starts[None, :]) & (token_index[:, None] < finish[None, :])
    member_int = member.astype(jnp.int32)
    request_local = jnp.sum(
        member_int * jnp.arange(lengths.shape[0], dtype=jnp.int32)[None, :], axis=1
    )
    token_group = jnp.sum(member_int * groups[None, :], axis=1)
    offset = token_index - jnp.sum(member_int * starts[None, :], axis=1)
    group_hit = token_group[:, None] == jnp.arange(prompt_length.shape[0], dtype=jnp.int32)[None, :]
    prompt_base = jnp.sum(jnp.where(group_hit, prompt_length[None, :], 0), axis=1)
    token_adapter = jnp.sum(member_int * request_adapter[None, :], axis=1)
    id_hit = (
        token_adapter[:, None] == jnp.arange(adapter_slot_index.shape[0], dtype=jnp.int32)[None, :]
    )
    token_slot = jnp.sum(jnp.where(id_hit, adapter_slot_index[None, :], 0), axis=1)
    return (request_local, token_group, prompt_base + offset, token_slot)


def page_layout(group_page_table, pool_total):
    page_ids = jnp.arange(pool_total, dtype=jnp.int32)
    matches = group_page_table[:, :, None] == page_ids[None, None, :]
    match_int = matches.astype(jnp.int32)
    group_ids = jnp.arange(group_page_table.shape[0], dtype=jnp.int32)
    slot_ids = jnp.arange(group_page_table.shape[1], dtype=jnp.int32)
    page_group = jnp.sum(match_int * group_ids[:, None, None], axis=(0, 1))
    page_slot = jnp.sum(match_int * slot_ids[None, :, None], axis=(0, 1))
    page_used = jnp.sum(match_int, axis=(0, 1)) > 0
    return (page_group, page_slot, page_used)


def expert_hidden(rows, gate_matrix, up_matrix, gate_offset, up_offset):
    gate_pre = lax.dot_general(
        rows, gate_matrix, LAST_DIMS, preferred_element_type=jnp.float32
    ) + gate_offset.astype(jnp.float32)
    up_pre = lax.dot_general(
        rows, up_matrix, LAST_DIMS, preferred_element_type=jnp.float32
    ) + up_offset.astype(jnp.float32)
    gate_pre = jnp.minimum(gate_pre, LIMIT)
    up_pre = jnp.clip(up_pre, -LIMIT, LIMIT)
    return ((up_pre + 1.0) * gate_pre * jax.nn.sigmoid(ALPHA * gate_pre)).astype(jnp.bfloat16)


def device(dp, ep):
    return {"dp": dp, "ep": ep}


def send(src, dst, send_sem, recv_sem, dp, ep):
    copy = pltpu.make_async_remote_copy(
        src_ref=src,
        dst_ref=dst,
        send_sem=send_sem,
        recv_sem=recv_sem,
        device_id=device(dp, ep),
        device_id_type=pl.DeviceIdType.MESH,
    )
    copy.start()
    return copy


def greet(peers):
    barrier = pltpu.get_barrier_semaphore()
    for dp, ep in peers:
        pl.semaphore_signal(
            barrier, inc=1, device_id=device(dp, ep), device_id_type=pl.DeviceIdType.MESH
        )
    return lambda: pl.semaphore_wait(barrier, len(peers))


def flip(index, bits):
    out = index
    for bit in (1, 2, 4):
        if bits & bit:
            out = out + bit * (1 - 2 * ((index // bit) % 2))
    return out


def token_fields(tokens, axis, lengths, groups, adapters, slots, prompt):
    shape = (tokens, 1) if axis == 0 else (1, tokens)
    token = lax.broadcasted_iota(jnp.int32, shape, axis)
    zero = jnp.zeros(shape, jnp.int32)
    request, group, position, slot = zero, zero, zero, zero
    start = lengths[0, 0] * 0
    for m in range(lengths.shape[1]):
        finish = start + lengths[0, m]
        inside = (token >= start) & (token < finish)
        request = jnp.where(inside, m, request)
        if axis == 0:
            group = jnp.where(inside, groups[m], group)
            position = jnp.where(inside, token - start + prompt[groups[m]], position)
        else:
            slot = jnp.where(inside, slots[adapters[m]], slot)
        start = finish
    return request, group, position, slot


def rotation(positions, head_width, lanes):
    half = head_width // 2
    lane = lax.broadcasted_iota(jnp.int32, (positions.shape[0], lanes), 1)
    place = lax.rem(lane, half).astype(jnp.float32)
    frequency = jnp.exp(place * (-2.0 * math.log(THETA) / head_width))
    angles = positions.astype(jnp.float32) * frequency
    cosine, sine = jnp.cos(angles), jnp.sin(angles)
    front = lax.rem(lane, head_width) < half
    signed = jnp.where(front, -sine, sine)

    def turn(values):
        values = values.astype(jnp.float32)
        partner = jnp.where(
            front, pltpu.roll(values, lanes - half, 1), pltpu.roll(values, half, 1)
        )
        return (values * cosine + partner * signed).astype(jnp.bfloat16)

    return turn


def page_groups(page, page_len, table, prompt):
    group, limit = jnp.int32(-1), jnp.int32(0)
    for s in range(table.shape[0]):
        for g in range(table.shape[1]):
            hit = table[s, g] == page
            group = jnp.where(hit, g, group)
            limit = jnp.where(hit, prompt[g] - s * page_len, limit)
    lane = lax.broadcasted_iota(jnp.int32, (1, page_len), 1)
    return jnp.where(lane < limit, group, -1)


def line_peers(i, nd):
    if nd != 4:
        return [lax.rem(i + d, nd) for d in range(1, nd)]
    high = i // 2
    return [3 * (1 - high), 2 - high, (1 - i) * (1 - high) + (5 - i) * high]


def spread(src, dst, send_sem, recv_sem, peers, i, j):
    return [send(src, dst, send_sem.at[n], recv_sem.at[i], t, j) for n, t in enumerate(peers)]


def collect(block, send_sem, recv_sem, peers, j):
    for n, t in enumerate(peers):
        pltpu.make_async_remote_copy(
            src_ref=block(t),
            dst_ref=block(t),
            send_sem=send_sem.at[n],
            recv_sem=recv_sem.at[t],
            device_id=device(t, j),
            device_id_type=pl.DeviceIdType.MESH,
        ).wait_recv()


def own_heads(wide, half, head_width):
    keys, values = wide[:, 0, :].astype(jnp.float32), wide[:, 1, :].astype(jnp.float32)
    lane = lax.broadcasted_iota(jnp.int32, keys.shape, 1)
    keys = jnp.where(half == 0, keys, pltpu.roll(keys, head_width, 1))
    values = jnp.where(half == 0, pltpu.roll(values, head_width, 1), values)
    return jnp.where(lane < head_width, keys, values).astype(jnp.bfloat16)


def layer_body(
    nd,
    ne,
    rank_size,
    head_width,
    small_count,
    pages_hbm,
    fresh_hbm,
    *rest,
):
    small_hbm, rest = rest[:small_count], rest[small_count:]
    (gate_hbm, up_hbm, down_hbm, project_hbm, layer_out), rest = rest[:5], rest[5:]
    small, rest = rest[:small_count], rest[small_count:]
    (
        lengths,
        groups,
        adapters,
        slots,
        table,
        prompt,
        expert_slots,
        sinks,
        queries,
        route_experts,
        route_weights,
        adapter_columns,
        residual,
        up,
        gate_offset,
        up_offset,
        down_offset,
        bias,
        gain,
    ) = small
    (
        pages_wide,
        fresh_wide,
        merged,
        combine,
        proj,
        proj_wide,
        pair_out,
        pair_in,
        rank,
        pages_all,
        weights,
        project_matrix,
        gathered,
        gate_matrix,
        up_matrix,
        down_matrix,
        down_parts,
        hidden,
        outs,
        outs_in,
        sums,
        proj_in,
        rank_in,
        up_wide,
        up_part,
        delta,
        delta_full,
        rank_s,
        rank_r,
        proj_s,
        proj_r,
        pair_s,
        pair_r,
        delta_s,
        delta_r,
        wide_s,
        wide_r,
        plane_s,
        plane_r,
        chip_s,
        chip_r,
        hop_s,
        hop_r,
        pass_s,
        pass_r,
        load_sem,
        unit_s,
        unit_r,
        relay_s,
        out_s,
        out_r,
        sum_s,
        sum_r,
        page_s,
        page_r,
        combine_s,
        combine_r,
        small_sem,
        wide_sem,
        plane_hop_s,
    ) = rest
    i, j = lax.axis_index("dp"), lax.axis_index("ep")
    heads = sinks.shape[0]
    lanes = 2 * head_width
    page_count, page_len = pages_hbm.shape[:2]
    kv_head = j * (fresh_hbm.shape[2] // head_width) // ne
    block = pl.ds(pl.multiple_of(kv_head // 2 * lanes, lanes), lanes)
    head_loads = [
        pltpu.make_async_copy(pages_hbm.at[:, :, :, block], pages_wide, wide_sem.at[0]),
        pltpu.make_async_copy(fresh_hbm.at[:, :, block], fresh_wide, wide_sem.at[1]),
    ]
    for copy in head_loads:
        copy.start()
    peers = line_peers(i, nd)
    near_first = peers[::-1]
    relays = nd == 4
    inner = (i == 1) | (i == nd - 2)
    far_item = lax.rem(6 - 3 * i + 6, 6)
    end = 3 - far_item

    def carry(block, send_sem, recv_sem, target):
        return pltpu.make_async_remote_copy(
            src_ref=block,
            dst_ref=block,
            send_sem=send_sem,
            recv_sem=recv_sem,
            device_id=device(target, j),
            device_id_type=pl.DeviceIdType.MESH,
        )

    def skips(target):
        apart = (i - target) * (i - target)
        return (apart == 9) | (inner & (apart == 4))

    def unless(skip, action):
        if skip is None:
            action()
        else:
            pl.when(jnp.logical_not(skip))(action)

    loads = [
        pltpu.make_async_copy(source, target, load_sem.at[n])
        for n, (source, target) in enumerate(
            (
                (gate_hbm.at[0], gate_matrix),
                (up_hbm.at[0], up_matrix),
                (down_hbm.at[0], down_matrix),
                (project_hbm, project_matrix),
            )
        )
    ]
    small_loads = [
        pltpu.make_async_copy(source, target, small_sem.at[n])
        for n, (source, target) in enumerate(zip(small_hbm, small))
    ]
    for copy in small_loads:
        copy.start()
    everyone = [(d, e) for d in range(nd) for e in range(ne) if d or e]
    met = greet([(lax.rem(i + d, nd), lax.rem(j + e, ne)) for d, e in everyone])
    half = lax.rem(kv_head, 2)
    head_loads[0].wait()
    pages_all[i] = own_heads(
        pages_wide[...].reshape(page_count * page_len, 2, lanes), half, head_width
    )
    met()
    page_copies = spread(pages_all.at[i], pages_all.at[i], page_s, page_r, peers, i, j)
    head_loads[1].wait()
    for copy in small_loads:
        copy.wait()
    for n in (3, 0, 1, 2):
        loads[n].start()
    rows = residual.shape[0]
    experts_of = route_experts[...]
    holders = jnp.zeros_like(experts_of)
    for e in range(expert_slots.shape[0]):
        holders = jnp.where(experts_of == e, expert_slots[e], holders)
    combine[...] = jnp.zeros_like(combine)
    for e in range(ne):
        combine[e : e + 1, :rows] = jnp.sum(
            jnp.where(holders == e, route_weights[...], 0.0), axis=0, keepdims=True
        )
    combine_copies = spread(combine, weights.at[i], combine_s, combine_r, peers, i, j)
    weights[i] = combine[...]
    tokens_row = queries.shape[0]
    fresh = own_heads(fresh_wide[...], half, head_width)
    scale = 1.0 / math.sqrt(head_width)
    request, group, position, _ = token_fields(
        tokens_row, 0, lengths, groups, adapters, slots, prompt
    )
    request_row, _, _, slot = token_fields(
        tokens_row, 1, lengths, groups, adapters, slots, prompt
    )
    turn = rotation(position, head_width, lanes)
    turned = [turn(queries[:, n * lanes : (n + 1) * lanes]) for n in range(heads // 2)]
    query_rows = jnp.concatenate(
        [pair[:, n * head_width : (n + 1) * head_width] for pair in turned for n in (0, 1)], axis=0
    )
    row_index = lax.broadcasted_iota(jnp.int32, (tokens_row, tokens_row), 0)
    column_index = lax.broadcasted_iota(jnp.int32, (tokens_row, tokens_row), 1)

    def masked_scores(keys, mask):
        width = keys.shape[0]
        scores = scale * lax.dot_general(
            query_rows, keys, LAST_DIMS, preferred_element_type=jnp.float32
        )
        return jnp.where(mask[None], scores.reshape(heads, tokens_row, width), NEG)

    score_list = [
        masked_scores(
            turn(fresh)[:, :head_width],
            (request == request_row) & (column_index <= row_index),
        )
    ]
    value_list = [fresh[:, head_width:]]
    key_groups = [page_groups(p, page_len, table, prompt) for p in range(nd * page_count)]
    collect(lambda t: pages_all.at[t], page_s, page_r, peers, j)
    width, part = residual.shape[1], delta.shape[2]
    own_part = pl.ds(pl.multiple_of(j * part, part), part)
    up_wide[:, :width] = up[...]
    up_wide[:, width:] = jnp.zeros((up.shape[0], ne * part - width), jnp.bfloat16)
    up_part[i] = up_wide[:, own_part]
    wide_copies = spread(up_wide.at[:, own_part], up_part.at[i], wide_s, wide_r, peers, i, j)
    for d in range(nd):
        shard = pages_all[d]
        mask = group == jnp.concatenate(
            key_groups[d * page_count : (d + 1) * page_count], axis=1
        )
        score_list.append(masked_scores(shard[:, :head_width], mask))
        value_list.append(shard[:, head_width:])
    sink = jnp.concatenate(
        [jnp.full((1, tokens_row, 1), sinks[h], jnp.float32) for h in range(heads)], axis=0
    )
    peak = sink
    for scores in score_list:
        peak = jnp.maximum(peak, jnp.max(scores, axis=-1, keepdims=True))
    denominator = jnp.exp(sink - peak)
    weighted = jnp.zeros((heads * tokens_row, head_width), jnp.float32)
    for scores, values in zip(score_list, value_list):
        probs = jnp.exp(scores - peak)
        denominator = denominator + jnp.sum(probs, axis=-1, keepdims=True)
        weighted = weighted + jnp.dot(
            probs.reshape(heads * tokens_row, -1).astype(jnp.bfloat16),
            values,
            preferred_element_type=jnp.float32,
        )
    attended = weighted.reshape(heads, tokens_row, head_width) / denominator
    attended = jnp.concatenate([attended[h] for h in range(heads)], axis=1).astype(jnp.bfloat16)
    rank_width = nd * up.shape[0]
    slot_rows = (
        lax.broadcasted_iota(jnp.int32, (rank_width, tokens_row), 0) // rank_size == slot
    )
    rank_all = lax.dot_general(
        adapter_columns[...], attended, LAST_DIMS, preferred_element_type=jnp.float32
    )
    rank_all = jnp.where(slot_rows, rank_all, 0.0)
    rank[...] = jnp.sum(
        rank_all.reshape(rank_width // rank_size, rank_size, tokens_row), axis=0
    ).astype(jnp.bfloat16)
    rank_copies, proj_copies = [], []
    for e in range(1, ne):
        rank_copies.append(
            send(
                rank, rank_in.at[e - 1], rank_s.at[e - 1], rank_r.at[e - 1], i, lax.rem(j + e, ne)
            )
        )
    loads[3].wait()
    projected = lax.dot_general(
        attended, project_matrix[...], LAST_DIMS, preferred_element_type=jnp.float32
    )
    for e in range(ne):
        proj_wide[e] = projected[e * rows : (e + 1) * rows]
    turns = (6, 2, 4, 0)
    pair_copies = []
    for n, bits in enumerate(turns):
        pair_out[n] = proj_wide[flip(j, bits + 1)].astype(jnp.bfloat16)
        pair_copies.append(
            send(pair_out.at[n], pair_in.at[n], pair_s.at[n], pair_r.at[n], i, flip(j, 1))
        )
    for n, bits in enumerate(turns):
        pair_copies[n].wait_recv()
        total = proj_wide[flip(j, bits)] + pair_in[n].astype(jnp.float32)
        if bits:
            proj[n] = total.astype(jnp.bfloat16)
            proj_copies.append(
                send(proj.at[n], proj_in.at[n], proj_s.at[n], proj_r.at[n], i, flip(j, bits))
            )
    for copy in rank_copies:
        copy.wait()
    collect(lambda t: up_part.at[t], wide_s, wide_r, peers, j)
    middle = rank[...].astype(jnp.float32)
    for e in range(1, ne):
        middle = middle + rank_in[e - 1].astype(jnp.float32)
    middles = jnp.concatenate([middle] * (rank_width // rank_size), axis=0)
    middles = jnp.where(slot_rows, middles, 0.0).astype(jnp.bfloat16)
    updates = lax.dot_general(
        middles,
        up_part[...].reshape(rank_width, part),
        (((0,), (0,)), ((), ())),
        preferred_element_type=jnp.float32,
    )
    updates = ADAPTER_SCALE * updates
    for e in range(ne):
        delta[e] = updates[e * rows : (e + 1) * rows].astype(jnp.bfloat16)
    delta_full[:, own_part] = delta[j]
    delta_copies = []
    for e in range(1, ne):
        tj = lax.rem(j + e, ne)
        delta_copies.append(
            send(
                delta.at[tj],
                delta_full.at[:, own_part],
                delta_s.at[e - 1],
                delta_r.at[e - 1],
                i,
                tj,
            )
        )
    for copy in proj_copies:
        copy.wait()
    for n in range(3):
        total = total + proj_in[n].astype(jnp.float32)
    total = total + residual[...].astype(jnp.float32) + bias[...].astype(jnp.float32).reshape(1, -1)
    for copy in delta_copies:
        copy.wait()
    total = total + delta_full[:, :width].astype(jnp.float32)
    rounded = total.astype(jnp.bfloat16)
    stream = rounded.astype(jnp.float32)
    mean_square = jnp.mean(stream * stream, axis=-1, keepdims=True)
    normed = stream * lax.rsqrt(mean_square + EPSILON) * gain[...].astype(jnp.float32).reshape(1, -1)
    gathered[j, i] = normed.astype(jnp.bfloat16)
    plane_copies = []
    for n, t in enumerate(peers):
        copy = carry(gathered.at[j, i], plane_s.at[n], plane_r.at[i], t)
        skip = skips(t) if relays else None
        plane_copies.append((copy, skip))
        unless(skip, copy.start)
    sibling, across, along = flip(j, 1), flip(j, 2), flip(j, 4)
    chip_copies = []

    def to_chips(d):
        for n, target in enumerate((across, along, sibling)):
            piece = gathered.at[j, d]
            chip_copies.append(send(piece, piece, chip_s.at[n, d], chip_r.at[n, d], i, target))

    to_chips(i)
    loads[2].wait()
    units_own = down_parts.shape[2]
    for d in range(nd):
        down_parts[d] = down_matrix[:, d * units_own : (d + 1) * units_own]
    def landed(t):
        return carry(gathered.at[j, t], plane_s.at[0], plane_r.at[t], t)

    def plane_hop(n, t):
        return carry(gathered.at[j, t], plane_hop_s.at[n], plane_r.at[t], end)

    if relays:

        @pl.when(inner)
        def _():
            for n, t in enumerate((3 - i, far_item)):
                landed(t).wait_recv()
                plane_hop(n, t).start()

    for t in near_first:
        unless(inner & (t != end) if relays else None, landed(t).wait_recv)
        to_chips(t)

    def from_chip(n, source):
        for d in range(nd):
            piece = gathered.at[source, d]
            pltpu.make_async_remote_copy(
                src_ref=piece,
                dst_ref=piece,
                send_sem=chip_s.at[n, d],
                recv_sem=chip_r.at[n, d],
                device_id=device(i, source),
                device_id_type=pl.DeviceIdType.MESH,
            ).wait_recv()

    core = lax.rem(j, 2)
    hop_from = along + core * (across - along)
    hop_to = across + core * (along - across)
    passed = []
    chunks = (0, 2, 4, 6)
    unit_copies = []

    def units(c):
        bits = chunks[c]
        blocks = [
            gathered[flip(j, bits + n)].astype(jnp.float32).reshape(nd * rows, -1) for n in (0, 1)
        ]
        tokens = jnp.concatenate(blocks, axis=0).astype(jnp.bfloat16)
        hidden[i, c] = expert_hidden(
            tokens, gate_matrix[...], up_matrix[...], gate_offset[...], up_offset[...]
        )
        for d, ti in enumerate(peers, 1):
            copy = carry(hidden.at[i, c], unit_s.at[d - 1, c], unit_r.at[i, c], ti)
            skip = skips(ti) if relays else None
            unit_copies.append((copy, skip))
            unless(skip, copy.start)

    def passage(item, c, n):
        return carry(hidden.at[item, c], relay_s.at[n, c], unit_r.at[item, c], end)

    def arrival(item, c):
        return carry(hidden.at[item, c], unit_s.at[0, c], unit_r.at[item, c], item)

    def relay(n, c, before):
        if not relays:
            return

        @pl.when(inner)
        def _():
            item = (3 - i, far_item)[n]
            arrival(item, c).wait_recv()
            if before is not None:
                passage(item, before, n).wait_send()
            passage(item, c, n).start()

    def pass_on(other):
        n = len(passed)
        passed.append(
            send(gathered.at[other], gathered.at[other], pass_s.at[n], pass_r.at[n], i, sibling)
        )

    out_copies = []

    def shard_down(c, item):
        return lax.dot_general(
            hidden[item, c], down_parts[item], LAST_DIMS, preferred_element_type=jnp.float32
        )

    def add_arrivals(c, items, result):
        for item in items:
            unless(inner & (item != end) if relays else None, arrival(item, c).wait_recv)
            result = result + shard_down(c, item)
        return result

    def begin(c):
        result = down_offset[...].astype(jnp.float32) + shard_down(c, i)
        return add_arrivals(c, near_first[:-1], result)

    def finish(c, result):
        result = add_arrivals(c, near_first[-1:], result)
        for n in (0, 1):
            other = flip(j, chunks[c] + n)
            for d in range(nd):
                start = (n * nd + d) * rows
                outs[other, d] = result[start : start + rows].astype(jnp.bfloat16)
            if chunks[c] + n:
                place = chunks[c] + n - 1
                out_copies.append(
                    send(
                        outs.at[other], outs_in.at[place], out_s.at[place], out_r.at[place], i, other
                    )
                )

    loads[0].wait()
    loads[1].wait()
    from_chip(2, sibling)
    units(0)
    from_chip(0, across)
    pass_on(across)
    from_chip(1, along)
    pass_on(along)
    hop = send(gathered.at[hop_from], gathered.at[hop_from], hop_s, hop_r, i, hop_to)
    passed[0].wait_recv()
    units(1)
    hop.wait_recv()
    pass_on(flip(j, 6))
    passed[1].wait_recv()
    units(2)
    relay(0, 0, None)
    passed[2].wait_recv()
    units(3)
    relay(0, 1, None)
    relay(1, 1, None)
    own_chip = begin(0)
    finish(1, begin(1))
    for c, near, far in ((2, 0, None), (3, 1, 1)):
        relay(0, c, near)
        relay(1, c, far)
        finish(c, begin(c))
    relay(1, 0, 2)
    finish(0, own_chip)
    for copy in out_copies:
        copy.wait_recv()
    collect(lambda t: weights.at[t], combine_s, combine_r, peers, j)
    diagonal = lax.broadcasted_iota(jnp.int32, (rows, rows), 0) == lax.broadcasted_iota(
        jnp.int32, (rows, rows), 1
    )
    for d in range(nd):
        total = 0.0
        for bits in range(ne):
            piece = outs[j, d] if bits == 0 else outs_in[bits - 1, d]
            line = weights[d, pl.ds(flip(j, bits), 1), :][:, :rows]
            factor = jnp.sum(jnp.where(diagonal, line, 0.0), axis=1, keepdims=True)
            total = total + piece.astype(jnp.float32) * factor
        sums[d] = total.astype(jnp.bfloat16)
    finals = [
        send(sums.at[t], merged.at[i], sum_s.at[n], sum_r.at[i], t, j)
        for n, t in enumerate(peers)
    ]
    merged[i] = sums[i]
    for copy, skip in unit_copies + plane_copies:
        unless(skip, copy.wait_send)
    if relays:

        @pl.when(inner)
        def _():
            for n, t in enumerate((3 - i, far_item)):
                plane_hop(n, t).wait_send()
            for n, c in ((0, 2), (0, 3), (1, 3), (1, 0)):
                passage(0, c, n).wait_send()

    waiting = chip_copies + passed + [hop] + out_copies + page_copies + combine_copies
    for copy in waiting + wide_copies + pair_copies:
        copy.wait_send()
    for copy in finals:
        copy.wait_send()
    collect(lambda t: merged.at[t], sum_s, sum_r, peers, j)
    update = jnp.concatenate([merged[d].astype(jnp.float32) for d in range(nd)], axis=1)
    layer_out[...] = (stream + update).astype(jnp.bfloat16)


def layer(nd, ne, rank_size, head_width, front, scalars, small, matrices):
    caches, fresh = front
    lanes = 2 * head_width
    page_rows = caches.shape[0] * caches.shape[1]
    residual, up = small[4:6]
    rows, width = residual.shape
    part = -(-width // (128 * ne)) * 128
    units = matrices[0].shape[1]
    dma = pltpu.SemaphoreType.DMA
    held = scalars + small
    args = front + held + matrices
    vmem = pl.BlockSpec(memory_space=pltpu.VMEM)
    bf16 = jnp.bfloat16
    return pl.pallas_call(
        functools.partial(layer_body, nd, ne, rank_size, head_width, len(held)),
        out_shape=jax.ShapeDtypeStruct((rows, width), bf16),
        in_specs=[pl.BlockSpec(memory_space=pltpu.HBM)] * len(args),
        out_specs=vmem,
        scratch_shapes=[pltpu.SMEM(x.shape, x.dtype) for x in scalars]
        + [pltpu.VMEM(x.shape, x.dtype) for x in small]
        + [
            pltpu.VMEM(caches.shape[:3] + (lanes,), bf16),
            pltpu.VMEM(fresh.shape[:2] + (lanes,), bf16),
            pltpu.VMEM((nd, rows, units), bf16),
            pltpu.VMEM((ne, 128), jnp.float32),
            pltpu.VMEM((3, rows, width), bf16),
            pltpu.VMEM((ne, rows, width), jnp.float32),
            pltpu.VMEM((4, rows, width), bf16),
            pltpu.VMEM((4, rows, width), bf16),
            pltpu.VMEM((rank_size, small[0].shape[0]), bf16),
            pltpu.VMEM((nd, page_rows, lanes), bf16),
            pltpu.VMEM((nd, ne, 128), jnp.float32),
            pltpu.VMEM(matrices[3].shape, bf16),
            pltpu.VMEM((ne, nd, rows, width), bf16),
            pltpu.VMEM((units, width), bf16),
            pltpu.VMEM((units, width), bf16),
            pltpu.VMEM((units, width), bf16),
            pltpu.VMEM((nd, units, width // nd), bf16),
            pltpu.VMEM((nd, 4, 2 * nd * rows, units), bf16),
            pltpu.VMEM((ne, nd, rows, units), bf16),
            pltpu.VMEM((ne - 1, nd, rows, units), bf16),
            pltpu.VMEM((nd, rows, units), bf16),
            pltpu.VMEM((3, rows, width), bf16),
            pltpu.VMEM((ne - 1, rank_size, small[0].shape[0]), bf16),
            pltpu.VMEM((up.shape[0], ne * part), bf16),
            pltpu.VMEM((nd, up.shape[0], part), bf16),
            pltpu.VMEM((ne, rows, part), bf16),
            pltpu.VMEM((rows, ne * part), bf16),
            dma((ne - 1,)),
            dma((ne - 1,)),
            dma((3,)),
            dma((3,)),
            dma((4,)),
            dma((4,)),
            dma((ne - 1,)),
            dma((ne - 1,)),
            dma((nd - 1,)),
            dma((nd,)),
            dma((nd - 1,)),
            dma((nd,)),
            dma((3, nd)),
            dma((3, nd)),
            dma,
            dma,
            dma((3,)),
            dma((3,)),
            dma((4,)),
            dma((nd - 1, 4)),
            dma((nd, 4)),
            dma((2, 4)),
            dma((ne - 1,)),
            dma((ne - 1,)),
            dma((nd - 1,)),
            dma((nd,)),
            dma((nd - 1,)),
            dma((nd,)),
            dma((nd - 1,)),
            dma((nd,)),
            dma((len(held),)),
            dma((2,)),
            dma((2,)),
        ],
        compiler_params=pltpu.CompilerParams(
            collective_id=2, has_side_effects=True, vmem_limit_bytes=60 * 2**20
        ),
    )(*args)


def on_device(
    residual,
    queries,
    fresh_key_value,
    prompt_page_cache,
    group_page_table,
    prompt_length,
    suffix_length,
    request_group,
    request_adapter_index,
    adapter_slot_index,
    adapter_down_maps,
    adapter_up_maps,
    sinks,
    output_weight,
    output_bias,
    norm_weight,
    token_experts,
    expert_gate_weight,
    expert_slot_index,
    gate_weight,
    up_weight,
    down_weight,
    gate_bias,
    up_bias,
    down_bias,
):
    heads_per_device = sinks.shape[0]
    tok_row = queries.shape[0]
    head_width = queries.shape[1] // heads_per_device
    kv_count = fresh_key_value.shape[2] // head_width
    ep_count = lax.axis_size("ep")
    data_parallel_count = lax.axis_size("dp")
    group_size = heads_per_device * ep_count // kv_count
    kv_head = lax.axis_index("ep") * heads_per_device // group_size
    tokens_per_device = tok_row // ep_count
    hidden_width = residual.shape[1]
    adapter_weights = adapter_down_maps.shape[0]
    adapter_rank_size = adapter_down_maps.shape[2]
    score_scale = 1.0 / math.sqrt(head_width)
    own_kv = lax.dynamic_slice_in_dim(fresh_key_value, kv_head * head_width, head_width, 2)
    experts = expert_slot_index.shape[0]
    top_count = token_experts.shape[1]
    capacity = max(2, 8 * tokens_per_device // experts)
    direct = experts == ep_count and ep_count == 8 and capacity >= tokens_per_device
    if direct:
        return layer(
            data_parallel_count,
            ep_count,
            adapter_rank_size,
            head_width,
            (prompt_page_cache, fresh_key_value),
            (
                suffix_length,
                request_group,
                request_adapter_index,
                adapter_slot_index,
                group_page_table.T,
                prompt_length,
                expert_slot_index,
                sinks,
            ),
            (
                queries,
                token_experts.T,
                expert_gate_weight.T,
                adapter_down_maps.transpose(0, 2, 1).reshape(-1, heads_per_device * head_width),
                residual,
                adapter_up_maps.reshape(-1, hidden_width),
                gate_bias,
                up_bias,
                down_bias,
                output_bias,
                norm_weight,
            ),
            (gate_weight, up_weight, down_weight, output_weight.T),
        )
    expert_hit = token_experts[:, :, None] == jnp.arange(experts, dtype=jnp.int32)[None, None, :]
    route_col = jnp.sum(jnp.where(expert_hit, expert_slot_index[None, None, :], 0), axis=2)
    request_local, token_group, positions, token_slot = token_layout(
        suffix_length[0],
        request_group,
        request_adapter_index,
        adapter_slot_index,
        prompt_length,
        tok_row,
    )
    queries_rot = rotate(
        queries.reshape(tok_row, heads_per_device, head_width).astype(jnp.float32), positions
    ).astype(jnp.bfloat16)
    keys_new = rotate(own_kv[:, 0:1, :].astype(jnp.float32), positions)[:, 0, :].astype(
        jnp.bfloat16
    )
    values_new = own_kv[:, 1, :]
    token_index = jnp.arange(tok_row, dtype=jnp.int32)
    allowed = (request_local[:, None] == request_local[None, :]) & (
        token_index[None, :] <= token_index[:, None]
    )
    local_scores = (
        jnp.einsum("thd,sd->hts", queries_rot, keys_new, preferred_element_type=jnp.float32)
        * score_scale
    )
    local_masked = jnp.where(allowed[None], local_scores, NEG)
    sink_col = sinks[:, None]
    run_max = jnp.maximum(sink_col, jnp.max(local_masked, axis=-1))
    local_exp = jnp.exp(local_masked - run_max[..., None])
    run_total = jnp.exp(sink_col - run_max) + jnp.sum(local_exp, axis=-1)
    run_acc = jnp.einsum(
        "hts,sd->htd",
        local_exp.astype(jnp.bfloat16),
        values_new,
        preferred_element_type=jnp.float32,
    )
    page_len = prompt_page_cache.shape[1]
    pool_total = prompt_page_cache.shape[0] * data_parallel_count
    page_group, page_slot, page_used = page_layout(group_page_table, pool_total)
    group_hit = page_group[:, None] == jnp.arange(prompt_length.shape[0], dtype=jnp.int32)[None, :]
    page_limit = jnp.sum(jnp.where(group_hit, prompt_length[None, :], 0), axis=1)
    own_pages = lax.dynamic_slice_in_dim(prompt_page_cache, kv_head * head_width, head_width, 3)
    shard_rows = lax.all_gather(own_pages, "dp", axis=0, tiled=True)
    piece_pages = shard_rows.shape[0]
    keys_piece = shard_rows[:, :, 0, :].reshape(piece_pages * page_len, head_width)
    values_piece = shard_rows[:, :, 1, :].reshape(piece_pages * page_len, head_width)
    key_pos = page_slot[:, None] * page_len + jnp.arange(page_len, dtype=jnp.int32)[None, :]
    key_valid = (page_used[:, None] & (key_pos < page_limit[:, None])).reshape(-1)
    key_group = jnp.broadcast_to(page_group[:, None], (piece_pages, page_len)).reshape(-1)
    visible = (token_group[:, None] == key_group[None, :]) & key_valid[None, :]
    scores = (
        jnp.einsum("thd,sd->hts", queries_rot, keys_piece, preferred_element_type=jnp.float32)
        * score_scale
    )
    masked = jnp.where(visible[None], scores, NEG)
    new_max = jnp.maximum(run_max, jnp.max(masked, axis=-1))
    factor = jnp.exp(run_max - new_max)
    weights = jnp.exp(masked - new_max[..., None])
    new_total = run_total * factor + jnp.sum(weights, axis=-1)
    new_acc = run_acc * factor[..., None] + jnp.einsum(
        "hts,sd->htd",
        weights.astype(jnp.bfloat16),
        values_piece,
        preferred_element_type=jnp.float32,
    )
    attention_output = (
        (new_acc / new_total[..., None])
        .transpose(1, 0, 2)
        .reshape(tok_row, heads_per_device * head_width)
        .astype(jnp.bfloat16)
    )
    adapter_onehot = token_slot[:, None] == jnp.arange(adapter_weights, dtype=jnp.int32)[None, :]
    adapter_pick_all = adapter_onehot.astype(jnp.float32)
    adapter_columns = adapter_down_maps.transpose(1, 0, 2).reshape(
        heads_per_device * head_width, adapter_weights * adapter_rank_size
    )
    projected_rows = jnp.dot(attention_output, output_weight, preferred_element_type=jnp.float32)
    reduced_rank = jnp.dot(
        attention_output, adapter_columns, preferred_element_type=jnp.float32
    ).reshape(tokens_per_device * lax.axis_size("ep"), adapter_weights, adapter_rank_size)
    reduced_rank = jnp.sum(reduced_rank * adapter_pick_all[:, :, None], axis=1)
    summed_rows = lax.psum_scatter(
        jnp.concatenate([projected_rows, reduced_rank], axis=1).astype(jnp.bfloat16),
        "ep",
        scatter_dimension=0,
        tiled=True,
    ).astype(jnp.float32)
    projection_sum = summed_rows[:, :hidden_width]
    adapter_middle = summed_rows[:, hidden_width:].astype(jnp.bfloat16)
    owner_onehot = lax.dynamic_slice_in_dim(
        adapter_onehot, lax.axis_index("ep") * tokens_per_device, tokens_per_device, 0
    )
    spread_rows = owner_onehot.astype(jnp.bfloat16)[:, :, None] * adapter_middle[:, None, :]
    holder_count = adapter_up_maps.shape[0]
    outgoing = spread_rows.reshape(
        tokens_per_device, data_parallel_count, holder_count * adapter_rank_size
    )
    incoming = lax.all_to_all(outgoing, "dp", split_axis=1, concat_axis=0, tiled=True)
    adapter_updates = jnp.dot(
        incoming.reshape(data_parallel_count * tokens_per_device, holder_count * adapter_rank_size),
        adapter_up_maps.reshape(holder_count * adapter_rank_size, hidden_width),
        preferred_element_type=jnp.float32,
    )
    adapter_updates = (
        (ADAPTER_SCALE * adapter_updates)
        .astype(jnp.bfloat16)
        .reshape(data_parallel_count, tokens_per_device, hidden_width)
    )
    returned_rows = lax.all_to_all(adapter_updates, "dp", split_axis=0, concat_axis=0, tiled=True)
    adapter_update = jnp.sum(returned_rows.astype(jnp.float32), axis=0)
    stream = settle(
        residual.astype(jnp.float32)
        + projection_sum
        + output_bias.astype(jnp.float32)
        + adapter_update
    )
    mean_square = jnp.mean(stream * stream, axis=-1, keepdims=True)
    normed = (stream * lax.rsqrt(mean_square + EPSILON) * norm_weight.astype(jnp.float32)).astype(
        jnp.bfloat16
    )
    slots_all = ep_count * capacity
    route_col = route_col.reshape(-1)
    col_hot = (route_col[:, None] == jnp.arange(ep_count, dtype=jnp.int32)[None, :]).astype(
        jnp.int32
    )
    route_order = jnp.arange(route_col.shape[0], dtype=jnp.int32)
    earlier = (route_order[None, :] < route_order[:, None]).astype(jnp.int32)
    route_rank = jnp.sum(earlier * (route_col[None, :] == route_col[:, None]), axis=1)
    target_slot = route_col * capacity + route_rank
    target_hot = (target_slot[:, None] == jnp.arange(slots_all, dtype=jnp.int32)[None, :]).reshape(
        tokens_per_device, top_count, slots_all
    )
    scatter_rows = jnp.sum(target_hot.astype(jnp.float32), axis=1)
    combine = jnp.sum(jnp.where(target_hot, expert_gate_weight[:, :, None], 0.0), axis=1)
    outbound = (
        jnp.dot(scatter_rows.T.astype(jnp.bfloat16), normed, preferred_element_type=jnp.float32)
        .astype(jnp.bfloat16)
        .reshape(ep_count, capacity, hidden_width)
    )
    received = lax.all_to_all(outbound, "ep", split_axis=0, concat_axis=0, tiled=True)
    rows_flat = lax.all_gather(received[None], "dp", axis=0, tiled=True).reshape(-1, hidden_width)
    hidden = expert_hidden(rows_flat, gate_weight[0], up_weight[0], gate_bias[0], up_bias[0])
    unit_weights = down_weight[0]
    unit_sum = lax.dot_general(
        lax.all_gather(hidden, "dp", axis=1, tiled=True),
        unit_weights,
        LAST_DIMS,
        preferred_element_type=jnp.float32,
    )
    expert_out = (
        (unit_sum + down_bias[0].astype(jnp.float32))
        .astype(jnp.bfloat16)
        .reshape(data_parallel_count, slots_all, -1)
    )
    home_rows = lax.all_to_all(expert_out, "dp", split_axis=0, concat_axis=2, tiled=True)
    back_rows = lax.all_to_all(
        home_rows.reshape(ep_count, capacity, hidden_width),
        "ep",
        split_axis=0,
        concat_axis=0,
        tiled=True,
    )
    merged = jnp.dot(
        combine,
        back_rows.reshape(slots_all, hidden_width).astype(jnp.float32),
        precision=lax.Precision.HIGHEST,
        preferred_element_type=jnp.float32,
    )
    return (stream + merged).astype(jnp.bfloat16)


def solution(mesh):
    placed = (
        P(("dp", "ep"), None),
        P("dp", "ep"),
        P("dp", None, None),
        P("dp", None, None, None),
        P(),
        P(),
        P("dp", None),
        P("dp"),
        P("dp"),
        P(),
        P(None, "ep", None),
        P("dp", None, None),
        P("ep"),
        P("ep", None),
        P(),
        P(),
        P(("dp", "ep"), None),
        P(("dp", "ep"), None),
        P(),
        P("ep", "dp", None),
        P("ep", "dp", None),
        P("ep", "dp", None),
        P("ep", "dp"),
        P("ep", "dp"),
        P("ep", "dp"),
    )
    return jax.shard_map(
        on_device, mesh=mesh, in_specs=placed, out_specs=P(("dp", "ep"), None), check_vma=False
    )
```

```python
import functools
import math

import jax
import jax.numpy as jnp
from jax import lax
from jax.experimental import pallas as pl
from jax.experimental.pallas import tpu as pltpu
from jax.sharding import PartitionSpec as P

THETA = 150000.0
NEG = -1e30
LIMIT = 7.0
ALPHA = 1.702
EPSILON = 1e-05
ADAPTER_SCALE = 2.0
LAST_DIMS = (((1,), (1,)), ((), ()))


def settle(values):
    return lax.optimization_barrier(values.astype(jnp.bfloat16)).astype(jnp.float32)


def rotate(values, positions):
    head_width = values.shape[-1]
    half_size = head_width // 2
    frequency = THETA ** (-2.0 * jnp.arange(half_size, dtype=jnp.float32) / head_width)
    angles = positions.astype(jnp.float32)[:, None] * frequency[None, :]
    cosine = jnp.cos(angles)[:, None, :]
    sine_part = jnp.sin(angles)[:, None, :]
    front_part = values[..., :half_size]
    back_part = values[..., half_size:]
    return jnp.concatenate(
        [front_part * cosine - back_part * sine_part, back_part * cosine + front_part * sine_part],
        axis=-1,
    )


def token_layout(lengths, groups, request_adapter, adapter_slot_index, prompt_length, tok_count):
    order = jnp.arange(lengths.shape[0], dtype=jnp.int32)
    finish = jnp.sum(jnp.where(order[None, :] <= order[:, None], lengths[None, :], 0), axis=1)
    starts = finish - lengths
    token_index = jnp.arange(tok_count, dtype=jnp.int32)
    member = (token_index[:, None] >= starts[None, :]) & (token_index[:, None] < finish[None, :])
    member_int = member.astype(jnp.int32)
    request_local = jnp.sum(
        member_int * jnp.arange(lengths.shape[0], dtype=jnp.int32)[None, :], axis=1
    )
    token_group = jnp.sum(member_int * groups[None, :], axis=1)
    offset = token_index - jnp.sum(member_int * starts[None, :], axis=1)
    group_hit = token_group[:, None] == jnp.arange(prompt_length.shape[0], dtype=jnp.int32)[None, :]
    prompt_base = jnp.sum(jnp.where(group_hit, prompt_length[None, :], 0), axis=1)
    token_adapter = jnp.sum(member_int * request_adapter[None, :], axis=1)
    id_hit = (
        token_adapter[:, None] == jnp.arange(adapter_slot_index.shape[0], dtype=jnp.int32)[None, :]
    )
    token_slot = jnp.sum(jnp.where(id_hit, adapter_slot_index[None, :], 0), axis=1)
    return (request_local, token_group, prompt_base + offset, token_slot)


def page_layout(group_page_table, pool_total):
    page_ids = jnp.arange(pool_total, dtype=jnp.int32)
    matches = group_page_table[:, :, None] == page_ids[None, None, :]
    match_int = matches.astype(jnp.int32)
    group_ids = jnp.arange(group_page_table.shape[0], dtype=jnp.int32)
    slot_ids = jnp.arange(group_page_table.shape[1], dtype=jnp.int32)
    page_group = jnp.sum(match_int * group_ids[:, None, None], axis=(0, 1))
    page_slot = jnp.sum(match_int * slot_ids[None, :, None], axis=(0, 1))
    page_used = jnp.sum(match_int, axis=(0, 1)) > 0
    return (page_group, page_slot, page_used)


def expert_hidden(rows, gate_matrix, up_matrix, gate_offset, up_offset):
    gate_pre = lax.dot_general(
        rows, gate_matrix, LAST_DIMS, preferred_element_type=jnp.float32
    ) + gate_offset.astype(jnp.float32)
    up_pre = lax.dot_general(
        rows, up_matrix, LAST_DIMS, preferred_element_type=jnp.float32
    ) + up_offset.astype(jnp.float32)
    gate_pre = jnp.minimum(gate_pre, LIMIT)
    up_pre = jnp.clip(up_pre, -LIMIT, LIMIT)
    return ((up_pre + 1.0) * gate_pre * jax.nn.sigmoid(ALPHA * gate_pre)).astype(jnp.bfloat16)


def device(dp, ep):
    return {"dp": dp, "ep": ep}


def send(src, dst, send_sem, recv_sem, dp, ep):
    copy = pltpu.make_async_remote_copy(
        src_ref=src,
        dst_ref=dst,
        send_sem=send_sem,
        recv_sem=recv_sem,
        device_id=device(dp, ep),
        device_id_type=pl.DeviceIdType.MESH,
    )
    copy.start()
    return copy


def greet(peers):
    barrier = pltpu.get_barrier_semaphore()
    for dp, ep in peers:
        pl.semaphore_signal(
            barrier, inc=1, device_id=device(dp, ep), device_id_type=pl.DeviceIdType.MESH
        )
    return lambda: pl.semaphore_wait(barrier, len(peers))


def flip(index, bits):
    out = index
    for bit in (1, 2, 4):
        if bits & bit:
            out = out + bit * (1 - 2 * ((index // bit) % 2))
    return out


def token_fields(tokens, axis, lengths, groups, adapters, slots, prompt):
    shape = (tokens, 1) if axis == 0 else (1, tokens)
    token = lax.broadcasted_iota(jnp.int32, shape, axis)
    zero = jnp.zeros(shape, jnp.int32)
    request, group, position, slot = zero, zero, zero, zero
    start = lengths[0, 0] * 0
    for m in range(lengths.shape[1]):
        finish = start + lengths[0, m]
        inside = (token >= start) & (token < finish)
        request = jnp.where(inside, m, request)
        if axis == 0:
            group = jnp.where(inside, groups[m], group)
            position = jnp.where(inside, token - start + prompt[groups[m]], position)
        else:
            slot = jnp.where(inside, slots[adapters[m]], slot)
        start = finish
    return request, group, position, slot


def rotation(positions, head_width, lanes):
    half = head_width // 2
    lane = lax.broadcasted_iota(jnp.int32, (positions.shape[0], lanes), 1)
    place = lax.rem(lane, half).astype(jnp.float32)
    frequency = jnp.exp(place * (-2.0 * math.log(THETA) / head_width))
    angles = positions.astype(jnp.float32) * frequency
    cosine, sine = jnp.cos(angles), jnp.sin(angles)
    front = lax.rem(lane, head_width) < half
    signed = jnp.where(front, -sine, sine)

    def turn(values):
        values = values.astype(jnp.float32)
        partner = jnp.where(
            front, pltpu.roll(values, lanes - half, 1), pltpu.roll(values, half, 1)
        )
        return (values * cosine + partner * signed).astype(jnp.bfloat16)

    return turn


def page_groups(page, page_len, table, prompt):
    group, limit = jnp.int32(-1), jnp.int32(0)
    for s in range(table.shape[0]):
        for g in range(table.shape[1]):
            hit = table[s, g] == page
            group = jnp.where(hit, g, group)
            limit = jnp.where(hit, prompt[g] - s * page_len, limit)
    lane = lax.broadcasted_iota(jnp.int32, (1, page_len), 1)
    return jnp.where(lane < limit, group, -1)


def line_peers(i, nd):
    if nd != 4:
        return [lax.rem(i + d, nd) for d in range(1, nd)]
    high = i // 2
    return [3 * (1 - high), 2 - high, (1 - i) * (1 - high) + (5 - i) * high]


def spread(src, dst, send_sem, recv_sem, peers, j):
    return [send(src, dst, send_sem, recv_sem, t, j) for t in peers]


def own_heads(wide, half, head_width):
    keys, values = wide[:, 0, :].astype(jnp.float32), wide[:, 1, :].astype(jnp.float32)
    lane = lax.broadcasted_iota(jnp.int32, keys.shape, 1)
    keys = jnp.where(half == 0, keys, pltpu.roll(keys, head_width, 1))
    values = jnp.where(half == 0, pltpu.roll(values, head_width, 1), values)
    return jnp.where(lane < head_width, keys, values).astype(jnp.bfloat16)


def layer_body(
    nd,
    ne,
    rank_size,
    head_width,
    small_count,
    pages_hbm,
    fresh_hbm,
    *rest,
):
    small_hbm, rest = rest[:small_count], rest[small_count:]
    (gate_hbm, up_hbm, down_hbm, project_hbm, layer_out), rest = rest[:5], rest[5:]
    small, rest = rest[:small_count], rest[small_count:]
    (
        lengths,
        groups,
        adapters,
        slots,
        table,
        prompt,
        expert_slots,
        sinks,
        queries,
        route_experts,
        route_weights,
        adapter_columns,
        residual,
        up,
        gate_offset,
        up_offset,
        down_offset,
        bias,
        gain,
    ) = small
    (
        pages_wide,
        fresh_wide,
        merged,
        combine,
        proj,
        proj_wide,
        pair_out,
        pair_in,
        rank,
        pages_all,
        weights,
        project_matrix,
        gathered,
        gate_matrix,
        up_matrix,
        down_matrix,
        down_parts,
        hidden,
        outs,
        outs_in,
        sums,
        proj_in,
        rank_in,
        up_wide,
        up_part,
        delta,
        delta_full,
        rank_s,
        rank_r,
        proj_s,
        proj_r,
        pair_s,
        pair_r,
        delta_s,
        delta_r,
        wide_s,
        wide_r,
        plane_s,
        plane_r,
        chip_s,
        chip_r,
        hop_s,
        hop_r,
        pass_s,
        pass_r,
        load_sem,
        unit_s,
        unit_r,
        relay_s,
        out_s,
        out_r,
        sum_s,
        sum_r,
        page_s,
        page_r,
        combine_s,
        combine_r,
        small_sem,
        wide_sem,
        plane_hop_s,
    ) = rest
    i, j = lax.axis_index("dp"), lax.axis_index("ep")
    heads = sinks.shape[0]
    lanes = 2 * head_width
    page_count, page_len = pages_hbm.shape[:2]
    kv_head = j * (fresh_hbm.shape[2] // head_width) // ne
    block = pl.ds(pl.multiple_of(kv_head // 2 * lanes, lanes), lanes)
    head_loads = [
        pltpu.make_async_copy(pages_hbm.at[:, :, :, block], pages_wide, wide_sem.at[0]),
        pltpu.make_async_copy(fresh_hbm.at[:, :, block], fresh_wide, wide_sem.at[1]),
    ]
    for copy in head_loads:
        copy.start()
    peers = line_peers(i, nd)
    near_first = peers[::-1]
    relays = nd == 4
    inner = (i == 1) | (i == nd - 2)
    far_item = lax.rem(6 - 3 * i + 6, 6)
    end = 3 - far_item

    def carry(block, send_sem, recv_sem, target):
        return pltpu.make_async_remote_copy(
            src_ref=block,
            dst_ref=block,
            send_sem=send_sem,
            recv_sem=recv_sem,
            device_id=device(target, j),
            device_id_type=pl.DeviceIdType.MESH,
        )

    def all_sent(block, send_sem):
        carry(block, send_sem, send_sem, peers[0]).wait_send()

    def all_arrived(block, recv_sem):
        carry(block, recv_sem, recv_sem, peers[0]).wait_recv()

    others = pl.ds(0, nd - 1)

    def skips(target):
        apart = (i - target) * (i - target)
        return (apart == 9) | (inner & (apart == 4))

    def unless(skip, action):
        if skip is None:
            action()
        else:
            pl.when(jnp.logical_not(skip))(action)

    loads = [
        pltpu.make_async_copy(source, target, load_sem.at[n])
        for n, (source, target) in enumerate(
            (
                (gate_hbm.at[0], gate_matrix),
                (up_hbm.at[0], up_matrix),
                (down_hbm.at[0], down_matrix),
                (project_hbm, project_matrix),
            )
        )
    ]
    small_loads = [
        pltpu.make_async_copy(source, target, small_sem.at[n])
        for n, (source, target) in enumerate(zip(small_hbm, small))
    ]
    for copy in small_loads:
        copy.start()
    everyone = [(d, e) for d in range(nd) for e in range(ne) if d or e]
    met = greet([(lax.rem(i + d, nd), lax.rem(j + e, ne)) for d, e in everyone])
    half = lax.rem(kv_head, 2)
    head_loads[0].wait()
    pages_all[i] = own_heads(
        pages_wide[...].reshape(page_count * page_len, 2, lanes), half, head_width
    )
    met()
    page_copies = spread(pages_all.at[i], pages_all.at[i], page_s, page_r, peers, j)
    head_loads[1].wait()
    for copy in small_loads:
        copy.wait()
    for n in (3, 0, 1, 2):
        loads[n].start()
    rows = residual.shape[0]
    experts_of = route_experts[...]
    holders = jnp.zeros_like(experts_of)
    for e in range(expert_slots.shape[0]):
        holders = jnp.where(experts_of == e, expert_slots[e], holders)
    combine[...] = jnp.zeros_like(combine)
    for e in range(ne):
        combine[e : e + 1, :rows] = jnp.sum(
            jnp.where(holders == e, route_weights[...], 0.0), axis=0, keepdims=True
        )
    combine_copies = spread(combine, weights.at[i], combine_s, combine_r, peers, j)
    weights[i] = combine[...]
    tokens_row = queries.shape[0]
    fresh = own_heads(fresh_wide[...], half, head_width)
    scale = 1.0 / math.sqrt(head_width)
    request, group, position, _ = token_fields(
        tokens_row, 0, lengths, groups, adapters, slots, prompt
    )
    request_row, _, _, slot = token_fields(
        tokens_row, 1, lengths, groups, adapters, slots, prompt
    )
    turn = rotation(position, head_width, lanes)
    turned = [turn(queries[:, n * lanes : (n + 1) * lanes]) for n in range(heads // 2)]
    query_rows = jnp.concatenate(
        [pair[:, n * head_width : (n + 1) * head_width] for pair in turned for n in (0, 1)], axis=0
    )
    row_index = lax.broadcasted_iota(jnp.int32, (tokens_row, tokens_row), 0)
    column_index = lax.broadcasted_iota(jnp.int32, (tokens_row, tokens_row), 1)

    def masked_scores(keys, mask):
        width = keys.shape[0]
        scores = scale * lax.dot_general(
            query_rows, keys, LAST_DIMS, preferred_element_type=jnp.float32
        )
        return jnp.where(mask[None], scores.reshape(heads, tokens_row, width), NEG)

    score_list = [
        masked_scores(
            turn(fresh)[:, :head_width],
            (request == request_row) & (column_index <= row_index),
        )
    ]
    value_list = [fresh[:, head_width:]]
    key_groups = [page_groups(p, page_len, table, prompt) for p in range(nd * page_count)]
    all_arrived(pages_all.at[others], page_r)
    width, part = residual.shape[1], delta.shape[2]
    own_part = pl.ds(pl.multiple_of(j * part, part), part)
    up_wide[:, :width] = up[...]
    up_wide[:, width:] = jnp.zeros((up.shape[0], ne * part - width), jnp.bfloat16)
    up_part[i] = up_wide[:, own_part]
    wide_copies = spread(up_wide.at[:, own_part], up_part.at[i], wide_s, wide_r, peers, j)
    for d in range(nd):
        shard = pages_all[d]
        mask = group == jnp.concatenate(
            key_groups[d * page_count : (d + 1) * page_count], axis=1
        )
        score_list.append(masked_scores(shard[:, :head_width], mask))
        value_list.append(shard[:, head_width:])
    sink = jnp.concatenate(
        [jnp.full((1, tokens_row, 1), sinks[h], jnp.float32) for h in range(heads)], axis=0
    )
    peak = sink
    for scores in score_list:
        peak = jnp.maximum(peak, jnp.max(scores, axis=-1, keepdims=True))
    denominator = jnp.exp(sink - peak)
    weighted = jnp.zeros((heads * tokens_row, head_width), jnp.float32)
    for scores, values in zip(score_list, value_list):
        probs = jnp.exp(scores - peak)
        denominator = denominator + jnp.sum(probs, axis=-1, keepdims=True)
        weighted = weighted + jnp.dot(
            probs.reshape(heads * tokens_row, -1).astype(jnp.bfloat16),
            values,
            preferred_element_type=jnp.float32,
        )
    attended = weighted.reshape(heads, tokens_row, head_width) / denominator
    attended = jnp.concatenate([attended[h] for h in range(heads)], axis=1).astype(jnp.bfloat16)
    rank_width = nd * up.shape[0]
    slot_rows = (
        lax.broadcasted_iota(jnp.int32, (rank_width, tokens_row), 0) // rank_size == slot
    )
    rank_all = lax.dot_general(
        adapter_columns[...], attended, LAST_DIMS, preferred_element_type=jnp.float32
    )
    rank_all = jnp.where(slot_rows, rank_all, 0.0)
    rank[...] = jnp.sum(
        rank_all.reshape(rank_width // rank_size, rank_size, tokens_row), axis=0
    ).astype(jnp.bfloat16)
    rank_copies, proj_copies = [], []
    for e in range(1, ne):
        rank_copies.append(
            send(
                rank, rank_in.at[e - 1], rank_s, rank_r, i, lax.rem(j + e, ne)
            )
        )
    loads[3].wait()
    projected = lax.dot_general(
        attended, project_matrix[...], LAST_DIMS, preferred_element_type=jnp.float32
    )
    for e in range(ne):
        proj_wide[e] = projected[e * rows : (e + 1) * rows]
    turns = (6, 2, 4, 0)
    pair_copies = []
    for n, bits in enumerate(turns):
        pair_out[n] = proj_wide[flip(j, bits + 1)].astype(jnp.bfloat16)
        pair_copies.append(
            send(pair_out.at[n], pair_in.at[n], pair_s, pair_r.at[n], i, flip(j, 1))
        )
    for n, bits in enumerate(turns):
        pair_copies[n].wait_recv()
        total = proj_wide[flip(j, bits)] + pair_in[n].astype(jnp.float32)
        if bits:
            proj[n] = total.astype(jnp.bfloat16)
            proj_copies.append(
                send(proj.at[n], proj_in.at[n], proj_s, proj_r, i, flip(j, bits))
            )
    all_sent(rank_in, rank_s)
    all_arrived(rank_in, rank_r)
    all_arrived(up_part.at[others], wide_r)
    middle = rank[...].astype(jnp.float32)
    for e in range(1, ne):
        middle = middle + rank_in[e - 1].astype(jnp.float32)
    middles = jnp.concatenate([middle] * (rank_width // rank_size), axis=0)
    middles = jnp.where(slot_rows, middles, 0.0).astype(jnp.bfloat16)
    updates = lax.dot_general(
        middles,
        up_part[...].reshape(rank_width, part),
        (((0,), (0,)), ((), ())),
        preferred_element_type=jnp.float32,
    )
    updates = ADAPTER_SCALE * updates
    for e in range(ne):
        delta[e] = updates[e * rows : (e + 1) * rows].astype(jnp.bfloat16)
    delta_full[:, own_part] = delta[j]
    delta_copies = []
    for e in range(1, ne):
        tj = lax.rem(j + e, ne)
        delta_copies.append(
            send(
                delta.at[tj],
                delta_full.at[:, own_part],
                delta_s,
                delta_r,
                i,
                tj,
            )
        )
    all_sent(proj, proj_s)
    all_arrived(proj_in, proj_r)
    for n in range(3):
        total = total + proj_in[n].astype(jnp.float32)
    total = total + residual[...].astype(jnp.float32) + bias[...].astype(jnp.float32).reshape(1, -1)
    all_sent(delta.at[pl.ds(0, ne - 1)], delta_s)
    all_arrived(delta.at[pl.ds(0, ne - 1)], delta_r)
    total = total + delta_full[:, :width].astype(jnp.float32)
    rounded = total.astype(jnp.bfloat16)
    stream = rounded.astype(jnp.float32)
    mean_square = jnp.mean(stream * stream, axis=-1, keepdims=True)
    normed = stream * lax.rsqrt(mean_square + EPSILON) * gain[...].astype(jnp.float32).reshape(1, -1)
    gathered[j, i] = normed.astype(jnp.bfloat16)
    plane_copies = []
    for n, t in enumerate(peers):
        copy = carry(gathered.at[j, i], plane_s, plane_r.at[i], t)
        skip = skips(t) if relays else None
        plane_copies.append((copy, skip))
        unless(skip, copy.start)
    sibling, across, along = flip(j, 1), flip(j, 2), flip(j, 4)
    chip_copies = []

    def to_chips(d):
        for n, target in enumerate((across, along, sibling)):
            piece = gathered.at[j, d]
            chip_copies.append(send(piece, piece, chip_s, chip_r.at[n], i, target))

    to_chips(i)
    loads[2].wait()
    units_own = down_parts.shape[2]
    for d in range(nd):
        down_parts[d] = down_matrix[:, d * units_own : (d + 1) * units_own]
    def landed(t):
        return carry(gathered.at[j, t], plane_s, plane_r.at[t], t)

    def plane_hop(n, t):
        return carry(gathered.at[j, t], plane_hop_s.at[n], plane_r.at[t], end)

    if relays:

        @pl.when(inner)
        def _():
            for n, t in enumerate((3 - i, far_item)):
                landed(t).wait_recv()
                plane_hop(n, t).start()

    for t in near_first:
        unless(inner & (t != end) if relays else None, landed(t).wait_recv)
        to_chips(t)

    def from_chip(n, source):
        all_arrived(gathered.at[source], chip_r.at[n])

    core = lax.rem(j, 2)
    hop_from = along + core * (across - along)
    hop_to = across + core * (along - across)
    passed = []
    chunks = (0, 2, 4, 6)
    unit_copies = []

    def units(c):
        bits = chunks[c]
        blocks = [
            gathered[flip(j, bits + n)].astype(jnp.float32).reshape(nd * rows, -1) for n in (0, 1)
        ]
        tokens = jnp.concatenate(blocks, axis=0).astype(jnp.bfloat16)
        hidden[i, c] = expert_hidden(
            tokens, gate_matrix[...], up_matrix[...], gate_offset[...], up_offset[...]
        )
        for ti in peers:
            copy = carry(hidden.at[i, c], unit_s, unit_r.at[i, c], ti)
            skip = skips(ti) if relays else None
            unit_copies.append((copy, skip))
            unless(skip, copy.start)

    def passage(item, c, n):
        return carry(hidden.at[item, c], relay_s.at[n, c], unit_r.at[item, c], end)

    def arrival(item, c):
        return carry(hidden.at[item, c], unit_s, unit_r.at[item, c], item)

    def relay(n, c, before):
        if not relays:
            return

        @pl.when(inner)
        def _():
            item = (3 - i, far_item)[n]
            arrival(item, c).wait_recv()
            if before is not None:
                passage(item, before, n).wait_send()
            passage(item, c, n).start()

    def pass_on(other):
        n = len(passed)
        passed.append(
            send(gathered.at[other], gathered.at[other], pass_s, pass_r.at[n], i, sibling)
        )

    out_copies = []

    def shard_down(c, item):
        return lax.dot_general(
            hidden[item, c], down_parts[item], LAST_DIMS, preferred_element_type=jnp.float32
        )

    def add_arrivals(c, items, result):
        for item in items:
            unless(inner & (item != end) if relays else None, arrival(item, c).wait_recv)
            result = result + shard_down(c, item)
        return result

    def begin(c):
        result = down_offset[...].astype(jnp.float32) + shard_down(c, i)
        return add_arrivals(c, near_first[:-1], result)

    def finish(c, result):
        result = add_arrivals(c, near_first[-1:], result)
        for n in (0, 1):
            other = flip(j, chunks[c] + n)
            for d in range(nd):
                start = (n * nd + d) * rows
                outs[other, d] = result[start : start + rows].astype(jnp.bfloat16)
            if chunks[c] + n:
                place = chunks[c] + n - 1
                out_copies.append(
                    send(
                        outs.at[other], outs_in.at[place], out_s, out_r, i, other
                    )
                )

    loads[0].wait()
    loads[1].wait()
    from_chip(2, sibling)
    units(0)
    from_chip(0, across)
    pass_on(across)
    from_chip(1, along)
    pass_on(along)
    hop = send(gathered.at[hop_from], gathered.at[hop_from], hop_s, hop_r, i, hop_to)
    passed[0].wait_recv()
    units(1)
    relay(0, 0, None)
    hop.wait_recv()
    pass_on(flip(j, 6))
    passed[1].wait_recv()
    units(2)
    relay(0, 1, None)
    passed[2].wait_recv()
    units(3)
    relay(1, 1, None)
    relay(0, 2, 0)
    own_chip = begin(0)
    finish(1, begin(1))
    relay(1, 2, None)
    relay(0, 3, 1)
    finish(2, begin(2))
    relay(1, 3, 1)
    finish(3, begin(3))
    relay(1, 0, 2)
    finish(0, own_chip)
    all_arrived(outs_in, out_r)
    all_arrived(weights.at[others], combine_r)
    diagonal = lax.broadcasted_iota(jnp.int32, (rows, rows), 0) == lax.broadcasted_iota(
        jnp.int32, (rows, rows), 1
    )
    for d in range(nd):
        total = 0.0
        for bits in range(ne):
            piece = outs[j, d] if bits == 0 else outs_in[bits - 1, d]
            line = weights[d, pl.ds(flip(j, bits), 1), :][:, :rows]
            factor = jnp.sum(jnp.where(diagonal, line, 0.0), axis=1, keepdims=True)
            total = total + piece.astype(jnp.float32) * factor
        sums[d] = total.astype(jnp.bfloat16)
    finals = [
        send(sums.at[t], merged.at[i], sum_s, sum_r, t, j)
        for t in peers
    ]
    merged[i] = sums[i]
    sends = pl.ds(0, 2 if relays else nd - 1)
    all_sent(hidden.at[sends], unit_s)
    all_sent(gathered.at[0, sends], plane_s)
    if relays:

        @pl.when(inner)
        def _():
            for n, t in enumerate((3 - i, far_item)):
                plane_hop(n, t).wait_send()
            for n, c in ((0, 2), (0, 3), (1, 3), (1, 0)):
                passage(0, c, n).wait_send()

    hop.wait_send()
    three = pl.ds(0, 3)
    for block, sem in (
        (gathered.at[three], chip_s),
        (gathered.at[three], pass_s),
        (outs.at[pl.ds(0, ne - 1)], out_s),
        (pages_all.at[others], page_s),
        (weights.at[others], combine_s),
        (up_part.at[others], wide_s),
        (pair_out, pair_s),
    ):
        all_sent(block, sem)
    all_sent(merged.at[others], sum_s)
    all_arrived(merged.at[others], sum_r)
    update = jnp.concatenate([merged[d].astype(jnp.float32) for d in range(nd)], axis=1)
    layer_out[...] = (stream + update).astype(jnp.bfloat16)


def layer(nd, ne, rank_size, head_width, front, scalars, small, matrices):
    caches, fresh = front
    lanes = 2 * head_width
    page_rows = caches.shape[0] * caches.shape[1]
    residual, up = small[4:6]
    rows, width = residual.shape
    part = -(-width // (128 * ne)) * 128
    units = matrices[0].shape[1]
    dma = pltpu.SemaphoreType.DMA
    held = scalars + small
    args = front + held + matrices
    vmem = pl.BlockSpec(memory_space=pltpu.VMEM)
    bf16 = jnp.bfloat16
    return pl.pallas_call(
        functools.partial(layer_body, nd, ne, rank_size, head_width, len(held)),
        out_shape=jax.ShapeDtypeStruct((rows, width), bf16),
        in_specs=[pl.BlockSpec(memory_space=pltpu.HBM)] * len(args),
        out_specs=vmem,
        scratch_shapes=[pltpu.SMEM(x.shape, x.dtype) for x in scalars]
        + [pltpu.VMEM(x.shape, x.dtype) for x in small]
        + [
            pltpu.VMEM(caches.shape[:3] + (lanes,), bf16),
            pltpu.VMEM(fresh.shape[:2] + (lanes,), bf16),
            pltpu.VMEM((nd, rows, units), bf16),
            pltpu.VMEM((ne, 128), jnp.float32),
            pltpu.VMEM((3, rows, width), bf16),
            pltpu.VMEM((ne, rows, width), jnp.float32),
            pltpu.VMEM((4, rows, width), bf16),
            pltpu.VMEM((4, rows, width), bf16),
            pltpu.VMEM((rank_size, small[0].shape[0]), bf16),
            pltpu.VMEM((nd, page_rows, lanes), bf16),
            pltpu.VMEM((nd, ne, 128), jnp.float32),
            pltpu.VMEM(matrices[3].shape, bf16),
            pltpu.VMEM((ne, nd, rows, width), bf16),
            pltpu.VMEM((units, width), bf16),
            pltpu.VMEM((units, width), bf16),
            pltpu.VMEM((units, width), bf16),
            pltpu.VMEM((nd, units, width // nd), bf16),
            pltpu.VMEM((nd, 4, 2 * nd * rows, units), bf16),
            pltpu.VMEM((ne, nd, rows, units), bf16),
            pltpu.VMEM((ne - 1, nd, rows, units), bf16),
            pltpu.VMEM((nd, rows, units), bf16),
            pltpu.VMEM((3, rows, width), bf16),
            pltpu.VMEM((ne - 1, rank_size, small[0].shape[0]), bf16),
            pltpu.VMEM((up.shape[0], ne * part), bf16),
            pltpu.VMEM((nd, up.shape[0], part), bf16),
            pltpu.VMEM((ne, rows, part), bf16),
            pltpu.VMEM((rows, ne * part), bf16),
            dma,
            dma,
            dma,
            dma,
            dma,
            dma((4,)),
            dma,
            dma,
            dma,
            dma,
            dma,
            dma((nd,)),
            dma,
            dma((3,)),
            dma,
            dma,
            dma,
            dma((3,)),
            dma((4,)),
            dma,
            dma((nd, 4)),
            dma((2, 4)),
            dma,
            dma,
            dma,
            dma,
            dma,
            dma,
            dma,
            dma,
            dma((len(held),)),
            dma((2,)),
            dma((2,)),
        ],
        compiler_params=pltpu.CompilerParams(
            collective_id=2, has_side_effects=True, vmem_limit_bytes=60 * 2**20
        ),
    )(*args)


def on_device(
    residual,
    queries,
    fresh_key_value,
    prompt_page_cache,
    group_page_table,
    prompt_length,
    suffix_length,
    request_group,
    request_adapter_index,
    adapter_slot_index,
    adapter_down_maps,
    adapter_up_maps,
    sinks,
    output_weight,
    output_bias,
    norm_weight,
    token_experts,
    expert_gate_weight,
    expert_slot_index,
    gate_weight,
    up_weight,
    down_weight,
    gate_bias,
    up_bias,
    down_bias,
):
    heads_per_device = sinks.shape[0]
    tok_row = queries.shape[0]
    head_width = queries.shape[1] // heads_per_device
    kv_count = fresh_key_value.shape[2] // head_width
    ep_count = lax.axis_size("ep")
    data_parallel_count = lax.axis_size("dp")
    group_size = heads_per_device * ep_count // kv_count
    kv_head = lax.axis_index("ep") * heads_per_device // group_size
    tokens_per_device = tok_row // ep_count
    hidden_width = residual.shape[1]
    adapter_weights = adapter_down_maps.shape[0]
    adapter_rank_size = adapter_down_maps.shape[2]
    score_scale = 1.0 / math.sqrt(head_width)
    own_kv = lax.dynamic_slice_in_dim(fresh_key_value, kv_head * head_width, head_width, 2)
    experts = expert_slot_index.shape[0]
    top_count = token_experts.shape[1]
    capacity = max(2, 8 * tokens_per_device // experts)
    direct = experts == ep_count and ep_count == 8 and capacity >= tokens_per_device
    if direct:
        return layer(
            data_parallel_count,
            ep_count,
            adapter_rank_size,
            head_width,
            (prompt_page_cache, fresh_key_value),
            (
                suffix_length,
                request_group,
                request_adapter_index,
                adapter_slot_index,
                group_page_table.T,
                prompt_length,
                expert_slot_index,
                sinks,
            ),
            (
                queries,
                token_experts.T,
                expert_gate_weight.T,
                adapter_down_maps.transpose(0, 2, 1).reshape(-1, heads_per_device * head_width),
                residual,
                adapter_up_maps.reshape(-1, hidden_width),
                gate_bias,
                up_bias,
                down_bias,
                output_bias,
                norm_weight,
            ),
            (gate_weight, up_weight, down_weight, output_weight.T),
        )
    expert_hit = token_experts[:, :, None] == jnp.arange(experts, dtype=jnp.int32)[None, None, :]
    route_col = jnp.sum(jnp.where(expert_hit, expert_slot_index[None, None, :], 0), axis=2)
    request_local, token_group, positions, token_slot = token_layout(
        suffix_length[0],
        request_group,
        request_adapter_index,
        adapter_slot_index,
        prompt_length,
        tok_row,
    )
    queries_rot = rotate(
        queries.reshape(tok_row, heads_per_device, head_width).astype(jnp.float32), positions
    ).astype(jnp.bfloat16)
    keys_new = rotate(own_kv[:, 0:1, :].astype(jnp.float32), positions)[:, 0, :].astype(
        jnp.bfloat16
    )
    values_new = own_kv[:, 1, :]
    token_index = jnp.arange(tok_row, dtype=jnp.int32)
    allowed = (request_local[:, None] == request_local[None, :]) & (
        token_index[None, :] <= token_index[:, None]
    )
    local_scores = (
        jnp.einsum("thd,sd->hts", queries_rot, keys_new, preferred_element_type=jnp.float32)
        * score_scale
    )
    local_masked = jnp.where(allowed[None], local_scores, NEG)
    sink_col = sinks[:, None]
    run_max = jnp.maximum(sink_col, jnp.max(local_masked, axis=-1))
    local_exp = jnp.exp(local_masked - run_max[..., None])
    run_total = jnp.exp(sink_col - run_max) + jnp.sum(local_exp, axis=-1)
    run_acc = jnp.einsum(
        "hts,sd->htd",
        local_exp.astype(jnp.bfloat16),
        values_new,
        preferred_element_type=jnp.float32,
    )
    page_len = prompt_page_cache.shape[1]
    pool_total = prompt_page_cache.shape[0] * data_parallel_count
    page_group, page_slot, page_used = page_layout(group_page_table, pool_total)
    group_hit = page_group[:, None] == jnp.arange(prompt_length.shape[0], dtype=jnp.int32)[None, :]
    page_limit = jnp.sum(jnp.where(group_hit, prompt_length[None, :], 0), axis=1)
    own_pages = lax.dynamic_slice_in_dim(prompt_page_cache, kv_head * head_width, head_width, 3)
    shard_rows = lax.all_gather(own_pages, "dp", axis=0, tiled=True)
    piece_pages = shard_rows.shape[0]
    keys_piece = shard_rows[:, :, 0, :].reshape(piece_pages * page_len, head_width)
    values_piece = shard_rows[:, :, 1, :].reshape(piece_pages * page_len, head_width)
    key_pos = page_slot[:, None] * page_len + jnp.arange(page_len, dtype=jnp.int32)[None, :]
    key_valid = (page_used[:, None] & (key_pos < page_limit[:, None])).reshape(-1)
    key_group = jnp.broadcast_to(page_group[:, None], (piece_pages, page_len)).reshape(-1)
    visible = (token_group[:, None] == key_group[None, :]) & key_valid[None, :]
    scores = (
        jnp.einsum("thd,sd->hts", queries_rot, keys_piece, preferred_element_type=jnp.float32)
        * score_scale
    )
    masked = jnp.where(visible[None], scores, NEG)
    new_max = jnp.maximum(run_max, jnp.max(masked, axis=-1))
    factor = jnp.exp(run_max - new_max)
    weights = jnp.exp(masked - new_max[..., None])
    new_total = run_total * factor + jnp.sum(weights, axis=-1)
    new_acc = run_acc * factor[..., None] + jnp.einsum(
        "hts,sd->htd",
        weights.astype(jnp.bfloat16),
        values_piece,
        preferred_element_type=jnp.float32,
    )
    attention_output = (
        (new_acc / new_total[..., None])
        .transpose(1, 0, 2)
        .reshape(tok_row, heads_per_device * head_width)
        .astype(jnp.bfloat16)
    )
    adapter_onehot = token_slot[:, None] == jnp.arange(adapter_weights, dtype=jnp.int32)[None, :]
    adapter_pick_all = adapter_onehot.astype(jnp.float32)
    adapter_columns = adapter_down_maps.transpose(1, 0, 2).reshape(
        heads_per_device * head_width, adapter_weights * adapter_rank_size
    )
    projected_rows = jnp.dot(attention_output, output_weight, preferred_element_type=jnp.float32)
    reduced_rank = jnp.dot(
        attention_output, adapter_columns, preferred_element_type=jnp.float32
    ).reshape(tokens_per_device * lax.axis_size("ep"), adapter_weights, adapter_rank_size)
    reduced_rank = jnp.sum(reduced_rank * adapter_pick_all[:, :, None], axis=1)
    summed_rows = lax.psum_scatter(
        jnp.concatenate([projected_rows, reduced_rank], axis=1).astype(jnp.bfloat16),
        "ep",
        scatter_dimension=0,
        tiled=True,
    ).astype(jnp.float32)
    projection_sum = summed_rows[:, :hidden_width]
    adapter_middle = summed_rows[:, hidden_width:].astype(jnp.bfloat16)
    owner_onehot = lax.dynamic_slice_in_dim(
        adapter_onehot, lax.axis_index("ep") * tokens_per_device, tokens_per_device, 0
    )
    spread_rows = owner_onehot.astype(jnp.bfloat16)[:, :, None] * adapter_middle[:, None, :]
    holder_count = adapter_up_maps.shape[0]
    outgoing = spread_rows.reshape(
        tokens_per_device, data_parallel_count, holder_count * adapter_rank_size
    )
    incoming = lax.all_to_all(outgoing, "dp", split_axis=1, concat_axis=0, tiled=True)
    adapter_updates = jnp.dot(
        incoming.reshape(data_parallel_count * tokens_per_device, holder_count * adapter_rank_size),
        adapter_up_maps.reshape(holder_count * adapter_rank_size, hidden_width),
        preferred_element_type=jnp.float32,
    )
    adapter_updates = (
        (ADAPTER_SCALE * adapter_updates)
        .astype(jnp.bfloat16)
        .reshape(data_parallel_count, tokens_per_device, hidden_width)
    )
    returned_rows = lax.all_to_all(adapter_updates, "dp", split_axis=0, concat_axis=0, tiled=True)
    adapter_update = jnp.sum(returned_rows.astype(jnp.float32), axis=0)
    stream = settle(
        residual.astype(jnp.float32)
        + projection_sum
        + output_bias.astype(jnp.float32)
        + adapter_update
    )
    mean_square = jnp.mean(stream * stream, axis=-1, keepdims=True)
    normed = (stream * lax.rsqrt(mean_square + EPSILON) * norm_weight.astype(jnp.float32)).astype(
        jnp.bfloat16
    )
    slots_all = ep_count * capacity
    route_col = route_col.reshape(-1)
    col_hot = (route_col[:, None] == jnp.arange(ep_count, dtype=jnp.int32)[None, :]).astype(
        jnp.int32
    )
    route_order = jnp.arange(route_col.shape[0], dtype=jnp.int32)
    earlier = (route_order[None, :] < route_order[:, None]).astype(jnp.int32)
    route_rank = jnp.sum(earlier * (route_col[None, :] == route_col[:, None]), axis=1)
    target_slot = route_col * capacity + route_rank
    target_hot = (target_slot[:, None] == jnp.arange(slots_all, dtype=jnp.int32)[None, :]).reshape(
        tokens_per_device, top_count, slots_all
    )
    scatter_rows = jnp.sum(target_hot.astype(jnp.float32), axis=1)
    combine = jnp.sum(jnp.where(target_hot, expert_gate_weight[:, :, None], 0.0), axis=1)
    outbound = (
        jnp.dot(scatter_rows.T.astype(jnp.bfloat16), normed, preferred_element_type=jnp.float32)
        .astype(jnp.bfloat16)
        .reshape(ep_count, capacity, hidden_width)
    )
    received = lax.all_to_all(outbound, "ep", split_axis=0, concat_axis=0, tiled=True)
    rows_flat = lax.all_gather(received[None], "dp", axis=0, tiled=True).reshape(-1, hidden_width)
    hidden = expert_hidden(rows_flat, gate_weight[0], up_weight[0], gate_bias[0], up_bias[0])
    unit_weights = down_weight[0]
    unit_sum = lax.dot_general(
        lax.all_gather(hidden, "dp", axis=1, tiled=True),
        unit_weights,
        LAST_DIMS,
        preferred_element_type=jnp.float32,
    )
    expert_out = (
        (unit_sum + down_bias[0].astype(jnp.float32))
        .astype(jnp.bfloat16)
        .reshape(data_parallel_count, slots_all, -1)
    )
    home_rows = lax.all_to_all(expert_out, "dp", split_axis=0, concat_axis=2, tiled=True)
    back_rows = lax.all_to_all(
        home_rows.reshape(ep_count, capacity, hidden_width),
        "ep",
        split_axis=0,
        concat_axis=0,
        tiled=True,
    )
    merged = jnp.dot(
        combine,
        back_rows.reshape(slots_all, hidden_width).astype(jnp.float32),
        precision=lax.Precision.HIGHEST,
        preferred_element_type=jnp.float32,
    )
    return (stream + merged).astype(jnp.bfloat16)


def solution(mesh):
    placed = (
        P(("dp", "ep"), None),
        P("dp", "ep"),
        P("dp", None, None),
        P("dp", None, None, None),
        P(),
        P(),
        P("dp", None),
        P("dp"),
        P("dp"),
        P(),
        P(None, "ep", None),
        P("dp", None, None),
        P("ep"),
        P("ep", None),
        P(),
        P(),
        P(("dp", "ep"), None),
        P(("dp", "ep"), None),
        P(),
        P("ep", "dp", None),
        P("ep", "dp", None),
        P("ep", "dp", None),
        P("ep", "dp"),
        P("ep", "dp"),
        P("ep", "dp"),
    )
    return jax.shard_map(
        on_device, mesh=mesh, in_specs=placed, out_specs=P(("dp", "ep"), None), check_vma=False
    )
```

```python
import functools
import math

import jax
import jax.numpy as jnp
from jax import lax
from jax.experimental import pallas as pl
from jax.experimental.pallas import tpu as pltpu
from jax.sharding import PartitionSpec as P

THETA = 150000.0
NEG = -1e30
LIMIT = 7.0
ALPHA = 1.702
EPSILON = 1e-05
ADAPTER_SCALE = 2.0
LAST_DIMS = (((1,), (1,)), ((), ()))


def settle(values):
    return lax.optimization_barrier(values.astype(jnp.bfloat16)).astype(jnp.float32)


def rotate(values, positions):
    head_width = values.shape[-1]
    half_size = head_width // 2
    frequency = THETA ** (-2.0 * jnp.arange(half_size, dtype=jnp.float32) / head_width)
    angles = positions.astype(jnp.float32)[:, None] * frequency[None, :]
    cosine = jnp.cos(angles)[:, None, :]
    sine_part = jnp.sin(angles)[:, None, :]
    front_part = values[..., :half_size]
    back_part = values[..., half_size:]
    return jnp.concatenate(
        [front_part * cosine - back_part * sine_part, back_part * cosine + front_part * sine_part],
        axis=-1,
    )


def token_layout(lengths, groups, request_adapter, adapter_slot_index, prompt_length, tok_count):
    order = jnp.arange(lengths.shape[0], dtype=jnp.int32)
    finish = jnp.sum(jnp.where(order[None, :] <= order[:, None], lengths[None, :], 0), axis=1)
    starts = finish - lengths
    token_index = jnp.arange(tok_count, dtype=jnp.int32)
    member = (token_index[:, None] >= starts[None, :]) & (token_index[:, None] < finish[None, :])
    member_int = member.astype(jnp.int32)
    request_local = jnp.sum(
        member_int * jnp.arange(lengths.shape[0], dtype=jnp.int32)[None, :], axis=1
    )
    token_group = jnp.sum(member_int * groups[None, :], axis=1)
    offset = token_index - jnp.sum(member_int * starts[None, :], axis=1)
    group_hit = token_group[:, None] == jnp.arange(prompt_length.shape[0], dtype=jnp.int32)[None, :]
    prompt_base = jnp.sum(jnp.where(group_hit, prompt_length[None, :], 0), axis=1)
    token_adapter = jnp.sum(member_int * request_adapter[None, :], axis=1)
    id_hit = (
        token_adapter[:, None] == jnp.arange(adapter_slot_index.shape[0], dtype=jnp.int32)[None, :]
    )
    token_slot = jnp.sum(jnp.where(id_hit, adapter_slot_index[None, :], 0), axis=1)
    return (request_local, token_group, prompt_base + offset, token_slot)


def page_layout(group_page_table, pool_total):
    page_ids = jnp.arange(pool_total, dtype=jnp.int32)
    matches = group_page_table[:, :, None] == page_ids[None, None, :]
    match_int = matches.astype(jnp.int32)
    group_ids = jnp.arange(group_page_table.shape[0], dtype=jnp.int32)
    slot_ids = jnp.arange(group_page_table.shape[1], dtype=jnp.int32)
    page_group = jnp.sum(match_int * group_ids[:, None, None], axis=(0, 1))
    page_slot = jnp.sum(match_int * slot_ids[None, :, None], axis=(0, 1))
    page_used = jnp.sum(match_int, axis=(0, 1)) > 0
    return (page_group, page_slot, page_used)


def expert_hidden(rows, gate_matrix, up_matrix, gate_offset, up_offset):
    gate_pre = lax.dot_general(
        rows, gate_matrix, LAST_DIMS, preferred_element_type=jnp.float32
    ) + gate_offset.astype(jnp.float32)
    up_pre = lax.dot_general(
        rows, up_matrix, LAST_DIMS, preferred_element_type=jnp.float32
    ) + up_offset.astype(jnp.float32)
    gate_pre = jnp.minimum(gate_pre, LIMIT)
    up_pre = jnp.clip(up_pre, -LIMIT, LIMIT)
    return ((up_pre + 1.0) * gate_pre * jax.nn.sigmoid(ALPHA * gate_pre)).astype(jnp.bfloat16)


def device(dp, ep):
    return {"dp": dp, "ep": ep}


def send(src, dst, send_sem, recv_sem, dp, ep):
    copy = pltpu.make_async_remote_copy(
        src_ref=src,
        dst_ref=dst,
        send_sem=send_sem,
        recv_sem=recv_sem,
        device_id=device(dp, ep),
        device_id_type=pl.DeviceIdType.MESH,
    )
    copy.start()
    return copy


def greet(peers):
    barrier = pltpu.get_barrier_semaphore()
    for dp, ep in peers:
        pl.semaphore_signal(
            barrier, inc=1, device_id=device(dp, ep), device_id_type=pl.DeviceIdType.MESH
        )
    return lambda: pl.semaphore_wait(barrier, len(peers))


def flip(index, bits):
    out = index
    for bit in (1, 2, 4):
        if bits & bit:
            out = out + bit * (1 - 2 * ((index // bit) % 2))
    return out


def token_fields(tokens, axis, lengths, groups, adapters, slots, prompt):
    shape = (tokens, 1) if axis == 0 else (1, tokens)
    token = lax.broadcasted_iota(jnp.int32, shape, axis)
    zero = jnp.zeros(shape, jnp.int32)
    request, group, position, slot = zero, zero, zero, zero
    start = lengths[0, 0] * 0
    for m in range(lengths.shape[1]):
        finish = start + lengths[0, m]
        inside = (token >= start) & (token < finish)
        request = jnp.where(inside, m, request)
        if axis == 0:
            group = jnp.where(inside, groups[m], group)
            position = jnp.where(inside, token - start + prompt[groups[m]], position)
        else:
            slot = jnp.where(inside, slots[adapters[m]], slot)
        start = finish
    return request, group, position, slot


def rotation(positions, head_width, lanes):
    half = head_width // 2
    lane = lax.broadcasted_iota(jnp.int32, (positions.shape[0], lanes), 1)
    place = lax.rem(lane, half).astype(jnp.float32)
    frequency = jnp.exp(place * (-2.0 * math.log(THETA) / head_width))
    angles = positions.astype(jnp.float32) * frequency
    cosine, sine = jnp.cos(angles), jnp.sin(angles)
    front = lax.rem(lane, head_width) < half
    signed = jnp.where(front, -sine, sine)

    def turn(values):
        values = values.astype(jnp.float32)
        partner = jnp.where(
            front, pltpu.roll(values, lanes - half, 1), pltpu.roll(values, half, 1)
        )
        return (values * cosine + partner * signed).astype(jnp.bfloat16)

    return turn


def page_groups(page, page_len, table, prompt):
    group, limit = jnp.int32(-1), jnp.int32(0)
    for s in range(table.shape[0]):
        for g in range(table.shape[1]):
            hit = table[s, g] == page
            group = jnp.where(hit, g, group)
            limit = jnp.where(hit, prompt[g] - s * page_len, limit)
    lane = lax.broadcasted_iota(jnp.int32, (1, page_len), 1)
    return jnp.where(lane < limit, group, -1)


def line_peers(i, nd):
    if nd != 4:
        return [lax.rem(i + d, nd) for d in range(1, nd)]
    high = i // 2
    return [3 * (1 - high), 2 - high, (1 - i) * (1 - high) + (5 - i) * high]


def spread(src, dst, send_sem, recv_sem, peers, j):
    return [send(src, dst, send_sem, recv_sem, t, j) for t in peers]


def own_heads(wide, half, head_width):
    keys, values = wide[:, 0, :].astype(jnp.float32), wide[:, 1, :].astype(jnp.float32)
    lane = lax.broadcasted_iota(jnp.int32, keys.shape, 1)
    keys = jnp.where(half == 0, keys, pltpu.roll(keys, head_width, 1))
    values = jnp.where(half == 0, pltpu.roll(values, head_width, 1), values)
    return jnp.where(lane < head_width, keys, values).astype(jnp.bfloat16)


def layer_body(
    nd,
    ne,
    rank_size,
    head_width,
    small_count,
    pages_hbm,
    fresh_hbm,
    *rest,
):
    small_hbm, rest = rest[:small_count], rest[small_count:]
    (gate_hbm, up_hbm, down_hbm, project_hbm, layer_out), rest = rest[:5], rest[5:]
    small, rest = rest[:small_count], rest[small_count:]
    (
        lengths,
        groups,
        adapters,
        slots,
        table,
        prompt,
        expert_slots,
        sinks,
        queries,
        route_experts,
        route_weights,
        adapter_columns,
        residual,
        up,
        gate_offset,
        up_offset,
        down_offset,
        bias,
        gain,
    ) = small
    (
        pages_wide,
        fresh_wide,
        merged,
        combine,
        proj,
        proj_wide,
        pair_out,
        pair_in,
        rank,
        pages_all,
        weights,
        project_matrix,
        gathered,
        gate_matrix,
        up_matrix,
        down_matrix,
        down_parts,
        hidden,
        outs,
        outs_in,
        sums,
        proj_in,
        rank_in,
        up_wide,
        up_part,
        delta,
        delta_full,
        rank_s,
        rank_r,
        proj_s,
        proj_r,
        pair_s,
        pair_r,
        delta_s,
        delta_r,
        wide_s,
        wide_r,
        plane_s,
        plane_r,
        chip_s,
        chip_r,
        hop_s,
        hop_r,
        pass_s,
        pass_r,
        load_sem,
        unit_s,
        unit_r,
        relay_s,
        out_s,
        out_r,
        sum_s,
        sum_r,
        page_s,
        page_r,
        combine_s,
        combine_r,
        small_sem,
        wide_sem,
        plane_hop_s,
    ) = rest
    i, j = lax.axis_index("dp"), lax.axis_index("ep")
    heads = sinks.shape[0]
    lanes = 2 * head_width
    page_count, page_len = pages_hbm.shape[:2]
    kv_head = j * (fresh_hbm.shape[2] // head_width) // ne
    block = pl.ds(pl.multiple_of(kv_head // 2 * lanes, lanes), lanes)
    head_loads = [
        pltpu.make_async_copy(pages_hbm.at[:, :, :, block], pages_wide, wide_sem.at[0]),
        pltpu.make_async_copy(fresh_hbm.at[:, :, block], fresh_wide, wide_sem.at[1]),
    ]
    for copy in head_loads:
        copy.start()
    peers = line_peers(i, nd)
    near_first = peers[::-1]
    relays = nd == 4
    inner = (i == 1) | (i == nd - 2)
    far_item = lax.rem(6 - 3 * i + 6, 6)
    end = 3 - far_item

    def carry(block, send_sem, recv_sem, target):
        return pltpu.make_async_remote_copy(
            src_ref=block,
            dst_ref=block,
            send_sem=send_sem,
            recv_sem=recv_sem,
            device_id=device(target, j),
            device_id_type=pl.DeviceIdType.MESH,
        )

    def all_sent(block, send_sem):
        carry(block, send_sem, send_sem, peers[0]).wait_send()

    def all_arrived(block, recv_sem):
        carry(block, recv_sem, recv_sem, peers[0]).wait_recv()

    others = pl.ds(0, nd - 1)

    def skips(target):
        apart = (i - target) * (i - target)
        return (apart == 9) | (inner & (apart == 4))

    def unless(skip, action):
        if skip is None:
            action()
        else:
            pl.when(jnp.logical_not(skip))(action)

    loads = [
        pltpu.make_async_copy(source, target, load_sem.at[n])
        for n, (source, target) in enumerate(
            (
                (gate_hbm.at[0], gate_matrix),
                (up_hbm.at[0], up_matrix),
                (down_hbm.at[0], down_matrix),
                (project_hbm, project_matrix),
            )
        )
    ]
    small_loads = [
        pltpu.make_async_copy(source, target, small_sem.at[n])
        for n, (source, target) in enumerate(zip(small_hbm, small))
    ]
    for copy in small_loads:
        copy.start()
    everyone = [(d, e) for d in range(nd) for e in range(ne) if d or e]
    met = greet([(lax.rem(i + d, nd), lax.rem(j + e, ne)) for d, e in everyone])
    half = lax.rem(kv_head, 2)
    head_loads[0].wait()
    pages_all[i] = own_heads(
        pages_wide[...].reshape(page_count * page_len, 2, lanes), half, head_width
    )
    met()
    page_copies = spread(pages_all.at[i], pages_all.at[i], page_s, page_r, peers, j)
    head_loads[1].wait()
    for copy in small_loads:
        copy.wait()
    for n in (3, 0, 1, 2):
        loads[n].start()
    rows = residual.shape[0]
    experts_of = route_experts[...]
    holders = jnp.zeros_like(experts_of)
    for e in range(expert_slots.shape[0]):
        holders = jnp.where(experts_of == e, expert_slots[e], holders)
    combine[...] = jnp.zeros_like(combine)
    for e in range(ne):
        combine[e : e + 1, :rows] = jnp.sum(
            jnp.where(holders == e, route_weights[...], 0.0), axis=0, keepdims=True
        )
    combine_copies = spread(combine, weights.at[i], combine_s, combine_r, peers, j)
    weights[i] = combine[...]
    tokens_row = queries.shape[0]
    fresh = own_heads(fresh_wide[...], half, head_width)
    scale = 1.0 / math.sqrt(head_width)
    request, group, position, _ = token_fields(
        tokens_row, 0, lengths, groups, adapters, slots, prompt
    )
    request_row, _, _, slot = token_fields(
        tokens_row, 1, lengths, groups, adapters, slots, prompt
    )
    turn = rotation(position, head_width, lanes)
    turned = [turn(queries[:, n * lanes : (n + 1) * lanes]) for n in range(heads // 2)]
    query_rows = jnp.concatenate(
        [pair[:, n * head_width : (n + 1) * head_width] for pair in turned for n in (0, 1)], axis=0
    )
    row_index = lax.broadcasted_iota(jnp.int32, (tokens_row, tokens_row), 0)
    column_index = lax.broadcasted_iota(jnp.int32, (tokens_row, tokens_row), 1)

    def masked_scores(keys, mask):
        width = keys.shape[0]
        scores = scale * lax.dot_general(
            query_rows, keys, LAST_DIMS, preferred_element_type=jnp.float32
        )
        return jnp.where(mask[None], scores.reshape(heads, tokens_row, width), NEG)

    score_list = [
        masked_scores(
            turn(fresh)[:, :head_width],
            (request == request_row) & (column_index <= row_index),
        )
    ]
    value_list = [fresh[:, head_width:]]
    homes = [i] + peers
    page_masks = [
        group
        == jnp.concatenate(
            [page_groups(t * page_count + q, page_len, table, prompt) for q in range(page_count)],
            axis=1,
        )
        for t in homes
    ]

    def score_pages(t, mask):
        shard = pages_all[t]
        score_list.append(masked_scores(shard[:, :head_width], mask))
        value_list.append(shard[:, head_width:])

    score_pages(i, page_masks[0])
    sink = jnp.concatenate(
        [jnp.full((1, tokens_row, 1), sinks[h], jnp.float32) for h in range(heads)], axis=0
    )
    peak = sink
    for scores in score_list:
        peak = jnp.maximum(peak, jnp.max(scores, axis=-1, keepdims=True))
    width, part = residual.shape[1], delta.shape[2]
    own_part = pl.ds(pl.multiple_of(j * part, part), part)
    up_wide[:, :width] = up[...]
    up_wide[:, width:] = jnp.zeros((up.shape[0], ne * part - width), jnp.bfloat16)
    up_part[i] = up_wide[:, own_part]
    all_arrived(pages_all.at[others], page_r)
    wide_copies = spread(up_wide.at[:, own_part], up_part.at[i], wide_s, wide_r, peers, j)
    for t, mask in zip(peers, page_masks[1:]):
        score_pages(t, mask)
    for scores in score_list[2:]:
        peak = jnp.maximum(peak, jnp.max(scores, axis=-1, keepdims=True))
    denominator = jnp.exp(sink - peak)
    weighted = jnp.zeros((heads * tokens_row, head_width), jnp.float32)
    for scores, values in zip(score_list, value_list):
        probs = jnp.exp(scores - peak)
        denominator = denominator + jnp.sum(probs, axis=-1, keepdims=True)
        weighted = weighted + jnp.dot(
            probs.reshape(heads * tokens_row, -1).astype(jnp.bfloat16),
            values,
            preferred_element_type=jnp.float32,
        )
    attended = weighted.reshape(heads, tokens_row, head_width) / denominator
    attended = jnp.concatenate([attended[h] for h in range(heads)], axis=1).astype(jnp.bfloat16)
    rank_width = nd * up.shape[0]
    slot_rows = (
        lax.broadcasted_iota(jnp.int32, (rank_width, tokens_row), 0) // rank_size == slot
    )
    rank_all = lax.dot_general(
        adapter_columns[...], attended, LAST_DIMS, preferred_element_type=jnp.float32
    )
    rank_all = jnp.where(slot_rows, rank_all, 0.0)
    rank[...] = jnp.sum(
        rank_all.reshape(rank_width // rank_size, rank_size, tokens_row), axis=0
    ).astype(jnp.bfloat16)
    rank_copies, proj_copies = [], []
    for e in range(1, ne):
        rank_copies.append(
            send(
                rank, rank_in.at[e - 1], rank_s, rank_r, i, lax.rem(j + e, ne)
            )
        )
    loads[3].wait()
    projected = lax.dot_general(
        attended, project_matrix[...], LAST_DIMS, preferred_element_type=jnp.float32
    )
    for e in range(ne):
        proj_wide[e] = projected[e * rows : (e + 1) * rows]
    turns = (6, 2, 4, 0)
    pair_copies = []
    for n, bits in enumerate(turns):
        pair_out[n] = proj_wide[flip(j, bits + 1)].astype(jnp.bfloat16)
        pair_copies.append(
            send(pair_out.at[n], pair_in.at[n], pair_s, pair_r.at[n], i, flip(j, 1))
        )
    for n, bits in enumerate(turns):
        pair_copies[n].wait_recv()
        total = proj_wide[flip(j, bits)] + pair_in[n].astype(jnp.float32)
        if bits:
            proj[n] = total.astype(jnp.bfloat16)
            proj_copies.append(
                send(proj.at[n], proj_in.at[n], proj_s, proj_r, i, flip(j, bits))
            )
    all_sent(rank_in, rank_s)
    all_arrived(rank_in, rank_r)
    all_arrived(up_part.at[others], wide_r)
    middle = rank[...].astype(jnp.float32)
    for e in range(1, ne):
        middle = middle + rank_in[e - 1].astype(jnp.float32)
    middles = jnp.concatenate([middle] * (rank_width // rank_size), axis=0)
    middles = jnp.where(slot_rows, middles, 0.0).astype(jnp.bfloat16)
    updates = lax.dot_general(
        middles,
        up_part[...].reshape(rank_width, part),
        (((0,), (0,)), ((), ())),
        preferred_element_type=jnp.float32,
    )
    updates = ADAPTER_SCALE * updates
    for e in range(ne):
        delta[e] = updates[e * rows : (e + 1) * rows].astype(jnp.bfloat16)
    delta_full[:, own_part] = delta[j]
    delta_copies = []
    for e in range(1, ne):
        tj = lax.rem(j + e, ne)
        delta_copies.append(
            send(
                delta.at[tj],
                delta_full.at[:, own_part],
                delta_s,
                delta_r,
                i,
                tj,
            )
        )
    all_sent(proj, proj_s)
    all_arrived(proj_in, proj_r)
    for n in range(3):
        total = total + proj_in[n].astype(jnp.float32)
    total = total + residual[...].astype(jnp.float32) + bias[...].astype(jnp.float32).reshape(1, -1)
    all_sent(delta.at[pl.ds(0, ne - 1)], delta_s)
    all_arrived(delta.at[pl.ds(0, ne - 1)], delta_r)
    total = total + delta_full[:, :width].astype(jnp.float32)
    rounded = total.astype(jnp.bfloat16)
    stream = rounded.astype(jnp.float32)
    mean_square = jnp.mean(stream * stream, axis=-1, keepdims=True)
    normed = stream * lax.rsqrt(mean_square + EPSILON) * gain[...].astype(jnp.float32).reshape(1, -1)
    gathered[j, i] = normed.astype(jnp.bfloat16)
    plane_copies = []
    for n, t in enumerate(peers):
        copy = carry(gathered.at[j, i], plane_s, plane_r.at[i], t)
        skip = skips(t) if relays else None
        plane_copies.append((copy, skip))
        unless(skip, copy.start)
    sibling, across, along = flip(j, 1), flip(j, 2), flip(j, 4)
    chip_copies = []

    def to_chips(d):
        for n, target in enumerate((across, along, sibling)):
            piece = gathered.at[j, d]
            chip_copies.append(send(piece, piece, chip_s, chip_r.at[n], i, target))

    to_chips(i)
    loads[2].wait()
    units_own = down_parts.shape[2]
    for d in range(nd):
        down_parts[d] = down_matrix[:, d * units_own : (d + 1) * units_own]
    def landed(t):
        return carry(gathered.at[j, t], plane_s, plane_r.at[t], t)

    def plane_hop(n, t):
        return carry(gathered.at[j, t], plane_hop_s.at[n], plane_r.at[t], end)

    if relays:

        @pl.when(inner)
        def _():
            for n, t in enumerate((3 - i, far_item)):
                landed(t).wait_recv()
                plane_hop(n, t).start()

    for t in near_first:
        unless(inner & (t != end) if relays else None, landed(t).wait_recv)
        to_chips(t)

    def from_chip(n, source):
        all_arrived(gathered.at[source], chip_r.at[n])

    core = lax.rem(j, 2)
    hop_from = along + core * (across - along)
    hop_to = across + core * (along - across)
    passed = []
    chunks = (0, 2, 4, 6)
    unit_copies = []

    def units(c):
        bits = chunks[c]
        blocks = [
            gathered[flip(j, bits + n)].astype(jnp.float32).reshape(nd * rows, -1) for n in (0, 1)
        ]
        tokens = jnp.concatenate(blocks, axis=0).astype(jnp.bfloat16)
        hidden[i, c] = expert_hidden(
            tokens, gate_matrix[...], up_matrix[...], gate_offset[...], up_offset[...]
        )
        for ti in peers:
            copy = carry(hidden.at[i, c], unit_s, unit_r.at[i, c], ti)
            skip = skips(ti) if relays else None
            unit_copies.append((copy, skip))
            unless(skip, copy.start)

    def passage(item, c, n):
        return carry(hidden.at[item, c], relay_s.at[n, c], unit_r.at[item, c], end)

    def arrival(item, c):
        return carry(hidden.at[item, c], unit_s, unit_r.at[item, c], item)

    def relay(n, c, before):
        if not relays:
            return

        @pl.when(inner)
        def _():
            item = (3 - i, far_item)[n]
            arrival(item, c).wait_recv()
            if before is not None:
                passage(item, before, n).wait_send()
            passage(item, c, n).start()

    def pass_on(other):
        n = len(passed)
        passed.append(
            send(gathered.at[other], gathered.at[other], pass_s, pass_r.at[n], i, sibling)
        )

    out_copies = []

    def shard_down(c, item):
        return lax.dot_general(
            hidden[item, c], down_parts[item], LAST_DIMS, preferred_element_type=jnp.float32
        )

    def add_arrivals(c, items, result):
        for item in items:
            unless(inner & (item != end) if relays else None, arrival(item, c).wait_recv)
            result = result + shard_down(c, item)
        return result

    def begin(c):
        result = down_offset[...].astype(jnp.float32) + shard_down(c, i)
        return add_arrivals(c, near_first[:-1], result)

    def finish(c, result):
        result = add_arrivals(c, near_first[-1:], result)
        for n in (0, 1):
            other = flip(j, chunks[c] + n)
            for d in range(nd):
                start = (n * nd + d) * rows
                outs[other, d] = result[start : start + rows].astype(jnp.bfloat16)
            if chunks[c] + n:
                place = chunks[c] + n - 1
                out_copies.append(
                    send(
                        outs.at[other], outs_in.at[place], out_s, out_r, i, other
                    )
                )

    loads[0].wait()
    loads[1].wait()
    from_chip(2, sibling)
    units(0)
    from_chip(0, across)
    pass_on(across)
    from_chip(1, along)
    pass_on(along)
    hop = send(gathered.at[hop_from], gathered.at[hop_from], hop_s, hop_r, i, hop_to)
    passed[0].wait_recv()
    units(1)
    relay(0, 0, None)
    hop.wait_recv()
    pass_on(flip(j, 6))
    passed[1].wait_recv()
    units(2)
    relay(0, 1, None)
    passed[2].wait_recv()
    units(3)
    relay(1, 1, None)
    relay(0, 2, 0)
    own_chip = begin(0)
    finish(1, begin(1))
    relay(1, 2, None)
    relay(0, 3, 1)
    finish(2, begin(2))
    relay(1, 3, 1)
    finish(3, begin(3))
    relay(1, 0, 2)
    finish(0, own_chip)
    all_arrived(outs_in, out_r)
    all_arrived(weights.at[others], combine_r)
    diagonal = lax.broadcasted_iota(jnp.int32, (rows, rows), 0) == lax.broadcasted_iota(
        jnp.int32, (rows, rows), 1
    )
    for d in range(nd):
        total = 0.0
        for bits in range(ne):
            piece = outs[j, d] if bits == 0 else outs_in[bits - 1, d]
            line = weights[d, pl.ds(flip(j, bits), 1), :][:, :rows]
            factor = jnp.sum(jnp.where(diagonal, line, 0.0), axis=1, keepdims=True)
            total = total + piece.astype(jnp.float32) * factor
        sums[d] = total.astype(jnp.bfloat16)
    finals = [
        send(sums.at[t], merged.at[i], sum_s, sum_r, t, j)
        for t in peers
    ]
    merged[i] = sums[i]
    sends = pl.ds(0, 2 if relays else nd - 1)
    all_sent(hidden.at[sends], unit_s)
    all_sent(gathered.at[0, sends], plane_s)
    if relays:

        @pl.when(inner)
        def _():
            for n, t in enumerate((3 - i, far_item)):
                plane_hop(n, t).wait_send()
            for n, c in ((0, 2), (0, 3), (1, 3), (1, 0)):
                passage(0, c, n).wait_send()

    hop.wait_send()
    three = pl.ds(0, 3)
    for block, sem in (
        (gathered.at[three], chip_s),
        (gathered.at[three], pass_s),
        (outs.at[pl.ds(0, ne - 1)], out_s),
        (pages_all.at[others], page_s),
        (weights.at[others], combine_s),
        (up_part.at[others], wide_s),
        (pair_out, pair_s),
    ):
        all_sent(block, sem)
    all_sent(merged.at[others], sum_s)
    all_arrived(merged.at[others], sum_r)
    update = jnp.concatenate([merged[d].astype(jnp.float32) for d in range(nd)], axis=1)
    layer_out[...] = (stream + update).astype(jnp.bfloat16)


def layer(nd, ne, rank_size, head_width, front, scalars, small, matrices):
    caches, fresh = front
    lanes = 2 * head_width
    page_rows = caches.shape[0] * caches.shape[1]
    residual, up = small[4:6]
    rows, width = residual.shape
    part = -(-width // (128 * ne)) * 128
    units = matrices[0].shape[1]
    dma = pltpu.SemaphoreType.DMA
    held = scalars + small
    args = front + held + matrices
    vmem = pl.BlockSpec(memory_space=pltpu.VMEM)
    bf16 = jnp.bfloat16
    return pl.pallas_call(
        functools.partial(layer_body, nd, ne, rank_size, head_width, len(held)),
        out_shape=jax.ShapeDtypeStruct((rows, width), bf16),
        in_specs=[pl.BlockSpec(memory_space=pltpu.HBM)] * len(args),
        out_specs=vmem,
        scratch_shapes=[pltpu.SMEM(x.shape, x.dtype) for x in scalars]
        + [pltpu.VMEM(x.shape, x.dtype) for x in small]
        + [
            pltpu.VMEM(caches.shape[:3] + (lanes,), bf16),
            pltpu.VMEM(fresh.shape[:2] + (lanes,), bf16),
            pltpu.VMEM((nd, rows, units), bf16),
            pltpu.VMEM((ne, 128), jnp.float32),
            pltpu.VMEM((3, rows, width), bf16),
            pltpu.VMEM((ne, rows, width), jnp.float32),
            pltpu.VMEM((4, rows, width), bf16),
            pltpu.VMEM((4, rows, width), bf16),
            pltpu.VMEM((rank_size, small[0].shape[0]), bf16),
            pltpu.VMEM((nd, page_rows, lanes), bf16),
            pltpu.VMEM((nd, ne, 128), jnp.float32),
            pltpu.VMEM(matrices[3].shape, bf16),
            pltpu.VMEM((ne, nd, rows, width), bf16),
            pltpu.VMEM((units, width), bf16),
            pltpu.VMEM((units, width), bf16),
            pltpu.VMEM((units, width), bf16),
            pltpu.VMEM((nd, units, width // nd), bf16),
            pltpu.VMEM((nd, 4, 2 * nd * rows, units), bf16),
            pltpu.VMEM((ne, nd, rows, units), bf16),
            pltpu.VMEM((ne - 1, nd, rows, units), bf16),
            pltpu.VMEM((nd, rows, units), bf16),
            pltpu.VMEM((3, rows, width), bf16),
            pltpu.VMEM((ne - 1, rank_size, small[0].shape[0]), bf16),
            pltpu.VMEM((up.shape[0], ne * part), bf16),
            pltpu.VMEM((nd, up.shape[0], part), bf16),
            pltpu.VMEM((ne, rows, part), bf16),
            pltpu.VMEM((rows, ne * part), bf16),
            dma,
            dma,
            dma,
            dma,
            dma,
            dma((4,)),
            dma,
            dma,
            dma,
            dma,
            dma,
            dma((nd,)),
            dma,
            dma((3,)),
            dma,
            dma,
            dma,
            dma((3,)),
            dma((4,)),
            dma,
            dma((nd, 4)),
            dma((2, 4)),
            dma,
            dma,
            dma,
            dma,
            dma,
            dma,
            dma,
            dma,
            dma((len(held),)),
            dma((2,)),
            dma((2,)),
        ],
        compiler_params=pltpu.CompilerParams(
            collective_id=2, has_side_effects=True, vmem_limit_bytes=60 * 2**20
        ),
    )(*args)


def on_device(
    residual,
    queries,
    fresh_key_value,
    prompt_page_cache,
    group_page_table,
    prompt_length,
    suffix_length,
    request_group,
    request_adapter_index,
    adapter_slot_index,
    adapter_down_maps,
    adapter_up_maps,
    sinks,
    output_weight,
    output_bias,
    norm_weight,
    token_experts,
    expert_gate_weight,
    expert_slot_index,
    gate_weight,
    up_weight,
    down_weight,
    gate_bias,
    up_bias,
    down_bias,
):
    heads_per_device = sinks.shape[0]
    tok_row = queries.shape[0]
    head_width = queries.shape[1] // heads_per_device
    kv_count = fresh_key_value.shape[2] // head_width
    ep_count = lax.axis_size("ep")
    data_parallel_count = lax.axis_size("dp")
    group_size = heads_per_device * ep_count // kv_count
    kv_head = lax.axis_index("ep") * heads_per_device // group_size
    tokens_per_device = tok_row // ep_count
    hidden_width = residual.shape[1]
    adapter_weights = adapter_down_maps.shape[0]
    adapter_rank_size = adapter_down_maps.shape[2]
    score_scale = 1.0 / math.sqrt(head_width)
    own_kv = lax.dynamic_slice_in_dim(fresh_key_value, kv_head * head_width, head_width, 2)
    experts = expert_slot_index.shape[0]
    top_count = token_experts.shape[1]
    capacity = max(2, 8 * tokens_per_device // experts)
    direct = experts == ep_count and ep_count == 8 and capacity >= tokens_per_device
    if direct:
        return layer(
            data_parallel_count,
            ep_count,
            adapter_rank_size,
            head_width,
            (prompt_page_cache, fresh_key_value),
            (
                suffix_length,
                request_group,
                request_adapter_index,
                adapter_slot_index,
                group_page_table.T,
                prompt_length,
                expert_slot_index,
                sinks,
            ),
            (
                queries,
                token_experts.T,
                expert_gate_weight.T,
                adapter_down_maps.transpose(0, 2, 1).reshape(-1, heads_per_device * head_width),
                residual,
                adapter_up_maps.reshape(-1, hidden_width),
                gate_bias,
                up_bias,
                down_bias,
                output_bias,
                norm_weight,
            ),
            (gate_weight, up_weight, down_weight, output_weight.T),
        )
    expert_hit = token_experts[:, :, None] == jnp.arange(experts, dtype=jnp.int32)[None, None, :]
    route_col = jnp.sum(jnp.where(expert_hit, expert_slot_index[None, None, :], 0), axis=2)
    request_local, token_group, positions, token_slot = token_layout(
        suffix_length[0],
        request_group,
        request_adapter_index,
        adapter_slot_index,
        prompt_length,
        tok_row,
    )
    queries_rot = rotate(
        queries.reshape(tok_row, heads_per_device, head_width).astype(jnp.float32), positions
    ).astype(jnp.bfloat16)
    keys_new = rotate(own_kv[:, 0:1, :].astype(jnp.float32), positions)[:, 0, :].astype(
        jnp.bfloat16
    )
    values_new = own_kv[:, 1, :]
    token_index = jnp.arange(tok_row, dtype=jnp.int32)
    allowed = (request_local[:, None] == request_local[None, :]) & (
        token_index[None, :] <= token_index[:, None]
    )
    local_scores = (
        jnp.einsum("thd,sd->hts", queries_rot, keys_new, preferred_element_type=jnp.float32)
        * score_scale
    )
    local_masked = jnp.where(allowed[None], local_scores, NEG)
    sink_col = sinks[:, None]
    run_max = jnp.maximum(sink_col, jnp.max(local_masked, axis=-1))
    local_exp = jnp.exp(local_masked - run_max[..., None])
    run_total = jnp.exp(sink_col - run_max) + jnp.sum(local_exp, axis=-1)
    run_acc = jnp.einsum(
        "hts,sd->htd",
        local_exp.astype(jnp.bfloat16),
        values_new,
        preferred_element_type=jnp.float32,
    )
    page_len = prompt_page_cache.shape[1]
    pool_total = prompt_page_cache.shape[0] * data_parallel_count
    page_group, page_slot, page_used = page_layout(group_page_table, pool_total)
    group_hit = page_group[:, None] == jnp.arange(prompt_length.shape[0], dtype=jnp.int32)[None, :]
    page_limit = jnp.sum(jnp.where(group_hit, prompt_length[None, :], 0), axis=1)
    own_pages = lax.dynamic_slice_in_dim(prompt_page_cache, kv_head * head_width, head_width, 3)
    shard_rows = lax.all_gather(own_pages, "dp", axis=0, tiled=True)
    piece_pages = shard_rows.shape[0]
    keys_piece = shard_rows[:, :, 0, :].reshape(piece_pages * page_len, head_width)
    values_piece = shard_rows[:, :, 1, :].reshape(piece_pages * page_len, head_width)
    key_pos = page_slot[:, None] * page_len + jnp.arange(page_len, dtype=jnp.int32)[None, :]
    key_valid = (page_used[:, None] & (key_pos < page_limit[:, None])).reshape(-1)
    key_group = jnp.broadcast_to(page_group[:, None], (piece_pages, page_len)).reshape(-1)
    visible = (token_group[:, None] == key_group[None, :]) & key_valid[None, :]
    scores = (
        jnp.einsum("thd,sd->hts", queries_rot, keys_piece, preferred_element_type=jnp.float32)
        * score_scale
    )
    masked = jnp.where(visible[None], scores, NEG)
    new_max = jnp.maximum(run_max, jnp.max(masked, axis=-1))
    factor = jnp.exp(run_max - new_max)
    weights = jnp.exp(masked - new_max[..., None])
    new_total = run_total * factor + jnp.sum(weights, axis=-1)
    new_acc = run_acc * factor[..., None] + jnp.einsum(
        "hts,sd->htd",
        weights.astype(jnp.bfloat16),
        values_piece,
        preferred_element_type=jnp.float32,
    )
    attention_output = (
        (new_acc / new_total[..., None])
        .transpose(1, 0, 2)
        .reshape(tok_row, heads_per_device * head_width)
        .astype(jnp.bfloat16)
    )
    adapter_onehot = token_slot[:, None] == jnp.arange(adapter_weights, dtype=jnp.int32)[None, :]
    adapter_pick_all = adapter_onehot.astype(jnp.float32)
    adapter_columns = adapter_down_maps.transpose(1, 0, 2).reshape(
        heads_per_device * head_width, adapter_weights * adapter_rank_size
    )
    projected_rows = jnp.dot(attention_output, output_weight, preferred_element_type=jnp.float32)
    reduced_rank = jnp.dot(
        attention_output, adapter_columns, preferred_element_type=jnp.float32
    ).reshape(tokens_per_device * lax.axis_size("ep"), adapter_weights, adapter_rank_size)
    reduced_rank = jnp.sum(reduced_rank * adapter_pick_all[:, :, None], axis=1)
    summed_rows = lax.psum_scatter(
        jnp.concatenate([projected_rows, reduced_rank], axis=1).astype(jnp.bfloat16),
        "ep",
        scatter_dimension=0,
        tiled=True,
    ).astype(jnp.float32)
    projection_sum = summed_rows[:, :hidden_width]
    adapter_middle = summed_rows[:, hidden_width:].astype(jnp.bfloat16)
    owner_onehot = lax.dynamic_slice_in_dim(
        adapter_onehot, lax.axis_index("ep") * tokens_per_device, tokens_per_device, 0
    )
    spread_rows = owner_onehot.astype(jnp.bfloat16)[:, :, None] * adapter_middle[:, None, :]
    holder_count = adapter_up_maps.shape[0]
    outgoing = spread_rows.reshape(
        tokens_per_device, data_parallel_count, holder_count * adapter_rank_size
    )
    incoming = lax.all_to_all(outgoing, "dp", split_axis=1, concat_axis=0, tiled=True)
    adapter_updates = jnp.dot(
        incoming.reshape(data_parallel_count * tokens_per_device, holder_count * adapter_rank_size),
        adapter_up_maps.reshape(holder_count * adapter_rank_size, hidden_width),
        preferred_element_type=jnp.float32,
    )
    adapter_updates = (
        (ADAPTER_SCALE * adapter_updates)
        .astype(jnp.bfloat16)
        .reshape(data_parallel_count, tokens_per_device, hidden_width)
    )
    returned_rows = lax.all_to_all(adapter_updates, "dp", split_axis=0, concat_axis=0, tiled=True)
    adapter_update = jnp.sum(returned_rows.astype(jnp.float32), axis=0)
    stream = settle(
        residual.astype(jnp.float32)
        + projection_sum
        + output_bias.astype(jnp.float32)
        + adapter_update
    )
    mean_square = jnp.mean(stream * stream, axis=-1, keepdims=True)
    normed = (stream * lax.rsqrt(mean_square + EPSILON) * norm_weight.astype(jnp.float32)).astype(
        jnp.bfloat16
    )
    slots_all = ep_count * capacity
    route_col = route_col.reshape(-1)
    col_hot = (route_col[:, None] == jnp.arange(ep_count, dtype=jnp.int32)[None, :]).astype(
        jnp.int32
    )
    route_order = jnp.arange(route_col.shape[0], dtype=jnp.int32)
    earlier = (route_order[None, :] < route_order[:, None]).astype(jnp.int32)
    route_rank = jnp.sum(earlier * (route_col[None, :] == route_col[:, None]), axis=1)
    target_slot = route_col * capacity + route_rank
    target_hot = (target_slot[:, None] == jnp.arange(slots_all, dtype=jnp.int32)[None, :]).reshape(
        tokens_per_device, top_count, slots_all
    )
    scatter_rows = jnp.sum(target_hot.astype(jnp.float32), axis=1)
    combine = jnp.sum(jnp.where(target_hot, expert_gate_weight[:, :, None], 0.0), axis=1)
    outbound = (
        jnp.dot(scatter_rows.T.astype(jnp.bfloat16), normed, preferred_element_type=jnp.float32)
        .astype(jnp.bfloat16)
        .reshape(ep_count, capacity, hidden_width)
    )
    received = lax.all_to_all(outbound, "ep", split_axis=0, concat_axis=0, tiled=True)
    rows_flat = lax.all_gather(received[None], "dp", axis=0, tiled=True).reshape(-1, hidden_width)
    hidden = expert_hidden(rows_flat, gate_weight[0], up_weight[0], gate_bias[0], up_bias[0])
    unit_weights = down_weight[0]
    unit_sum = lax.dot_general(
        lax.all_gather(hidden, "dp", axis=1, tiled=True),
        unit_weights,
        LAST_DIMS,
        preferred_element_type=jnp.float32,
    )
    expert_out = (
        (unit_sum + down_bias[0].astype(jnp.float32))
        .astype(jnp.bfloat16)
        .reshape(data_parallel_count, slots_all, -1)
    )
    home_rows = lax.all_to_all(expert_out, "dp", split_axis=0, concat_axis=2, tiled=True)
    back_rows = lax.all_to_all(
        home_rows.reshape(ep_count, capacity, hidden_width),
        "ep",
        split_axis=0,
        concat_axis=0,
        tiled=True,
    )
    merged = jnp.dot(
        combine,
        back_rows.reshape(slots_all, hidden_width).astype(jnp.float32),
        precision=lax.Precision.HIGHEST,
        preferred_element_type=jnp.float32,
    )
    return (stream + merged).astype(jnp.bfloat16)


def solution(mesh):
    placed = (
        P(("dp", "ep"), None),
        P("dp", "ep"),
        P("dp", None, None),
        P("dp", None, None, None),
        P(),
        P(),
        P("dp", None),
        P("dp"),
        P("dp"),
        P(),
        P(None, "ep", None),
        P("dp", None, None),
        P("ep"),
        P("ep", None),
        P(),
        P(),
        P(("dp", "ep"), None),
        P(("dp", "ep"), None),
        P(),
        P("ep", "dp", None),
        P("ep", "dp", None),
        P("ep", "dp", None),
        P("ep", "dp"),
        P("ep", "dp"),
        P("ep", "dp"),
    )
    return jax.shard_map(
        on_device, mesh=mesh, in_specs=placed, out_specs=P(("dp", "ep"), None), check_vma=False
    )
```
